32 devices in a mesh: rep: 2 (over y), shard: 16 (over z, x, core).
Axes of the slice: x: 2, y: 2, z: 4, core: 2. Of those that a mesh axis runs over, the one named last changes fastest.
Arguments:
- block_input: bfloat16 [32768, 768], P(('rep', 'shard')), may hold values from -6 to 6
- history: bfloat16 [4, 32768, 768], P(None, ('rep', 'shard')), may hold values from -6 to 6
- cotangent: bfloat16 [32768, 768], P(('rep', 'shard')), may hold values from -6 to 6
- span_start: int32 [32], P(('rep', 'shard')), may hold values from 0 to 768, as said below
- w_qkv: bfloat16 [768, 2304], P('shard'), may hold values from -0.21875 to 0.21875
- w_out: bfloat16 [768, 768], P('shard'), may hold values from -4 to 4
- w_up: bfloat16 [768, 3072], P('shard'), may hold values from -0.21875 to 0.21875
- w_down: bfloat16 [3072, 768], P('shard'), may hold values from -0.109375 to 0.109375
- ln_gains: bfloat16 [2, 768], P(None, 'shard'), may hold values from 0.5 to 1.5
- ln_biases: bfloat16 [2, 768], P(None, 'shard'), may hold values from -3 to 3
- mix_weights: float32 [5], replicated, may hold values from 0.3 to 1
Outputs:
- next_input: bfloat16 [32768, 768], P(('rep', 'shard'))
- grad_input: float32 [32768, 768], P(('rep', 'shard'))
- grad_history: float32 [4, 32768, 768], P(None, ('rep', 'shard'))
- grad_mix: float32 [5], replicated
- grad_w_qkv: float32 [768, 2304], P('shard')
- grad_w_out: float32 [768, 768], P('shard')
- grad_w_up: float32 [768, 3072], P('shard')
- grad_w_down: float32 [3072, 768], P('shard')
- grad_gains: float32 [2, 768], P(None, 'shard')
- grad_bias_first: float32 [768], P('shard')
- grad_bias_second: float32 [768], P('shard')
The draws below stay inside these ranges and needn't reach their ends.
Inputs may be any that keep to these rules, and one draw needn't show every extreme that they name: Sequence n's picture span covers positions span_start[n] to span_start[n] + 255 of that sequence.
All inputs are finite; a program needn't handle non-finite values.
Results may differ from the reference program's by a relative error of at most 0.017.
Values may be sent and summed in bfloat16 or wider, within the bound.
A program may use at most 256 MiB of HBM per device.

```python
import jax
import jax.numpy as jnp
from jax import lax

D = 768
FF = 3072
HEADS = 12
HEAD_DIM = 64
SEQ_LEN = 1024
SPAN = 256
PAST = 4
SEQS = 32
TOKENS = 32768
MIX = 5


def draw_span_start(key, part):
    key_base = jax.random.fold_in(key, 11)
    key_main, key_low, key_high = jax.random.split(key_base, 3)
    starts = jax.random.randint(key_main, (SEQS,), 0, SEQ_LEN - SPAN + 1)
    low_slot = jax.random.randint(key_low, (), 0, SEQS)
    high_slot = (low_slot + 1 + jax.random.randint(key_high, (), 0, SEQS - 1)) % SEQS
    starts = starts.at[low_slot].set(0)
    starts = starts.at[high_slot].set(SEQ_LEN - SPAN)
    return starts.astype(jnp.int32)


def shard_levels(key, shape, cuts, smallest, top_value):
    loudness = 1.0
    for position, shards_of in cuts:
        heights = jax.random.uniform(jax.random.fold_in(jax.random.fold_in(key, 6), position), (shards_of,), jnp.float32, smallest / len(cuts), top_value / len(cuts))
        loudness = loudness * jnp.repeat(jnp.exp(heights), shape[position] // shards_of).reshape((-1,) + (1,) * (len(shape) - 1 - position))
    return loudness


def centred(key, dims, width, bound, cuts=(), kind=jnp.bfloat16):
    entries = jax.random.normal(key, dims, jnp.float32) * width
    if len(cuts) > 0:
        entries = shard_levels(key, dims, cuts, -0.22, 0.18) * entries
    return jnp.clip(entries, min=-bound, max=bound).astype(kind)


def setup_inputs(seed: int = 0) -> dict:
    arg_keys = jax.random.split(jax.random.key(seed), 12)
    return {
        "block_input": centred(arg_keys[0], (TOKENS, D), 1.0, 6.0, ((0, 32),)),
        "history": centred(arg_keys[1], (PAST, TOKENS, D), 1.0, 6.0, ((1, 32),)),
        "cotangent": centred(arg_keys[2], (TOKENS, D), 1.0, 6.0, ((0, 32),)),
        "span_start": draw_span_start(jax.random.fold_in(arg_keys[11], 71), 0),
        "w_qkv": centred(arg_keys[4], (D, 3 * D), D ** -0.5, 0.21875, ((0, 16),)),
        "w_out": centred(arg_keys[5], (D, D), (max(1, D // 384)) ** -0.5, 4.0, ((0, 16),)),
        "w_up": centred(arg_keys[6], (D, FF), D ** -0.5, 0.21875, ((0, 16),)),
        "w_down": centred(arg_keys[7], (FF, D), FF ** -0.5, 0.109375, ((0, 16),)),
        "ln_gains": jnp.clip(1.0 + 0.1 * jax.random.normal(arg_keys[8], (2, D), jnp.float32), 0.5, 1.5).astype(jnp.bfloat16),
        "ln_biases": centred(arg_keys[9], (2, D), 0.3, 3.0, ((1, 16),)),
        "mix_weights": jnp.clip(jax.random.uniform(arg_keys[10], (MIX,), jnp.float32, 0.3, 1.0), 0.3, 1.0),
    }


@jax.custom_vjp
def low(v):
    return lax.optimization_barrier(v.astype(jnp.bfloat16)).astype(jnp.float32)

@jax.custom_vjp
def low_back(v):
    return v

def low_keep(v):
    return (low(v), None)

def low_pass(kept, grad):
    return (grad,)

def back_keep(v):
    return (v, None)

def back_low(kept, grad):
    return (low(grad),)
low.defvjp(low_keep, low_pass)
low_back.defvjp(back_keep, back_low)
HIGH = lax.Precision.HIGHEST

def layer_norm(values, gain_row, bias_row):
    average = lax.optimization_barrier(jnp.mean(values, axis=-1, keepdims=True))
    centered = values - average
    inverse_std = lax.rsqrt(lax.optimization_barrier(jnp.mean(centered * centered, axis=-1, keepdims=True)) + 1e-05)
    return centered * inverse_std * gain_row + bias_row

def rotary_tables(length, head_width):
    half_width = head_width // 2
    frequency = jnp.exp(-jnp.log(10000.0) * jnp.arange(half_width, dtype=jnp.float32) * (2.0 / head_width))
    angles = jnp.arange(length, dtype=jnp.float32)[:, None] * frequency[None, :]
    angles = jnp.concatenate([angles, angles], axis=-1)[:, None, :]
    return (jnp.cos(angles), jnp.sin(angles))

def rotate(values, cosine, sine):
    half_width = values.shape[-1] // 2
    turned = jnp.concatenate([-values[..., half_width:], values[..., :half_width]], axis=-1)
    return values * cosine + turned * sine

def visible(length, span_begin):
    positions = jnp.arange(length, dtype=jnp.int32)
    inside = (positions >= span_begin) & (positions < span_begin + SPAN)
    return (positions[None, :] <= positions[:, None]) | inside[:, None] & inside[None, :]

def block_sequence(weights_in, sequence, span_begin):
    w_qkv, w_out, w_up, w_down, gains, biases = weights_in
    length = sequence.shape[0]
    act1 = low(layer_norm(sequence, gains[0], biases[0]))
    projected = low_back(jnp.dot(act1, w_qkv, precision=HIGH))
    queries = projected[:, :D].reshape(length, HEADS, HEAD_DIM)
    keys_all = projected[:, D:2 * D].reshape(length, HEADS, HEAD_DIM)
    values_all = projected[:, 2 * D:].reshape(length, HEADS, HEAD_DIM)
    cosine, sine = rotary_tables(length, HEAD_DIM)
    q_rot = low(rotate(queries, cosine, sine))
    k_rot = low(rotate(keys_all, cosine, sine))
    v_low = low(values_all)
    scores = low_back(HEAD_DIM ** (-0.5) * jnp.einsum('qhd,khd->hqk', q_rot, k_rot, precision=HIGH))
    scores = jnp.where(visible(length, span_begin)[None], scores, -1e+30)
    probs = jax.nn.softmax(scores, axis=-1)
    mixed = jnp.einsum('hqk,khd->qhd', low(probs), v_low, precision=HIGH).reshape(length, D)
    mixed = low_back(low(mixed))
    middle = sequence + low_back(jnp.dot(mixed, w_out, precision=HIGH))
    act2 = low(layer_norm(middle, gains[1], biases[1]))
    upper = low_back(jnp.dot(act2, w_up, precision=HIGH))
    hidden = low(jax.nn.gelu(upper, approximate=False))
    return middle + low_back(jnp.dot(hidden, w_down, precision=HIGH))

def forward(block_input, history, weights_in, mix_weights, span_start):
    sequences = block_input.reshape(-1, SEQ_LEN, D)

    def one_sequence(inputs):
        sequence, span_begin = inputs
        return jax.checkpoint(lambda weights_now, rows_in: block_sequence(weights_now, rows_in, span_begin))(weights_in, sequence)
    outputs = lax.map(one_sequence, (sequences, span_start)).reshape(-1, D)
    earlier = jnp.einsum('k,ktd->td', mix_weights[:PAST], history, precision=HIGH)
    return earlier + mix_weights[PAST] * outputs

def reference(block_input, history, cotangent, span_start, w_qkv, w_out, w_up, w_down, ln_gains, ln_biases, mix_weights):
    weights_in = tuple((item.astype(jnp.float32) for item in (w_qkv, w_out, w_up, w_down, ln_gains, ln_biases)))

    def run(inputs_now, history_now, weights_now, mix_now):
        return forward(inputs_now, history_now, weights_now, mix_now, span_start)
    result, pull_back = jax.vjp(run, block_input.astype(jnp.float32), history.astype(jnp.float32), weights_in, mix_weights.astype(jnp.float32))
    grad_input, grad_history, grad_weights, grad_mix = pull_back(cotangent.astype(jnp.float32))
    return (result.astype(jnp.bfloat16), grad_input, grad_history, grad_mix, grad_weights[0], grad_weights[1], grad_weights[2], grad_weights[3], grad_weights[4], grad_weights[5][0], grad_weights[5][1])
```

```python
import functools
import jax
import jax.numpy as jnp
import numpy as np
from jax import lax
from jax.experimental import pallas as pl
from jax.experimental.pallas import tpu as pltpu
from jax.sharding import PartitionSpec as P

BF = jnp.bfloat16
F32 = jnp.float32
HEADS = 12
SPAN = 256
BL = 256
NEG = -1e30
EPS = 1e-05
FB = 256


def dot(a, b):
    return lax.dot_general(a, b, (((1,), (0,)), ((), ())), preferred_element_type=F32)


def dot_bt(a, b):
    return lax.dot_general(a, b, (((1,), (1,)), ((), ())), preferred_element_type=F32)


def dot_at(a, b):
    return lax.dot_general(a, b, (((0,), (0,)), ((), ())), preferred_element_type=F32)


def iota(shape, axis):
    return lax.broadcasted_iota(jnp.int32, shape, axis)


def cols(start, width=128):
    return pl.ds(pl.multiple_of(start, 128), width)


def rows(start, height):
    return pl.ds(pl.multiple_of(start, height), height)


def norm_parts(values):
    average = jnp.mean(values, axis=-1, keepdims=True)
    centered = values - average
    inverse_std = lax.rsqrt(jnp.mean(centered * centered, axis=-1, keepdims=True) + EPS)
    return centered * inverse_std, inverse_std


def norm_back(incoming, normed, inverse_std, gain_row):
    scaled = incoming * gain_row
    inner = (
        scaled
        - jnp.mean(scaled, axis=-1, keepdims=True)
        - normed * jnp.mean(scaled * normed, axis=-1, keepdims=True)
    )
    return inverse_std * inner


def fold8(values):
    return jnp.sum(values.reshape(values.shape[0] // 8, 8, values.shape[1]), axis=0)


def turn(values, low_quarter):
    return jnp.where(low_quarter, pltpu.roll(values, 96, 1), pltpu.roll(values, 32, 1))


def gelu_parts(upper):
    size = jnp.abs(upper)
    t = 1.0 / (1.0 + 0.2316419 * size)
    density = jnp.exp(-0.5 * upper * upper) * 0.3989422804014327
    poly = ((((1.330274429 * t - 1.821255978) * t + 1.781477937) * t - 0.356563782) * t + 0.319381530) * t
    tail = density * poly
    cdf = jnp.where(upper >= 0, 1.0 - tail, tail)
    return upper * cdf, cdf + upper * density


def split3(values):
    high = values.astype(BF)
    rest = values - high.astype(F32)
    mid = rest.astype(BF)
    return high, mid, (rest - mid.astype(F32)).astype(BF)


def block_bias(start, query0, key0, causal, transposed):
    query = query0 + iota((BL, BL), 1 if transposed else 0)
    key = key0 + iota((BL, BL), 0 if transposed else 1)
    inside = (query >= start) & (query < start + SPAN) & (key >= start) & (key < start + SPAN)
    seen = (inside | (key <= query)) if causal else inside
    return jnp.where(seen, 0.0, NEG).astype(F32)


def fill_bias(start, bias_ref, blocks, transposed):
    span_block = start // BL
    for i in range(blocks):
        bias_ref[i] = block_bias(start, i * BL, i * BL, True, transposed)
    extra = block_bias(start, span_block * BL, (span_block + 1) * BL, False, transposed)
    bias_ref[blocks] = jnp.where(span_block + 1 < blocks, extra, NEG)


def attend_forward(start, qkv_ref, bias_ref, out_ref, lse_ref):
    length, width = out_ref.shape
    blocks = length // BL
    fill_bias(start, bias_ref, blocks, False)
    span_block = start // BL
    next_block = jnp.minimum(span_block + 1, blocks - 1)
    first = iota((BL, 128), 1) < 64
    first_all = iota((length, 128), 1) < 64
    zero = jnp.zeros((), BF)
    one = jnp.ones((), BF)

    def pair(h, carry):
        qc, kc, vc = cols(h * 128), cols(width + h * 128), cols(2 * width + h * 128)
        keys = qkv_ref[:, kc]
        values = qkv_ref[:, vc]
        with_ones = (jnp.where(first_all, values, one), jnp.where(first_all, one, values))
        qx = qkv_ref[rows(span_block * BL, BL), qc]
        kx = qkv_ref[rows(next_block * BL, BL), kc]
        vx = qkv_ref[rows(next_block * BL, BL), vc]
        extra = []
        for head in (0, 1):
            mine = first if head == 0 else ~first
            s = dot_bt(jnp.where(mine, qx, zero), kx) + bias_ref[blocks]
            peak = jnp.max(s, axis=1, keepdims=True)
            extra.append((peak, dot(jnp.exp(s - peak).astype(BF), jnp.where(mine, vx, one))))
        for i in range(blocks):
            outs, peaks = [], []
            here = span_block == i
            qi = qkv_ref[pl.ds(i * BL, BL), qc]
            for head in (0, 1):
                mine = first if head == 0 else ~first
                qm = jnp.where(mine, qi, zero)
                extra_peak, extra_out = extra[head]
                diag = dot_bt(qm, keys[i * BL : (i + 1) * BL]) + bias_ref[i]
                peak = jnp.max(diag, axis=1, keepdims=True)
                if i > 0:
                    left = dot_bt(qm, keys[: i * BL])
                    peak = jnp.maximum(peak, jnp.max(left, axis=1, keepdims=True))
                if i < blocks - 1:
                    peak = jnp.maximum(peak, jnp.where(here, extra_peak, NEG))
                out = dot(jnp.exp(diag - peak).astype(BF), with_ones[head][i * BL : (i + 1) * BL])
                if i > 0:
                    out = out + dot(jnp.exp(left - peak).astype(BF), with_ones[head][: i * BL])
                if i < blocks - 1:
                    out = out + jnp.where(here, jnp.exp(extra_peak - peak), 0.0) * extra_out
                outs.append(out)
                peaks.append(peak)
            top = jnp.where(first, outs[0], outs[1])
            total = pltpu.roll(jnp.where(first, outs[1], outs[0]), 64, 1)
            out_ref[pl.ds(i * BL, BL), qc] = (top / total).astype(BF)
            lse_ref[pl.ds(i * BL, BL), qc] = jnp.where(first, peaks[0], peaks[1]) + jnp.log(total)
        return carry

    lax.fori_loop(0, width // 128, pair, 0)


def attend_backward(start, qkv_ref, do_ref, out_ref, lse_ref, cos_ref, sin_ref, bias_ref, dq_ref):
    length, width = out_ref.shape
    blocks = length // BL
    fill_bias(start, bias_ref, blocks, True)
    span_block = start // BL
    next_block = jnp.minimum(span_block + 1, blocks - 1)
    lane_all = iota((length, 128), 1)
    lane = iota((BL, 128), 1)
    first = lane < 64
    low_quarter = (lane % 64) < 32
    zero = jnp.zeros((), BF)
    one = jnp.ones((), BF)

    def extend(values, column, head, lanes):
        a, b, c = split3(-column)
        base = 64 * (1 - head)
        parts = jnp.where(
            lanes == base, a, jnp.where(lanes == base + 1, b, jnp.where(lanes == base + 2, c, zero))
        )
        return jnp.where(lanes < 64, values, parts) if head == 0 else jnp.where(lanes < 64, parts, values)

    def keep(values, head, lanes, other):
        return jnp.where(lanes < 64, values, other) if head == 0 else jnp.where(lanes < 64, other, values)

    def rotate_back(values, cosine, sine):
        return values * cosine - turn(values, low_quarter) * sine

    def pair(h, carry):
        qc, kc, vc = cols(h * 128), cols(width + h * 128), cols(2 * width + h * 128)

        def query_side(at, lanes):
            q = qkv_ref[at, qc]
            do = do_ref[at, qc]
            lse = lse_ref[at, qc]
            product = do.astype(F32) * out_ref[at, qc].astype(F32)
            sides = []
            for head in (0, 1):
                mine = (lanes < 64) if head == 0 else (lanes >= 64)
                delta = jnp.sum(jnp.where(mine, product, 0.0), axis=1, keepdims=True)
                sides.append(
                    (
                        extend(q, lse[:, 64 * head : 64 * head + 1], head, lanes),
                        keep(q, head, lanes, zero),
                        extend(do, delta, head, lanes),
                        keep(do, head, lanes, zero),
                    )
                )
            return sides

        everything = query_side(slice(None), lane_all)
        extra_side = query_side(rows(span_block * BL, BL), lane)
        kx = qkv_ref[rows(next_block * BL, BL), kc]
        vx = qkv_ref[rows(next_block * BL, BL), vc]

        def block(k, v, head, qa, qm, da, dm, bias):
            s = dot_bt(keep(k, head, lane, one), qa)
            if bias is not None:
                s = s + bias
            p = jnp.exp(s)
            ds = (p * dot_bt(keep(v, head, lane, one), da)).astype(BF)
            return dot(p.astype(BF), dm), dot(ds, qm), dot_at(ds, keep(k, head, lane, zero))

        parts = [block(kx, vx, head, *extra_side[head], bias_ref[blocks]) for head in (0, 1)]
        dvx, dkx, dqx = [a + b for a, b in zip(*parts)]
        for j in range(blocks):
            at = slice(j * BL, (j + 1) * BL)
            rest = slice((j + 1) * BL, length)
            kj = qkv_ref[at, kc]
            vj = qkv_ref[at, vc]
            dv = jnp.where(span_block + 1 == j, dvx, 0.0) if j > 0 else None
            dk = jnp.where(span_block + 1 == j, dkx, 0.0) if j > 0 else None
            dq = jnp.where(span_block == j, dqx, 0.0) if j < blocks - 1 else None
            dq_rest = None
            add = lambda old, new: new if old is None else old + new
            for head in (0, 1):
                side = everything[head]
                a, b, c = block(kj, vj, head, *[item[at] for item in side], bias_ref[j])
                dv, dk, dq = add(dv, a), add(dk, b), add(dq, c)
                if j < blocks - 1:
                    a, b, c = block(kj, vj, head, *[item[rest] for item in side], None)
                    dv, dk, dq_rest = add(dv, a), add(dk, b), add(dq_rest, c)
            cosine, sine = cos_ref[at], sin_ref[at]
            if j > 0:
                dq = dq + dq_ref[at]
            qkv_ref[at, vc] = dv.astype(BF)
            qkv_ref[at, kc] = rotate_back(dk, cosine, sine).astype(BF)
            qkv_ref[at, qc] = rotate_back(dq * 0.125, cosine, sine).astype(BF)
            if j < blocks - 1:
                dq_ref[rest] = dq_rest if j == 0 else dq_ref[rest] + dq_rest
        return carry

    lax.fori_loop(0, width // 128, pair, 0)


def first_norm(x_ref, par_ref, act_ref):
    height = 128

    def chunk(r, carry):
        at = rows(r * height, height)
        normed, _ = norm_parts(x_ref[at, :].astype(F32))
        act_ref[at, :] = (normed * par_ref[0:1, :] + par_ref[2:3, :]).astype(BF)
        return carry

    lax.fori_loop(0, x_ref.shape[0] // height, chunk, 0)


def project(act_ref, wq_ref, cos_ref, sin_ref, qkv_ref):
    width = act_ref.shape[1]
    low_quarter = (iota((act_ref.shape[0], 128), 1) % 64) < 32

    def rotated(c, carry):
        out = dot(act_ref[...], wq_ref[:, cols(c * 256, 256)])
        scale = jnp.where(c < width // 256, 0.125, 1.0)
        for half in (0, 1):
            u = out[:, half * 128 : half * 128 + 128]
            u = (u * cos_ref[...] + turn(u, low_quarter) * sin_ref[...]) * scale
            qkv_ref[:, cols(c * 256 + half * 128)] = u.astype(BF)
        return carry

    def plain(c, carry):
        at = cols(2 * width + c * 256, 256)
        qkv_ref[:, at] = dot(act_ref[...], wq_ref[:, at]).astype(BF)
        return carry

    lax.fori_loop(0, 2 * width // 256, rotated, 0)
    lax.fori_loop(0, width // 256, plain, 0)


def attention_out(x_ref, mixed_ref, wo_ref, par_ref, middle_ref, act_ref, actt_ref):
    height = 256

    def chunk(r, carry):
        at = rows(r * height, height)
        middle = x_ref[at, :].astype(F32) + dot(mixed_ref[at, :], wo_ref[...])
        middle_ref[at, :] = middle
        normed, _ = norm_parts(middle)
        act = (normed * par_ref[1:2, :] + par_ref[3:4, :]).astype(BF)
        act_ref[at, :] = act
        actt_ref[:, rows(r * height, height)] = act.T
        return carry

    lax.fori_loop(0, x_ref.shape[0] // height, chunk, 0)


def feed_forward(act_ref, actt_ref, gb_ref, wu_ref, wd_ref, out_ref, dact_ref):
    out_ref[...] = jnp.zeros_like(out_ref)
    dact_ref[...] = jnp.zeros_like(dact_ref)
    feed_forward_blocks(0, wd_ref.shape[0] // FB, act_ref, actt_ref, gb_ref, wu_ref, wd_ref, out_ref, dact_ref)


def feed_forward_blocks(low, high, act_ref, actt_ref, gb_ref, wu_ref, wd_ref, out_ref, dact_ref):
    def block(b, carry):
        c = cols(b * FB, FB)
        r = rows(b * FB, FB)
        wu = wu_ref[:, c]
        wd = wd_ref[r, :]
        hidden, slope = gelu_parts(dot(act_ref[...], wu))
        hidden = hidden.astype(BF)
        out_ref[...] += dot(hidden, wd)
        gu = (dot_bt(gb_ref[...], wd) * slope).astype(BF)
        dact_ref[...] += dot_bt(gu, wu)
        wd_ref[r, :] = dot_at(hidden, gb_ref[...]).astype(BF)
        wu_ref[:, c] = dot(actt_ref[...], gu).astype(BF)
        return carry

    lax.fori_loop(low, high, block, 0)


def branch_grad(mix4, g_ref, gb_ref):
    height = 256

    def chunk(r, carry):
        at = rows(r * height, height)
        gb_ref[at, :] = (mix4 * g_ref[at, :].astype(F32)).astype(BF)
        return carry

    lax.fori_loop(0, g_ref.shape[0] // height, chunk, 0)


def middle_back(mix4, g_ref, earlier_ref, middle_ref, out_ref, dact_ref, mixed_ref, wo_ref, par_ref,
                next_ref, ga_ref, do_ref, go_ref, small_ref):
    height = 256
    width = g_ref.shape[1]
    zero = jnp.zeros((8, width), F32)

    def chunk(r, carry):
        gain, bias, terms = carry
        at = rows(r * height, height)
        g = g_ref[at, :].astype(F32)
        middle = middle_ref[at, :]
        output = middle + out_ref[at, :]
        next_ref[at, :] = (earlier_ref[at, :].astype(F32) + mix4 * output).astype(BF)
        terms = terms + fold8(g * output)
        normed, inverse = norm_parts(middle)
        dact = dact_ref[at, :]
        gain = gain + fold8(dact * normed)
        bias = bias + fold8(dact)
        grad = mix4 * g + norm_back(dact, normed, inverse, par_ref[1:2, :])
        dact_ref[at, :] = grad
        low = grad.astype(BF)
        ga_ref[at, :] = low
        do_ref[at, :] = dot_bt(low, wo_ref[...]).astype(BF)
        return gain, bias, terms

    gain, bias, terms = lax.fori_loop(0, g_ref.shape[0] // height, chunk, (zero, zero, zero))
    small_ref[1:2, :] = jnp.sum(gain, axis=0, keepdims=True)
    small_ref[3:4, :] = jnp.sum(bias, axis=0, keepdims=True)
    small_ref[4:5, :] = jnp.sum(terms, axis=0, keepdims=True)
    go_ref[...] = dot_at(mixed_ref[...], ga_ref[...]).astype(BF)


def project_grad(act_ref, actt_ref, qkv_ref, gq_ref):
    actt_ref[...] = act_ref[...].T

    def block(c, carry):
        at = cols(c * 256, 256)
        gq_ref[:, at] = dot(actt_ref[...], qkv_ref[:, at]).astype(BF)
        return carry

    lax.fori_loop(0, qkv_ref.shape[1] // 256, block, 0)


def first_back(x_ref, qkv_ref, wq_ref, par_ref, dmid_ref, small_ref):
    height = 256
    zero = jnp.zeros((8, x_ref.shape[1]), F32)

    def chunk(r, carry):
        gain, bias = carry
        at = rows(r * height, height)
        dact = dot_bt(qkv_ref[at, :], wq_ref[...])
        normed, inverse = norm_parts(x_ref[at, :].astype(F32))
        gain = gain + fold8(dact * normed)
        bias = bias + fold8(dact)
        dmid_ref[at, :] += norm_back(dact, normed, inverse, par_ref[0:1, :])
        return gain, bias

    gain, bias = lax.fori_loop(0, x_ref.shape[0] // height, chunk, (zero, zero))
    small_ref[0:1, :] = jnp.sum(gain, axis=0, keepdims=True)
    small_ref[2:3, :] = jnp.sum(bias, axis=0, keepdims=True)


def block_kernel(start_ref, mix_ref, x_hbm, g_hbm, earlier_hbm, par_ref, cos_ref, sin_ref, wq_hbm, wo_hbm, wu_hbm, wd_hbm,
                 next_hbm, dx_hbm, gq_hbm, go_hbm, gu_hbm, gd_hbm, small_ref,
                 x, g, gb, act1, act2, actt, mixed, earlier, qkv, lse, middle, out, dact, wq, wo, wu, wd, gq, go, bias, dq, sems):
    loads = [
        pltpu.make_async_copy(a, b, sems.at[i])
        for i, (a, b) in enumerate(
            [(x_hbm, x), (wq_hbm, wq), (g_hbm, g), (earlier_hbm, earlier), (wo_hbm, wo), (wu_hbm, wu), (wd_hbm, wd)]
        )
    ]
    for copy in loads:
        copy.start()
    small_ref[...] = jnp.zeros_like(small_ref)
    start = start_ref[0]
    mix4 = mix_ref[4]
    loads[0].wait()
    first_norm(x, par_ref, act1)
    loads[1].wait()
    project(act1, wq, cos_ref, sin_ref, qkv)
    attend_forward(start, qkv, bias, mixed, lse)
    for copy in loads[2:]:
        copy.wait()
    branch_grad(mix4, g, gb)
    attention_out(x, mixed, wo, par_ref, middle, act2, actt)
    feed_forward(act2, actt, gb, wu, wd, out, dact)
    ga, do, nxt = gb, act2, earlier
    middle_back(mix4, g, earlier, middle, out, dact, mixed, wo, par_ref, nxt, ga, do, go, small_ref)
    stores = [
        pltpu.make_async_copy(a, b, sems.at[i])
        for i, (a, b) in enumerate(
            [(nxt, next_hbm), (wu, gu_hbm), (wd, gd_hbm), (go, go_hbm), (gq, gq_hbm), (dact, dx_hbm)]
        )
    ]
    for copy in stores[:4]:
        copy.start()
    attend_backward(start, qkv, do, mixed, lse, cos_ref, sin_ref, bias, dq)
    project_grad(act1, actt, qkv, gq)
    stores[4].start()
    first_back(x, qkv, wq, par_ref, dact, small_ref)
    stores[5].start()
    for copy in stores:
        copy.wait()


def rotary_tables(length):
    freq = np.exp(-np.log(10000.0) * np.arange(32) / 32.0)
    angles = np.arange(length)[:, None] * freq[None, :]
    c, s = np.cos(angles), np.sin(angles)
    return (
        jnp.asarray(np.concatenate([c, c, c, c], axis=1), F32),
        jnp.asarray(np.concatenate([-s, s, -s, s], axis=1), F32),
    )


def history_kernel(mix_ref, history_ref, g_ref, grad_ref, earlier_ref, terms_ref):
    g = g_ref[...].astype(F32)
    earlier = None
    parts = []
    for k in range(history_ref.shape[0]):
        h = history_ref[k].astype(F32)
        grad_ref[k] = mix_ref[k] * g
        term = mix_ref[k] * h
        earlier = term if earlier is None else earlier + term
        parts.append(jnp.sum(fold8(h * g), axis=0, keepdims=True))
    earlier_ref[...] = earlier.astype(BF)
    new = jnp.concatenate(parts + [jnp.zeros((8 - len(parts), g.shape[1]), F32)], axis=0)

    @pl.when(pl.program_id(0) == 0)
    def _():
        terms_ref[...] = new

    @pl.when(pl.program_id(0) > 0)
    def _():
        terms_ref[...] += new


def history_pass(mix, history, g):
    past, length, width = history.shape
    height = 128
    return pl.pallas_call(
        history_kernel,
        grid=(length // height,),
        in_specs=[
            pl.BlockSpec(memory_space=pltpu.SMEM),
            pl.BlockSpec((past, height, width), lambda i: (0, i, 0)),
            pl.BlockSpec((height, width), lambda i: (i, 0)),
        ],
        out_specs=(
            pl.BlockSpec((past, height, width), lambda i: (0, i, 0)),
            pl.BlockSpec((height, width), lambda i: (i, 0)),
            pl.BlockSpec((8, width), lambda i: (0, 0)),
        ),
        out_shape=(
            jax.ShapeDtypeStruct((past, length, width), F32),
            jax.ShapeDtypeStruct((length, width), BF),
            jax.ShapeDtypeStruct((8, width), F32),
        ),
        name="history_pass",
    )(mix, history, g)


VMEM_LIMIT = 67043328


def block_pass(start, mix, x, g, earlier, par, wq, wo, wu, wd):
    length, width = x.shape
    ff = wd.shape[0]
    cosine, sine = rotary_tables(length)
    smem = pl.BlockSpec(memory_space=pltpu.SMEM)
    vmem = pl.BlockSpec(memory_space=pltpu.VMEM)
    anys = pl.BlockSpec(memory_space=pl.ANY)
    low = pltpu.VMEM((length, width), BF)
    full = pltpu.VMEM((length, width), F32)
    return pl.pallas_call(
        block_kernel,
        in_specs=[smem, smem, anys, anys, anys, vmem, vmem, vmem, anys, anys, anys, anys],
        out_specs=(anys,) * 6 + (vmem,),
        out_shape=(
            jax.ShapeDtypeStruct((length, width), BF),
            jax.ShapeDtypeStruct((length, width), F32),
            jax.ShapeDtypeStruct((width, 3 * width), BF),
            jax.ShapeDtypeStruct((width, width), BF),
            jax.ShapeDtypeStruct((width, ff), BF),
            jax.ShapeDtypeStruct((ff, width), BF),
            jax.ShapeDtypeStruct((8, width), F32),
        ),
        scratch_shapes=[low] * 5
        + [pltpu.VMEM((width, length), BF)]
        + [low] * 2
        + [pltpu.VMEM((length, 3 * width), BF)]
        + [full] * 4
        + [
            pltpu.VMEM((width, 3 * width), BF),
            pltpu.VMEM((width, width), BF),
            pltpu.VMEM((width, ff), BF),
            pltpu.VMEM((ff, width), BF),
            pltpu.VMEM((width, 3 * width), BF),
            pltpu.VMEM((width, width), BF),
            pltpu.VMEM((length // BL + 1, BL, BL), F32),
            pltpu.VMEM((length, 128), F32),
            pltpu.SemaphoreType.DMA((8,)),
        ],
        compiler_params=pltpu.CompilerParams(vmem_limit_bytes=VMEM_LIMIT),
        name="block_pass",
    )(start, mix, x, g, earlier, par, cosine, sine, wq, wo, wu, wd)


def local(block_input, history, cotangent, span_start, w_qkv, w_out, w_up, w_down, ln_gains, ln_biases, mix_weights):
    gather = lambda item, axis: lax.all_gather(item, "shard", axis=axis, tiled=True)
    norms = gather(jnp.concatenate([ln_gains, ln_biases]), 1).astype(F32)
    par = jnp.concatenate([norms, norms])
    grad_history, earlier, terms = history_pass(mix_weights, history, cotangent)
    nxt, grad_input, gq, go, gu, gd, small = block_pass(
        span_start, mix_weights, block_input, cotangent, earlier, par,
        gather(w_qkv, 0), gather(w_out, 0), gather(w_up, 0), gather(w_down, 0),
    )
    past = history.shape[0]
    partial_mix = jnp.concatenate([jnp.sum(terms[:past], axis=1), jnp.sum(small[4:5], axis=1)])
    grad_mix = lax.psum(partial_mix, ("rep", "shard"))

    def owned(item, axis):
        part = lax.psum_scatter(item.astype(BF), "shard", scatter_dimension=axis, tiled=True)
        return lax.psum(part, "rep").astype(F32)

    norm_grads = owned(small[:4], 1)
    return (
        nxt, grad_input, grad_history, grad_mix,
        owned(gq, 0), owned(go, 0), owned(gu, 0), owned(gd, 0),
        norm_grads[0:2], norm_grads[2], norm_grads[3],
    )


def solution(mesh):
    token = P(("rep", "shard"), None)
    kept = P("shard", None)
    past = P(None, ("rep", "shard"), None)
    norm = P(None, "shard")
    return jax.shard_map(
        local,
        mesh=mesh,
        in_specs=(token, past, token, P(("rep", "shard")), kept, kept, kept, kept, norm, norm, P()),
        out_specs=(token, token, past, P(), kept, kept, kept, kept, norm, P("shard"), P("shard")),
        check_vma=False,
    )
```

```python
import functools
import jax
import jax.numpy as jnp
import numpy as np
from jax import lax
from jax.experimental import pallas as pl
from jax.experimental.pallas import tpu as pltpu
from jax.sharding import PartitionSpec as P

BF = jnp.bfloat16
F32 = jnp.float32
HEADS = 12
SPAN = 256
BL = 256
NEG = -1e30
EPS = 1e-05
FB = 256


def dot(a, b):
    return lax.dot_general(a, b, (((1,), (0,)), ((), ())), preferred_element_type=F32)


def dot_bt(a, b):
    return lax.dot_general(a, b, (((1,), (1,)), ((), ())), preferred_element_type=F32)


def dot_at(a, b):
    return lax.dot_general(a, b, (((0,), (0,)), ((), ())), preferred_element_type=F32)


def iota(shape, axis):
    return lax.broadcasted_iota(jnp.int32, shape, axis)


def cols(start, width=128):
    return pl.ds(pl.multiple_of(start, 128), width)


def rows(start, height):
    return pl.ds(pl.multiple_of(start, height), height)


def norm_parts(values):
    average = jnp.mean(values, axis=-1, keepdims=True)
    centered = values - average
    inverse_std = lax.rsqrt(jnp.mean(centered * centered, axis=-1, keepdims=True) + EPS)
    return centered * inverse_std, inverse_std


def norm_back(incoming, normed, inverse_std, gain_row):
    scaled = incoming * gain_row
    inner = (
        scaled
        - jnp.mean(scaled, axis=-1, keepdims=True)
        - normed * jnp.mean(scaled * normed, axis=-1, keepdims=True)
    )
    return inverse_std * inner


def fold8(values):
    return jnp.sum(values.reshape(values.shape[0] // 8, 8, values.shape[1]), axis=0)


def turn(values, low_quarter):
    return jnp.where(low_quarter, pltpu.roll(values, 96, 1), pltpu.roll(values, 32, 1))


def gelu_parts(upper):
    size = jnp.abs(upper)
    t = 1.0 / (1.0 + 0.2316419 * size)
    density = jnp.exp(-0.5 * upper * upper) * 0.3989422804014327
    poly = ((((1.330274429 * t - 1.821255978) * t + 1.781477937) * t - 0.356563782) * t + 0.319381530) * t
    tail = density * poly
    cdf = jnp.where(upper >= 0, 1.0 - tail, tail)
    return upper * cdf, cdf + upper * density


def split3(values):
    high = values.astype(BF)
    rest = values - high.astype(F32)
    mid = rest.astype(BF)
    return high, mid, (rest - mid.astype(F32)).astype(BF)


def block_bias(start, query0, key0, causal, transposed):
    query = query0 + iota((BL, BL), 1 if transposed else 0)
    key = key0 + iota((BL, BL), 0 if transposed else 1)
    inside = (query >= start) & (query < start + SPAN) & (key >= start) & (key < start + SPAN)
    seen = (inside | (key <= query)) if causal else inside
    return jnp.where(seen, 0.0, NEG).astype(F32)


def fill_bias(start, bias_ref, blocks, transposed):
    span_block = start // BL
    for i in range(blocks):
        bias_ref[i] = block_bias(start, i * BL, i * BL, True, transposed)
    extra = block_bias(start, span_block * BL, (span_block + 1) * BL, False, transposed)
    bias_ref[blocks] = jnp.where(span_block + 1 < blocks, extra, NEG)


def pick(span_block, blocks, load):
    value = load(0)
    for b in range(1, blocks - 1):
        value = lax.select(span_block == b, load(b), value)
    return value


def forward_pair(h, start, qkv_ref, bias_ref, out_ref, lse_ref):
    length, width = out_ref.shape
    blocks = length // BL
    span_block = start // BL
    first = iota((BL, 128), 1) < 64
    first_all = iota((length, 128), 1) < 64
    zero = jnp.zeros((), BF)
    one = jnp.ones((), BF)

    oc, qc, kc, vc = pair_columns(h)
    keys = qkv_ref[:, kc]
    values = qkv_ref[:, vc]
    with_ones = (jnp.where(first_all, values, one), jnp.where(first_all, one, values))
    qx = pick(span_block, blocks, lambda b: qkv_ref[pl.ds(b * BL, BL), qc])
    kx = pick(span_block, blocks, lambda b: qkv_ref[pl.ds((b + 1) * BL, BL), kc])
    vx = pick(span_block, blocks, lambda b: qkv_ref[pl.ds((b + 1) * BL, BL), vc])
    extra = []
    for head in (0, 1):
        mine = first if head == 0 else ~first
        s = dot_bt(jnp.where(mine, qx, zero), kx) + bias_ref[blocks]
        peak = jnp.max(s, axis=1, keepdims=True)
        extra.append((peak, dot(jnp.exp(s - peak).astype(BF), jnp.where(mine, vx, one))))
    for i in range(blocks):
        outs, peaks = [], []
        here = span_block == i
        qi = qkv_ref[pl.ds(i * BL, BL), qc]
        for head in (0, 1):
            mine = first if head == 0 else ~first
            qm = jnp.where(mine, qi, zero)
            extra_peak, extra_out = extra[head]
            diag = dot_bt(qm, keys[i * BL : (i + 1) * BL]) + bias_ref[i]
            peak = jnp.max(diag, axis=1, keepdims=True)
            if i > 0:
                left = dot_bt(qm, keys[: i * BL])
                peak = jnp.maximum(peak, jnp.max(left, axis=1, keepdims=True))
            if i < blocks - 1:
                peak = jnp.maximum(peak, jnp.where(here, extra_peak, NEG))
            out = dot(jnp.exp(diag - peak).astype(BF), with_ones[head][i * BL : (i + 1) * BL])
            if i > 0:
                out = out + dot(jnp.exp(left - peak).astype(BF), with_ones[head][: i * BL])
            if i < blocks - 1:
                out = out + jnp.where(here, jnp.exp(extra_peak - peak), 0.0) * extra_out
            outs.append(out)
            peaks.append(peak)
        top = jnp.where(first, outs[0], outs[1])
        total = pltpu.roll(jnp.where(first, outs[1], outs[0]), 64, 1)
        out_ref[pl.ds(i * BL, BL), oc] = (top / total).astype(BF)
        lse_ref[pl.ds(i * BL, BL), oc] = jnp.where(first, peaks[0], peaks[1]) + jnp.log(total)


def backward_pair(h, start, qkv_ref, do_ref, out_ref, lse_ref, cos_ref, sin_ref, bias_ref, dq_ref):
    length, width = out_ref.shape
    blocks = length // BL
    span_block = start // BL
    lane_all = iota((length, 128), 1)
    lane = iota((BL, 128), 1)
    first = lane < 64
    low_quarter = (lane % 64) < 32
    zero = jnp.zeros((), BF)
    one = jnp.ones((), BF)

    def extend(values, column, head, lanes):
        a, b, c = split3(-column)
        base = 64 * (1 - head)
        parts = jnp.where(
            lanes == base, a, jnp.where(lanes == base + 1, b, jnp.where(lanes == base + 2, c, zero))
        )
        return jnp.where(lanes < 64, values, parts) if head == 0 else jnp.where(lanes < 64, parts, values)

    def keep(values, head, lanes, other):
        return jnp.where(lanes < 64, values, other) if head == 0 else jnp.where(lanes < 64, other, values)

    def rotate_back(values, cosine, sine):
        return values * cosine - turn(values, low_quarter) * sine

    oc, qc, kc, vc = pair_columns(h)

    def query_side(load, lanes):
        q, do, lse, out = load(qkv_ref, qc), load(do_ref, oc), load(lse_ref, oc), load(out_ref, oc)
        product = do.astype(F32) * out.astype(F32)
        sides = []
        for head in (0, 1):
            mine = (lanes < 64) if head == 0 else (lanes >= 64)
            delta = jnp.sum(jnp.where(mine, product, 0.0), axis=1, keepdims=True)
            sides.append(
                (
                    extend(q, lse[:, 64 * head : 64 * head + 1], head, lanes),
                    keep(q, head, lanes, zero),
                    extend(do, delta, head, lanes),
                    keep(do, head, lanes, zero),
                )
            )
        return sides

    everything = query_side(lambda ref, at: ref[:, at], lane_all)
    extra_side = query_side(
        lambda ref, at: pick(span_block, blocks, lambda b: ref[pl.ds(b * BL, BL), at]), lane
    )
    kx = pick(span_block, blocks, lambda b: qkv_ref[pl.ds((b + 1) * BL, BL), kc])
    vx = pick(span_block, blocks, lambda b: qkv_ref[pl.ds((b + 1) * BL, BL), vc])

    def block(k, v, head, qa, qm, da, dm, bias):
        s = dot_bt(keep(k, head, lane, one), qa)
        if bias is not None:
            s = s + bias
        p = jnp.exp(s)
        ds = (p * dot_bt(keep(v, head, lane, one), da)).astype(BF)
        return dot(p.astype(BF), dm), dot(ds, qm), dot_at(ds, keep(k, head, lane, zero))

    parts = [block(kx, vx, head, *extra_side[head], bias_ref[blocks]) for head in (0, 1)]
    dvx, dkx, dqx = [a + b for a, b in zip(*parts)]
    for j in range(blocks):
        at = slice(j * BL, (j + 1) * BL)
        rest = slice((j + 1) * BL, length)
        kj = qkv_ref[at, kc]
        vj = qkv_ref[at, vc]
        dv = jnp.where(span_block + 1 == j, dvx, 0.0) if j > 0 else None
        dk = jnp.where(span_block + 1 == j, dkx, 0.0) if j > 0 else None
        dq = jnp.where(span_block == j, dqx, 0.0) if j < blocks - 1 else None
        dq_rest = None
        add = lambda old, new: new if old is None else old + new
        for head in (0, 1):
            side = everything[head]
            a, b, c = block(kj, vj, head, *[item[at] for item in side], bias_ref[j])
            dv, dk, dq = add(dv, a), add(dk, b), add(dq, c)
            if j < blocks - 1:
                a, b, c = block(kj, vj, head, *[item[rest] for item in side], None)
                dv, dk, dq_rest = add(dv, a), add(dk, b), add(dq_rest, c)
        cosine, sine = cos_ref[at], sin_ref[at]
        if j > 0:
            dq = dq + dq_ref[at]
        qkv_ref[at, vc] = dv.astype(BF)
        qkv_ref[at, kc] = rotate_back(dk, cosine, sine).astype(BF)
        qkv_ref[at, qc] = rotate_back(dq * 0.125, cosine, sine).astype(BF)
        if j < blocks - 1:
            dq_ref[rest] = dq_rest if j == 0 else dq_ref[rest] + dq_rest


MESH = pl.DeviceIdType.MESH
UNITS = 12
LAST = UNITS + 5


class Place:
    def __init__(self):
        self.y = lax.axis_index("rep")
        s = lax.axis_index("shard")
        self.z, self.x, self.c = s // 4, (s // 2) % 2, s % 2

    def at(self, y, z, x, c):
        return (y, (z * 2 + x) * 2 + c)

    def twin(self):
        return self.at(self.y, self.z, self.x, 1 - self.c)

    def across_x(self):
        return self.at(self.y, self.z, 1 - self.x, self.c)

    def across_y(self):
        return self.at(1 - self.y, self.z, self.x, self.c)

    def along_z(self, k):
        return self.at(self.y, (self.z + k) % 4, self.x, self.c)

    def peers(self):
        return [self.twin(), self.across_x(), self.across_y()] + [self.along_z(k) for k in (1, 2, 3)]


def half(y):
    return pl.ds(pl.multiple_of(y * 384, 128), 384)


def remote(src, dst, sems, slot, kind, device):
    return pltpu.make_async_remote_copy(
        src_ref=src,
        dst_ref=dst,
        send_sem=sems.at[0, slot, kind],
        recv_sem=sems.at[1, slot, kind],
        device_id=device,
        device_id_type=MESH,
    )


class Gather:
    def __init__(self, place, w_ref, sems):
        self.p, self.w, self.sems = place, w_ref, sems

    def copies(self, stage, u, mine):
        p, w = self.p, self.w
        slot = u % 2
        y, z, x, c = p.y, p.z, p.x, p.c

        def same(ref, kind, device):
            return remote(ref, ref, self.sems, slot, kind, device)

        if stage == 0:
            return [
                same(w.at[u, z if mine else (z + 4 - k) % 4, x, c, :, half(y)], k - 1, p.along_z(k)) for k in (1, 2, 3)
            ]
        if stage == 1:
            return [
                same(w.at[u, :, x if mine else 1 - x, c, :, half(y)], 3, p.across_x()),
                same(w.at[u, :, x, c, :, half(y if mine else 1 - y)], 4, p.across_y()),
            ]
        if stage == 2:
            return [
                same(w.at[u, 0:2, x if mine else 1 - x, c, :, half(1 - y)], 5, p.across_x()),
                same(w.at[u, 2:4, 1 - x, c, :, half(y if mine else 1 - y)], 6, p.across_y()),
            ]
        return [same(w.at[u, :, :, c if mine else 1 - c], 7, p.twin())]

    def step(self, stage, u):
        if stage > 0:
            for copy in self.copies(stage - 1, u, False):
                copy.wait_recv()
            for copy in self.copies(stage - 1, u, True):
                copy.wait_send()
        if stage < 4:
            for copy in self.copies(stage, u, True):
                copy.start()

    def tick(self, n):
        for stage in (4, 3, 2, 1, 0):
            u = n - stage
            if isinstance(n, int):
                if 0 <= u < UNITS:
                    self.step(stage, u)
            else:
                pl.when((u >= 0) & (u < UNITS))(functools.partial(self.step, stage, u))


class Reduce:
    def __init__(self, place, w_ref, own_ref, rc, rdx, rdy, rxx, rxy, rz, sems):
        self.p, self.w, self.own, self.sems = place, w_ref, own_ref, sems
        self.rc, self.rdx, self.rdy, self.rxx, self.rxy, self.rz = rc, rdx, rdy, rxx, rxy, rz

    def copies(self, stage, n, mine):
        p, w = self.p, self.w
        u = unit_of(n)
        slot = n % 2
        y, z, x, c = p.y, p.z, p.x, p.c

        def send(src, dst, kind, device):
            return remote(src, dst, self.sems, slot, kind, device)

        if stage == 0:
            return [send(w.at[u, :, :, 1 - c], self.rc.at[slot], 0, p.twin())]
        if stage == 1:
            return [
                send(w.at[u, 0:2, 1 - x, c, :, half(1 - y)], self.rdx.at[slot], 1, p.across_x()),
                send(w.at[u, 2:4, 1 - x, c, :, half(1 - y)], self.rdy.at[slot], 2, p.across_y()),
            ]
        if stage == 2:
            return [
                send(w.at[u, :, 1 - x, c, :, half(y)], self.rxx.at[slot], 3, p.across_x()),
                send(w.at[u, :, x, c, :, half(1 - y)], self.rxy.at[slot], 4, p.across_y()),
            ]
        if stage == 3:
            return [
                send(w.at[u, (z + k) % 4, x, c, :, half(y)], self.rz.at[slot, k - 1], 4 + k, p.along_z(k))
                for k in (1, 2, 3)
            ]
        there = self.own.at[u, :, half(y if mine else 1 - y)]
        return [send(there, there, 8, p.across_y())]

    def add(self, stage, n):
        p, w = self.p, self.w
        u = unit_of(n)
        slot = n % 2
        y, z, x, c = p.y, p.z, p.x, p.c
        f = lambda value: value.astype(F32)
        if stage == 1:

            def piece(zz, carry):
                w[u, zz, :, c] = (f(w[u, zz, :, c]) + f(self.rc[slot, zz])).astype(BF)
                return carry

            lax.fori_loop(0, 4, piece, 0)
        if stage == 2:
            w[u, 0:2, x, c, :, half(1 - y)] = (f(w[u, 0:2, x, c, :, half(1 - y)]) + f(self.rdx[slot])).astype(BF)
            w[u, 2:4, 1 - x, c, :, half(y)] = (f(w[u, 2:4, 1 - x, c, :, half(y)]) + f(self.rdy[slot])).astype(BF)
        if stage == 3:
            w[u, :, x, c, :, half(y)] = (
                f(w[u, :, x, c, :, half(y)]) + f(self.rxx[slot]) + f(self.rxy[slot])
            ).astype(BF)
        if stage == 4:
            total = f(w[u, z, x, c, :, half(y)])
            for k in (0, 1, 2):
                total = total + f(self.rz[slot, k])
            self.own[u, :, half(y)] = total.astype(BF)

    def step(self, stage, n):
        if stage > 0:
            for copy in self.copies(stage - 1, n, False):
                copy.wait_recv()
            for copy in self.copies(stage - 1, n, True):
                copy.wait_send()
            self.add(stage, n)
        if stage < 5:
            for copy in self.copies(stage, n, True):
                copy.start()

    def tick(self, t):
        for stage in (5, 4, 3, 2, 1, 0):
            n = t - stage
            if isinstance(t, int):
                if 0 <= n < UNITS:
                    self.step(stage, n)
            else:
                pl.when((n >= 0) & (n < UNITS))(functools.partial(self.step, stage, n))


def unit_of(n):
    if isinstance(n, int):
        return 8 + n if n < 4 else n if n < 8 else 3 if n == 8 else n - 9
    return jnp.where(n < 4, 8 + n, jnp.where(n < 8, n, jnp.where(n == 8, 3, n - 9)))


def small_sum(place, value, stage_ref, land_ref, z_ref, sems, with_y):
    steps = [(0, place.twin()), (1, place.across_x())] + ([(2, place.across_y())] if with_y else [])
    for i, device in steps:
        stage_ref[i] = value
        copy = remote(stage_ref.at[i], land_ref.at[i], sems, 0, i, device)
        copy.start()
        copy.wait()
        value = value + land_ref[i]
    z_ref[0] = value
    sent = [remote(z_ref.at[0], z_ref.at[k], sems, 0, 2 + k, place.along_z(k)) for k in (1, 2, 3)]
    for copy in sent:
        copy.start()
    for copy in sent:
        copy.wait()
    total = None
    for zz in range(4):
        part = z_ref[(place.z + 4 - zz) % 4]
        total = part if total is None else total + part
    return total


def history_kernel(mix_ref, history_ref, g_ref, grad_ref, earlier_ref, terms_ref):
    g = g_ref[...].astype(F32)
    earlier = None
    parts = []
    for k in range(history_ref.shape[0]):
        h = history_ref[k].astype(F32)
        grad_ref[k] = mix_ref[k] * g
        term = mix_ref[k] * h
        earlier = term if earlier is None else earlier + term
        parts.append(jnp.sum(fold8(h * g), axis=0, keepdims=True))
    earlier_ref[...] = earlier.astype(BF)
    new = jnp.concatenate(parts + [jnp.zeros((8 - len(parts), g.shape[1]), F32)], axis=0)

    @pl.when(pl.program_id(0) == 0)
    def _():
        terms_ref[...] = new

    @pl.when(pl.program_id(0) > 0)
    def _():
        terms_ref[...] += new


def history_pass(mix, history, g):
    past, length, width = history.shape
    height = 128
    return pl.pallas_call(
        history_kernel,
        grid=(length // height,),
        in_specs=[
            pl.BlockSpec(memory_space=pltpu.SMEM),
            pl.BlockSpec((past, height, width), lambda i: (0, i, 0)),
            pl.BlockSpec((height, width), lambda i: (i, 0)),
        ],
        out_specs=(
            pl.BlockSpec((past, height, width), lambda i: (0, i, 0)),
            pl.BlockSpec((height, width), lambda i: (i, 0)),
            pl.BlockSpec((8, width), lambda i: (0, 0)),
        ),
        out_shape=(
            jax.ShapeDtypeStruct((past, length, width), F32),
            jax.ShapeDtypeStruct((length, width), BF),
            jax.ShapeDtypeStruct((8, width), F32),
        ),
        name="history_pass",
    )(mix, history, g)


def first_norm(x_ref, par_ref, act_ref):
    height = 128

    def chunk(r, carry):
        at = rows(r * height, height)
        normed, _ = norm_parts(x_ref[at, :].astype(F32))
        act_ref[at, :] = (normed * par_ref[0:1, :] + par_ref[2:3, :]).astype(BF)
        return carry

    lax.fori_loop(0, x_ref.shape[0] // height, chunk, 0)


def pair_columns(h):
    base = (h // 2) * 768 + (h % 2) * 128
    return cols(h * 128), cols(base), cols(base + 256), cols(base + 512)


def unit(w_ref, u):
    return w_ref[u].reshape(768, 768)


def project(j, act_ref, w_ref, cos_ref, sin_ref, qkv_ref):
    height = 256
    low_quarter = (iota((height, 128), 1) % 64) < 32

    def chunk(r, carry):
        at = rows(r * height, height)
        out = dot(act_ref[at, :], unit(w_ref, j))
        cosine, sine = cos_ref[at, :], sin_ref[at, :]
        for piece in range(6):
            u = out[:, piece * 128 : piece * 128 + 128]
            if piece < 4:
                u = u * cosine + turn(u, low_quarter) * sine
            if piece < 2:
                u = u * 0.125
            qkv_ref[at, cols(j * 768 + piece * 128)] = u.astype(BF)
        return carry

    lax.fori_loop(0, act_ref.shape[0] // height, chunk, 0)


def attention_out(x_ref, mixed_ref, w_ref, par_ref, middle_ref, act_ref, actt_ref, out_ref, dact_ref):
    height = 256

    def chunk(r, carry):
        at = rows(r * height, height)
        middle = x_ref[at, :].astype(F32) + dot(mixed_ref[at, :], unit(w_ref, 3))
        middle_ref[at, :] = middle
        out_ref[at, :] = middle
        dact_ref[at, :] = jnp.zeros_like(middle)
        normed, _ = norm_parts(middle)
        act = (normed * par_ref[1:2, :] + par_ref[3:4, :]).astype(BF)
        act_ref[at, :] = act
        actt_ref[:, rows(r * height, height)] = act.T
        return carry

    lax.fori_loop(0, x_ref.shape[0] // height, chunk, 0)


def down_pieces():
    return [(x, c, q) for x in (0, 1) for c in (0, 1) for q in range(4)]


def feed_forward(z, act_ref, actt_ref, gb_ref, w_ref, hid_ref, gu_ref, out_ref, dact_ref):
    height = 256

    def chunk(r, carry):
        at = rows(r * height, height)
        up = unit(w_ref, 8 + z)
        down = jnp.concatenate([w_ref[4 + q, z, x, c] for x, c, q in down_pieces()], axis=0)
        hidden, slope = gelu_parts(dot(act_ref[at, :], up))
        hidden = hidden.astype(BF)
        hid_ref[at, :] = hidden
        gu = (dot_bt(gb_ref[at, :], down) * slope).astype(BF)
        gu_ref[at, :] = gu
        out_ref[at, :] += dot(hidden, down)
        dact_ref[at, :] += dot_bt(gu, up)
        return carry

    lax.fori_loop(0, act_ref.shape[0] // height, chunk, 0)
    grad = dot_at(hid_ref[...], gb_ref[...]).astype(BF)
    for i, (x, c, q) in enumerate(down_pieces()):
        w_ref[4 + q, z, x, c] = grad[48 * i : 48 * i + 48]
    w_ref[8 + z] = dot(actt_ref[...], gu_ref[...]).astype(BF).reshape(w_ref.shape[1:])


def branch_grad(mix4, g_ref, gb_ref):
    height = 256

    def chunk(r, carry):
        at = rows(r * height, height)
        gb_ref[at, :] = (mix4 * g_ref[at, :].astype(F32)).astype(BF)
        return carry

    lax.fori_loop(0, g_ref.shape[0] // height, chunk, 0)


def middle_back(mix4, g_ref, earlier_ref, middle_ref, out_ref, dact_ref, mixed_ref, w_ref, par_ref,
                next_ref, ga_ref, do_ref, small_ref):
    height = 256
    width = g_ref.shape[1]
    zero = jnp.zeros((8, width), F32)

    def chunk(r, carry):
        gain, bias, terms = carry
        at = rows(r * height, height)
        g = g_ref[at, :].astype(F32)
        output = out_ref[at, :]
        next_ref[at, :] = (earlier_ref[at, :].astype(F32) + mix4 * output).astype(BF)
        terms = terms + fold8(g * output)
        normed, inverse = norm_parts(middle_ref[at, :])
        dact = dact_ref[at, :]
        gain = gain + fold8(dact * normed)
        bias = bias + fold8(dact)
        grad = mix4 * g + norm_back(dact, normed, inverse, par_ref[1:2, :])
        dact_ref[at, :] = grad
        low = grad.astype(BF)
        ga_ref[at, :] = low
        do_ref[at, :] = dot_bt(low, unit(w_ref, 3)).astype(BF)
        return gain, bias, terms

    gain, bias, terms = lax.fori_loop(0, g_ref.shape[0] // height, chunk, (zero, zero, zero))
    small_ref[1:2, :] = jnp.sum(gain, axis=0, keepdims=True)
    small_ref[3:4, :] = jnp.sum(bias, axis=0, keepdims=True)
    small_ref[5:6, :] = jnp.sum(terms, axis=0, keepdims=True)
    w_ref[3] = dot_at(mixed_ref[...], ga_ref[...]).astype(BF).reshape(w_ref.shape[1:])


def project_back(j, actt_ref, qkv_ref, w_ref, out_ref):
    height = 256

    def chunk(r, carry):
        at = rows(r * height, height)
        share = dot_bt(qkv_ref[at, cols(j * 768, 768)], unit(w_ref, j))
        out_ref[at, :] = jnp.where(j == 0, 0.0, out_ref[at, :]) + share
        return carry

    lax.fori_loop(0, qkv_ref.shape[0] // height, chunk, 0)
    w_ref[j] = dot(actt_ref[...], qkv_ref[:, cols(j * 768, 768)]).astype(BF).reshape(w_ref.shape[1:])


def first_back(x_ref, dact_ref, par_ref, dmid_ref, small_ref):
    height = 128
    zero = jnp.zeros((8, x_ref.shape[1]), F32)

    def chunk(r, carry):
        gain, bias = carry
        at = rows(r * height, height)
        dact = dact_ref[at, :]
        normed, inverse = norm_parts(x_ref[at, :].astype(F32))
        gain = gain + fold8(dact * normed)
        bias = bias + fold8(dact)
        dmid_ref[at, :] += norm_back(dact, normed, inverse, par_ref[0:1, :])
        return gain, bias

    gain, bias = lax.fori_loop(0, x_ref.shape[0] // height, chunk, (zero, zero))
    small_ref[0:1, :] = jnp.sum(gain, axis=0, keepdims=True)
    small_ref[2:3, :] = jnp.sum(bias, axis=0, keepdims=True)


def fill_tables(table_ref, cos_ref, sin_ref):
    blocks = cos_ref.shape[0] // 32
    cb, sb, sign = table_ref[0], table_ref[1], table_ref[2]

    def block(a, carry):
        ca, sa = table_ref[3, pl.ds(a, 1), :], table_ref[4, pl.ds(a, 1), :]
        at = rows(a * 32, 32)
        cos_ref[at, :] = ca * cb - sa * sb
        sin_ref[at, :] = (sa * cb + ca * sb) * sign
        return carry

    lax.fori_loop(0, blocks, block, 0)


def rotary_table(length):
    freq = np.tile(np.exp(-np.log(10000.0) * np.arange(32) / 32.0), 4)[None, :]
    fine = np.arange(32)[:, None] * freq
    coarse = 32 * np.arange(32)[:, None] * freq
    sign = np.tile(np.repeat([-1.0, 1.0], 32), 2)[None, :] * np.ones((32, 1))
    return jnp.asarray(np.stack([np.cos(fine), np.sin(fine), sign, np.cos(coarse), np.sin(coarse)]), F32)


def block_kernel(joined, *refs):
    if joined:
        start_ref, mix_ref, x_hbm, g_hbm, earlier_hbm, par_in, terms_ref, table_ref, wq_hbm, wo_hbm, wu_hbm, wd_hbm = refs[:12]
        next_hbm, dx_hbm, own_hbm, small_out = refs[12:16]
        refs = refs[16:]
    else:
        start_ref, mix_ref, x_hbm, g_hbm, earlier_hbm, par_in, terms_ref, table_ref, w_hbm = refs[:9]
        next_hbm, dx_hbm, grad_hbm, small_out = refs[9:13]
        refs = refs[13:]
    x, g, gb, act1, act2, actt, mixed, earlier, hid, gu, qkv, lse, middle, out, dact = refs[:15]
    w, bias, dq, cosine, sine, small, par, loads = refs[15:23]
    start = start_ref[0]
    mix4 = mix_ref[4]

    load = lambda src, dst, i: pltpu.make_async_copy(src, dst, loads.at[i])
    first = [load(x_hbm, x, 0)]
    later = [load(g_hbm, g, 1), load(earlier_hbm, earlier, 2)]
    if joined:
        own, rc, rdx, rdy, rxx, rxy, rz, stage_ref, land_ref, z_ref, gsems, rsems, ssems = refs[23:]
        place = Place()
        home = w.at[:, place.z, place.x, place.c]
        for j in range(3):
            for t in range(3):
                first.append(
                    load(wq_hbm.at[:, pl.ds(768 * t + 256 * j, 256)], home.at[j, :, pl.ds(256 * t, 256)], 3 + 3 * j + t)
                )
        first.append(load(wo_hbm, home.at[3], 12))
        first.append(load(wd_hbm, home.at[4:8], 13))
        for k in range(4):
            first.append(load(wu_hbm.at[:, pl.ds(768 * k, 768)], home.at[8 + k], 14 + k))
    else:
        first.append(load(w_hbm, w, 3))
    for copy in first + later:
        copy.start()
    if joined:
        for copy in first[1:]:
            copy.wait()
        barrier = pltpu.get_barrier_semaphore()
        for peer in place.peers():
            pl.semaphore_signal(barrier, inc=1, device_id=peer, device_id_type=MESH)
        pl.semaphore_wait(barrier, 6)
        gather = Gather(place, w, gsems)
        reduce = Reduce(place, w, own, rc, rdx, rdy, rxx, rxy, rz, rsems)
        gather.tick(0)
    else:
        first[1].wait()
    first[0].wait()
    if joined:
        par[...] = small_sum(place, par_in[...], stage_ref.at[0], land_ref.at[0], z_ref.at[0], ssems.at[0], False)
        gather.tick(1)
    else:
        par[...] = par_in[...]
    small[...] = jnp.zeros_like(small)
    first_norm(x, par, act1)
    fill_tables(table_ref, cosine, sine)
    if joined:
        gather.tick(2)
    fill_bias(start, bias, x.shape[0] // BL, False)
    for copy in later:
        copy.wait()
    branch_grad(mix4, g, gb)
    if joined:
        gather.tick(3)
        gather.tick(4)

    def forward_group(j, carry):
        project(j, act1, w, cosine, sine, qkv)

        def inner(i, carry):
            forward_pair(2 * j + i, start, qkv, bias, mixed, lse)
            if joined:
                gather.tick(5 + 2 * j + i)
            return carry

        return lax.fori_loop(0, 2, inner, carry)

    lax.fori_loop(0, 3, forward_group, 0)
    attention_out(x, mixed, w, par, middle, act2, actt, out, dact)
    if joined:
        gather.tick(11)

    def ff_group(z, carry):
        if joined:
            gather.tick(12 + z)
        feed_forward(z, act2, actt, gb, w, hid, gu, out, dact)
        if joined:
            reduce.tick(z)
        return carry

    lax.fori_loop(0, 4, ff_group, 0)
    if joined:
        reduce.tick(4)
    ga, do, nxt = gb, act2, earlier
    middle_back(mix4, g, earlier, middle, out, dact, mixed, w, par, nxt, ga, do, small)
    store_next = load(nxt, next_hbm, 0)
    store_next.start()
    if joined:
        reduce.tick(5)
    fill_bias(start, bias, x.shape[0] // BL, True)
    actt[...] = act1[...].T

    def backward_group(j, carry):
        def inner(i, carry):
            backward_pair(2 * j + i, start, qkv, do, mixed, lse, cosine, sine, bias, dq)

            @pl.when(i == 1)
            def _():
                project_back(j, actt, qkv, w, out)

            if joined:
                reduce.tick(6 + 2 * j + i)
            return carry

        return lax.fori_loop(0, 2, inner, carry)

    lax.fori_loop(0, 3, backward_group, 0)
    first_back(x, out, par, dact, small)
    store_dx = load(dact, dx_hbm, 1)
    store_dx.start()
    for k in range(4):
        small[4:5, 128 * k : 128 * k + 128] = fold_lanes(terms_ref[k : k + 1, :])
    small[4:5, 512:640] = fold_lanes(small[5:6, :])
    small[5:6, :] = jnp.zeros_like(small[5:6, :])
    if joined:
        reduce.tick(12)
        small_out[...] = small_sum(place, small[...], stage_ref.at[1], land_ref.at[1], z_ref.at[1], ssems.at[1], True)
        for t in range(13, LAST):
            reduce.tick(t)
        store_grad = load(own, own_hbm, 2)
    else:
        small_out[...] = small[...]
        store_grad = load(w, grad_hbm, 2)
    store_grad.start()
    store_next.wait()
    store_dx.wait()
    store_grad.wait()


def fold_lanes(row):
    total = row[:, 0:128]
    for i in range(1, row.shape[1] // 128):
        total = total + row[:, 128 * i : 128 * i + 128]
    return total


VMEM_LIMIT = 67043328
UNIT = (4, 2, 2, 48, 768)


def block_pass(joined, start, mix, x, g, earlier, par, terms, *weights):
    length, width = x.shape
    smem = pl.BlockSpec(memory_space=pltpu.SMEM)
    vmem = pl.BlockSpec(memory_space=pltpu.VMEM)
    anys = pl.BlockSpec(memory_space=pl.ANY)
    low = pltpu.VMEM((length, width), BF)
    full = pltpu.VMEM((length, width), F32)
    dma = pltpu.SemaphoreType.DMA
    small = (8, width)
    scratch = [low] * 5 + [pltpu.VMEM((width, length), BF)] + [low] * 4 + [pltpu.VMEM((length, 3 * width), BF)]
    scratch += [full] * 4
    scratch += [
        pltpu.VMEM((UNITS,) + UNIT, BF),
        pltpu.VMEM((length // BL + 1, BL, BL), F32),
        pltpu.VMEM((length, 128), F32),
        pltpu.VMEM((length, 128), F32),
        pltpu.VMEM((length, 128), F32),
        pltpu.VMEM(small, F32),
        pltpu.VMEM(small, F32),
        dma((18,)),
    ]
    grads = (UNITS,) + UNIT
    if joined:
        grads = (UNITS, 48, width)
        scratch += [
            pltpu.VMEM(grads, BF),
            pltpu.VMEM((2, 4, 2, 48, width), BF),
            pltpu.VMEM((2, 2, 48, width // 2), BF),
            pltpu.VMEM((2, 2, 48, width // 2), BF),
            pltpu.VMEM((2, 4, 48, width // 2), BF),
            pltpu.VMEM((2, 4, 48, width // 2), BF),
            pltpu.VMEM((2, 3, 48, width // 2), BF),
            pltpu.VMEM((2, 3) + small, F32),
            pltpu.VMEM((2, 3) + small, F32),
            pltpu.VMEM((2, 4) + small, F32),
            dma((2, 2, 8)),
            dma((2, 2, 9)),
            dma((2, 2, 1, 6)),
        ]
    params = dict(vmem_limit_bytes=VMEM_LIMIT)
    if joined:
        params.update(collective_id=0, has_side_effects=True)
    return pl.pallas_call(
        functools.partial(block_kernel, joined),
        in_specs=[smem, smem, anys, anys, anys, vmem, vmem, vmem] + [anys] * len(weights),
        out_specs=(anys, anys, anys, vmem),
        out_shape=(
            jax.ShapeDtypeStruct((length, width), BF),
            jax.ShapeDtypeStruct((length, width), F32),
            jax.ShapeDtypeStruct(grads, BF),
            jax.ShapeDtypeStruct(small, F32),
        ),
        scratch_shapes=scratch,
        compiler_params=pltpu.CompilerParams(**params),
        name="block_pass",
    )(start, mix, x, g, earlier, par, terms, rotary_table(length), *weights)


def to_units(wq, wo, wu, wd):
    d = wo.shape[0]
    parts = [
        wq.reshape(d, 3, 3, 256).transpose(2, 0, 1, 3).reshape(3, d, d),
        wo[None],
        wd.reshape(16, 4, 48, d).transpose(1, 0, 2, 3).reshape(4, d, d),
        wu.reshape(d, 4, d).transpose(1, 0, 2),
    ]
    return jnp.concatenate(parts).reshape((UNITS,) + UNIT)


def from_units(units, height):
    d = units.shape[-1]
    units = units.reshape(UNITS, -1, d)
    r = units.shape[1]
    gq = units[0:3].reshape(3, r, 3, 256).transpose(1, 2, 0, 3).reshape(r, 3 * d)
    gd = units[4:8].reshape(4, r // height, height, d).transpose(1, 0, 2, 3).reshape(4 * r, d)
    return gq, units[3], units[8:12].transpose(1, 0, 2).reshape(r, 4 * d), gd


def local(block_input, history, cotangent, span_start, w_qkv, w_out, w_up, w_down, ln_gains, ln_biases, mix_weights, joined):
    shard = lax.axis_index("shard")
    width = block_input.shape[1]
    own = ln_gains.shape[1]
    grad_history, earlier, terms = history_pass(mix_weights, history, cotangent)
    mine = jnp.concatenate([ln_gains, ln_biases]).astype(F32)
    if joined:
        par = lax.dynamic_update_slice(jnp.zeros((8, width), F32), mine, (0, shard * own))
        nxt, grad_input, units, small = block_pass(
            True, span_start, mix_weights, block_input, cotangent, earlier, par, terms,
            w_qkv, w_out, w_up, w_down.reshape(4, own, width),
        )
        gq, go, gu, gd = [item.astype(F32) for item in from_units(units, own)]
        norm_grads = lax.dynamic_slice(small, (0, shard * own), (4, own))
        grad_mix = jnp.sum(small[4, : 5 * 128].reshape(5, 128), axis=1)
    else:
        gather = lambda item, axis: lax.all_gather(item, "shard", axis=axis, tiled=True)
        par = jnp.concatenate([gather(mine.astype(BF), 1).astype(F32), jnp.zeros((4, width), F32)])
        weights = to_units(gather(w_qkv, 0), gather(w_out, 0), gather(w_up, 0), gather(w_down, 0))
        nxt, grad_input, units, small = block_pass(
            False, span_start, mix_weights, block_input, cotangent, earlier, par, terms, weights
        )

        def owned(item, axis):
            part = lax.psum_scatter(item.astype(BF), "shard", scatter_dimension=axis, tiled=True)
            return lax.psum(part, "rep").astype(F32)

        gq, go, gu, gd = [owned(item, 0) for item in from_units(units, 48)]
        norm_grads = owned(small[:4], 1)
        grad_mix = lax.psum(jnp.sum(small[4, : 5 * 128].reshape(5, 128), axis=1), ("rep", "shard"))
    return nxt, grad_input, grad_history, grad_mix, gq, go, gu, gd, norm_grads[0:2], norm_grads[2], norm_grads[3]


def solution(mesh):
    token = P(("rep", "shard"), None)
    kept = P("shard", None)
    past = P(None, ("rep", "shard"), None)
    norm = P(None, "shard")
    joined = mesh.shape["rep"] == 2 and mesh.shape["shard"] == 16
    return jax.shard_map(
        functools.partial(local, joined=joined),
        mesh=mesh,
        in_specs=(token, past, token, P(("rep", "shard")), kept, kept, kept, kept, norm, norm, P()),
        out_specs=(token, token, past, P(), kept, kept, kept, kept, norm, P("shard"), P("shard")),
        check_vma=False,
    )
```

```python
import functools
import jax
import jax.numpy as jnp
import numpy as np
from jax import lax
from jax.experimental import pallas as pl
from jax.experimental.pallas import tpu as pltpu
from jax.sharding import PartitionSpec as P

BF = jnp.bfloat16
F32 = jnp.float32
HEADS = 12
SPAN = 256
BL = 256
NEG = -1e30
EPS = 1e-05
FB = 256


def dot(a, b):
    return lax.dot_general(a, b, (((1,), (0,)), ((), ())), preferred_element_type=F32)


def dot_bt(a, b):
    return lax.dot_general(a, b, (((1,), (1,)), ((), ())), preferred_element_type=F32)


def dot_at(a, b):
    return lax.dot_general(a, b, (((0,), (0,)), ((), ())), preferred_element_type=F32)


def iota(shape, axis):
    return lax.broadcasted_iota(jnp.int32, shape, axis)


def cols(start, width=128):
    return pl.ds(pl.multiple_of(start, 128), width)


def rows(start, height):
    return pl.ds(pl.multiple_of(start, height), height)


def norm_parts(values):
    average = jnp.mean(values, axis=-1, keepdims=True)
    centered = values - average
    inverse_std = lax.rsqrt(jnp.mean(centered * centered, axis=-1, keepdims=True) + EPS)
    return centered * inverse_std, inverse_std


def norm_back(incoming, normed, inverse_std, gain_row):
    scaled = incoming * gain_row
    inner = (
        scaled
        - jnp.mean(scaled, axis=-1, keepdims=True)
        - normed * jnp.mean(scaled * normed, axis=-1, keepdims=True)
    )
    return inverse_std * inner


def fold8(values):
    return jnp.sum(values.reshape(values.shape[0] // 8, 8, values.shape[1]), axis=0)


def turn(values, low_quarter):
    return jnp.where(low_quarter, pltpu.roll(values, 96, 1), pltpu.roll(values, 32, 1))


def gelu_parts(upper):
    size = jnp.abs(upper)
    t = 1.0 / (1.0 + 0.2316419 * size)
    density = jnp.exp(-0.5 * upper * upper) * 0.3989422804014327
    poly = ((((1.330274429 * t - 1.821255978) * t + 1.781477937) * t - 0.356563782) * t + 0.319381530) * t
    tail = density * poly
    cdf = jnp.where(upper >= 0, 1.0 - tail, tail)
    return upper * cdf, cdf + upper * density


def split3(values):
    high = values.astype(BF)
    rest = values - high.astype(F32)
    mid = rest.astype(BF)
    return high, mid, (rest - mid.astype(F32)).astype(BF)


def block_bias(start, query0, key0, causal, transposed):
    query = query0 + iota((BL, BL), 1 if transposed else 0)
    key = key0 + iota((BL, BL), 0 if transposed else 1)
    inside = (query >= start) & (query < start + SPAN) & (key >= start) & (key < start + SPAN)
    seen = (inside | (key <= query)) if causal else inside
    return jnp.where(seen, 0.0, NEG).astype(F32)


def fill_bias(start, bias_ref, blocks, transposed):
    span_block = start // BL
    for i in range(blocks):
        bias_ref[i] = block_bias(start, i * BL, i * BL, True, transposed)
    extra = block_bias(start, span_block * BL, (span_block + 1) * BL, False, transposed)
    bias_ref[blocks] = jnp.where(span_block + 1 < blocks, extra, NEG)


def pick(span_block, blocks, load):
    value = load(0)
    for b in range(1, blocks - 1):
        value = lax.select(span_block == b, load(b), value)
    return value


def forward_pair(h, start, qkv_ref, bias_ref, out_ref, lse_ref, after):
    length, width = out_ref.shape
    blocks = length // BL
    span_block = start // BL
    first = iota((BL, 128), 1) < 64
    first_all = iota((length, 128), 1) < 64
    zero = jnp.zeros((), BF)
    one = jnp.ones((), BF)

    oc, qc, kc, vc = pair_columns(h)
    keys = qkv_ref[:, kc]
    values = qkv_ref[:, vc]
    with_ones = (jnp.where(first_all, values, one), jnp.where(first_all, one, values))
    qx = pick(span_block, blocks, lambda b: qkv_ref[pl.ds(b * BL, BL), qc])
    kx = pick(span_block, blocks, lambda b: qkv_ref[pl.ds((b + 1) * BL, BL), kc])
    vx = pick(span_block, blocks, lambda b: qkv_ref[pl.ds((b + 1) * BL, BL), vc])
    extra = []
    for head in (0, 1):
        mine = first if head == 0 else ~first
        s = dot_bt(jnp.where(mine, qx, zero), kx) + bias_ref[blocks]
        peak = jnp.max(s, axis=1, keepdims=True)
        extra.append((peak, dot(jnp.exp(s - peak).astype(BF), jnp.where(mine, vx, one))))
    for i in range(blocks):
        outs, peaks = [], []
        here = span_block == i
        qi = qkv_ref[pl.ds(i * BL, BL), qc]
        for head in (0, 1):
            mine = first if head == 0 else ~first
            qm = jnp.where(mine, qi, zero)
            extra_peak, extra_out = extra[head]
            diag = dot_bt(qm, keys[i * BL : (i + 1) * BL]) + bias_ref[i]
            peak = jnp.max(diag, axis=1, keepdims=True)
            if i > 0:
                left = dot_bt(qm, keys[: i * BL])
                peak = jnp.maximum(peak, jnp.max(left, axis=1, keepdims=True))
            if i < blocks - 1:
                peak = jnp.maximum(peak, jnp.where(here, extra_peak, NEG))
            out = dot(jnp.exp(diag - peak).astype(BF), with_ones[head][i * BL : (i + 1) * BL])
            if i > 0:
                out = out + dot(jnp.exp(left - peak).astype(BF), with_ones[head][: i * BL])
            if i < blocks - 1:
                out = out + jnp.where(here, jnp.exp(extra_peak - peak), 0.0) * extra_out
            outs.append(out)
            peaks.append(peak)
        top = jnp.where(first, outs[0], outs[1])
        total = pltpu.roll(jnp.where(first, outs[1], outs[0]), 64, 1)
        out_ref[pl.ds(i * BL, BL), oc] = (top / total).astype(BF)
        lse_ref[pl.ds(i * BL, BL), oc] = jnp.where(first, peaks[0], peaks[1]) + jnp.log(total)
        after(i)


def backward_pair(h, start, qkv_ref, do_ref, out_ref, lse_ref, cos_ref, sin_ref, bias_ref, dq_ref, after):
    length, width = out_ref.shape
    blocks = length // BL
    span_block = start // BL
    lane_all = iota((length, 128), 1)
    lane = iota((BL, 128), 1)
    first = lane < 64
    low_quarter = (lane % 64) < 32
    zero = jnp.zeros((), BF)
    one = jnp.ones((), BF)

    def extend(values, column, head, lanes):
        a, b, c = split3(-column)
        base = 64 * (1 - head)
        parts = jnp.where(
            lanes == base, a, jnp.where(lanes == base + 1, b, jnp.where(lanes == base + 2, c, zero))
        )
        return jnp.where(lanes < 64, values, parts) if head == 0 else jnp.where(lanes < 64, parts, values)

    def keep(values, head, lanes, other):
        return jnp.where(lanes < 64, values, other) if head == 0 else jnp.where(lanes < 64, other, values)

    def rotate_back(values, cosine, sine):
        return values * cosine - turn(values, low_quarter) * sine

    oc, qc, kc, vc = pair_columns(h)

    def query_side(load, lanes):
        q, do, lse, out = load(qkv_ref, qc), load(do_ref, oc), load(lse_ref, oc), load(out_ref, oc)
        product = do.astype(F32) * out.astype(F32)
        sides = []
        for head in (0, 1):
            mine = (lanes < 64) if head == 0 else (lanes >= 64)
            delta = jnp.sum(jnp.where(mine, product, 0.0), axis=1, keepdims=True)
            sides.append(
                (
                    extend(q, lse[:, 64 * head : 64 * head + 1], head, lanes),
                    keep(q, head, lanes, zero),
                    extend(do, delta, head, lanes),
                    keep(do, head, lanes, zero),
                )
            )
        return sides

    everything = query_side(lambda ref, at: ref[:, at], lane_all)
    extra_side = query_side(
        lambda ref, at: pick(span_block, blocks, lambda b: ref[pl.ds(b * BL, BL), at]), lane
    )
    kx = pick(span_block, blocks, lambda b: qkv_ref[pl.ds((b + 1) * BL, BL), kc])
    vx = pick(span_block, blocks, lambda b: qkv_ref[pl.ds((b + 1) * BL, BL), vc])

    def block(k, v, head, qa, qm, da, dm, bias):
        s = dot_bt(keep(k, head, lane, one), qa)
        if bias is not None:
            s = s + bias
        p = jnp.exp(s)
        ds = (p * dot_bt(keep(v, head, lane, one), da)).astype(BF)
        return dot(p.astype(BF), dm), dot(ds, qm), dot_at(ds, keep(k, head, lane, zero))

    parts = [block(kx, vx, head, *extra_side[head], bias_ref[blocks]) for head in (0, 1)]
    dvx, dkx, dqx = [a + b for a, b in zip(*parts)]
    for j in range(blocks):
        at = slice(j * BL, (j + 1) * BL)
        rest = slice((j + 1) * BL, length)
        kj = qkv_ref[at, kc]
        vj = qkv_ref[at, vc]
        dv = jnp.where(span_block + 1 == j, dvx, 0.0) if j > 0 else None
        dk = jnp.where(span_block + 1 == j, dkx, 0.0) if j > 0 else None
        dq = jnp.where(span_block == j, dqx, 0.0) if j < blocks - 1 else None
        dq_rest = None
        add = lambda old, new: new if old is None else old + new
        for head in (0, 1):
            side = everything[head]
            a, b, c = block(kj, vj, head, *[item[at] for item in side], bias_ref[j])
            dv, dk, dq = add(dv, a), add(dk, b), add(dq, c)
            if j < blocks - 1:
                a, b, c = block(kj, vj, head, *[item[rest] for item in side], None)
                dv, dk, dq_rest = add(dv, a), add(dk, b), add(dq_rest, c)
        cosine, sine = cos_ref[at], sin_ref[at]
        if j > 0:
            dq = dq + dq_ref[at]
        qkv_ref[at, vc] = dv.astype(BF)
        qkv_ref[at, kc] = rotate_back(dk, cosine, sine).astype(BF)
        qkv_ref[at, qc] = rotate_back(dq * 0.125, cosine, sine).astype(BF)
        if j < blocks - 1:
            dq_ref[rest] = dq_rest if j == 0 else dq_ref[rest] + dq_rest
        after(j)


MESH = pl.DeviceIdType.MESH
UNITS = 12
PIECE = 48
GAP = 4
GATHER_AT = (0, 2, 5, 7, 9)
REDUCE_AT = (0, 2, 5, 7, 10, 12)


class Place:
    def __init__(self):
        self.y = lax.axis_index("rep")
        s = lax.axis_index("shard")
        self.z, self.x, self.c = s // 4, (s // 2) % 2, s % 2

    def at(self, y, z, x, c):
        return (y, (z * 2 + x) * 2 + c)

    def twin(self):
        return self.at(self.y, self.z, self.x, 1 - self.c)

    def across_x(self):
        return self.at(self.y, self.z, 1 - self.x, self.c)

    def across_y(self):
        return self.at(1 - self.y, self.z, self.x, self.c)

    def along_z(self, k):
        return self.at(self.y, (self.z + k) % 4, self.x, self.c)

    def flat(self):
        return ((self.y * 4 + self.z) * 2 + self.x) * 2 + self.c

    def other(self, k):
        there = (self.flat() + k) % 32
        return there // 16, there % 16


def half(y):
    return pl.ds(pl.multiple_of(y * 384, 128), 384)


def remote(src, dst, sems, slot, kind, device):
    return pltpu.make_async_remote_copy(
        src_ref=src,
        dst_ref=dst,
        send_sem=sems.at[0, slot, kind],
        recv_sem=sems.at[1, slot, kind],
        device_id=device,
        device_id_type=MESH,
    )


class Gather:
    def __init__(self, place, w_ref, sems):
        self.p, self.w, self.sems = place, w_ref, sems

    def copies(self, stage, u, mine):
        p, w = self.p, self.w
        slot = u
        y, z, x, c = p.y, p.z, p.x, p.c

        def same(ref, kind, device):
            return remote(ref, ref, self.sems, slot, kind, device)

        if stage == 0:
            return [
                same(w.at[u, z if mine else (z + 4 - k) % 4, x, c, :, half(y)], k - 1, p.along_z(k)) for k in (1, 2, 3)
            ]
        if stage == 1:
            return [
                same(w.at[u, :, x if mine else 1 - x, c, :, half(y)], 3, p.across_x()),
                same(w.at[u, :, x, c, :, half(y if mine else 1 - y)], 4, p.across_y()),
            ]
        if stage == 2:
            return [
                same(w.at[u, 0:2, x if mine else 1 - x, c, :, half(1 - y)], 5, p.across_x()),
                same(w.at[u, 2:4, 1 - x, c, :, half(y if mine else 1 - y)], 6, p.across_y()),
            ]
        return [same(w.at[u, :, :, c if mine else 1 - c], 7, p.twin())]

    def step(self, stage, u):
        if stage > 0:
            for copy in self.copies(stage - 1, u, False):
                copy.wait_recv()
            for copy in self.copies(stage - 1, u, True):
                copy.wait_send()
        if stage < 4:
            for copy in self.copies(stage, u, True):
                copy.start()

    def half_tick(self, m, odd):
        for stage in (4, 3, 2, 1, 0):
            if GATHER_AT[stage] % 2 == odd:
                u = m - GATHER_AT[stage] // 2
                if isinstance(u, int):
                    if 0 <= u < UNITS:
                        self.step(stage, u)
                else:
                    pl.when((u >= 0) & (u < UNITS))(functools.partial(self.step, stage, u))


class Reduce:
    def __init__(self, place, w_ref, own_ref, rc, rdx, rdy, rxx, rxy, rz, sems):
        self.p, self.w, self.own, self.sems = place, w_ref, own_ref, sems
        self.rc, self.rdx, self.rdy, self.rxx, self.rxy, self.rz = rc, rdx, rdy, rxx, rxy, rz

    def copies(self, stage, n, mine):
        p, w = self.p, self.w
        u = held_in(n)
        slot = n % GAP
        y, z, x, c = p.y, p.z, p.x, p.c

        def send(src, dst, kind, device):
            return remote(src, dst, self.sems, slot, kind, device)

        if stage == 0:
            return [send(w.at[u, :, :, 1 - c], self.rc.at[n % 2], 0, p.twin())]
        if stage == 1:
            return [
                send(w.at[u, 0:2, 1 - x, c, :, half(1 - y)], self.rdx.at[slot], 1, p.across_x()),
                send(w.at[u, 2:4, 1 - x, c, :, half(1 - y)], self.rdy.at[slot], 2, p.across_y()),
            ]
        if stage == 2:
            return [
                send(w.at[u, :, 1 - x, c, :, half(y)], self.rxx.at[slot], 3, p.across_x()),
                send(w.at[u, :, x, c, :, half(1 - y)], self.rxy.at[slot], 4, p.across_y()),
            ]
        if stage == 3:
            return [
                send(w.at[u, (z + k) % 4, x, c, :, half(y)], self.rz.at[slot, k - 1], 4 + k, p.along_z(k))
                for k in (1, 2, 3)
            ]
        there = self.own.at[unit_of(n), :, half(y if mine else 1 - y)]
        return [send(there, there, 8, p.across_y())]

    def add(self, stage, n):
        p, w = self.p, self.w
        u = held_in(n)
        slot = n % GAP
        y, z, x, c = p.y, p.z, p.x, p.c
        f = lambda value: value.astype(F32)
        if stage == 1:

            def piece(zz, carry):
                w[u, zz, :, c] = (f(w[u, zz, :, c]) + f(self.rc[n % 2, zz])).astype(BF)
                return carry

            lax.fori_loop(0, 4, piece, 0)
        if stage == 2:
            w[u, 0:2, x, c, :, half(1 - y)] = (f(w[u, 0:2, x, c, :, half(1 - y)]) + f(self.rdx[slot])).astype(BF)
            w[u, 2:4, 1 - x, c, :, half(y)] = (f(w[u, 2:4, 1 - x, c, :, half(y)]) + f(self.rdy[slot])).astype(BF)
        if stage == 3:
            w[u, :, x, c, :, half(y)] = (
                f(w[u, :, x, c, :, half(y)]) + f(self.rxx[slot]) + f(self.rxy[slot])
            ).astype(BF)
        if stage == 4:
            total = f(w[u, z, x, c, :, half(y)])
            for k in (0, 1, 2):
                total = total + f(self.rz[slot, k])
            self.own[unit_of(n), :, half(y)] = total.astype(BF)

    def step(self, stage, n):
        if stage > 0:
            for copy in self.copies(stage - 1, n, False):
                copy.wait_recv()
            for copy in self.copies(stage - 1, n, True):
                copy.wait_send()
            self.add(stage, n)
        if stage < 5:
            for copy in self.copies(stage, n, True):
                copy.start()

    def half_tick(self, m, odd):
        for stage in (5, 4, 3, 2, 1, 0):
            if REDUCE_AT[stage] % 2 == odd:
                place = m - REDUCE_AT[stage] // 2
                if isinstance(place, int):
                    if place in PLACES:
                        self.step(stage, PLACES.index(place))
                else:
                    late = (place >= 11) & (place < 20) & ((place - 11) % 4 == 0)
                    n = jnp.where(place < 9, place, 9 + (place - 11) // 4)
                    pl.when(((place >= 0) & (place < 9)) | late)(functools.partial(self.step, stage, n))


PLACES = (0, 1, 2, 3, 4, 5, 6, 7, 8, 11, 15, 19)


def unit_of(n):
    if isinstance(n, int):
        return 4 + n if n < 8 else 3 if n == 8 else n - 9
    return jnp.where(n < 8, 4 + n, jnp.where(n == 8, 3, n - 9))


def held_in(n):
    if isinstance(n, int):
        return 4 + n if n < 8 else 3 if n == 8 else n - 5
    return jnp.where(n < 8, 4 + n, jnp.where(n == 8, 3, n - 5))


def assemble(tile, pieces, load):
    total = None
    for dst, key, src, length in pieces:
        at = max(dst, 128 * tile)
        while at < min(dst + length, 128 * tile + 128):
            lane = src + at - dst
            count = min(dst + length, 128 * tile + 128, at + 128 - lane % 128) - at
            value = load(key, lane // 128)
            shift = (at - lane) % 128
            value = value if shift == 0 else pltpu.roll(value, shift, 1)
            lanes = iota(value.shape, 1)
            low = at - 128 * tile
            inside = (lanes >= low) & (lanes < low + count)
            total = jnp.where(inside, value, 0.0 if total is None else total)
            at += count
    return total


def split_up(raw_ref, home_ref):
    load = lambda key, t: raw_ref[:, 128 * t : 128 * t + 128].astype(F32)
    for q in range(4):
        pieces = [(PIECE * s, 0, 4 * PIECE * s + PIECE * q, PIECE) for s in range(16)]
        for t in range(6):
            home_ref[5 + 2 * q, :, 128 * t : 128 * t + 128] = assemble(t, pieces, load).astype(BF)


def merge_up(own_ref, raw_ref):
    load = lambda q, t: own_ref[5 + 2 * q, :, 128 * t : 128 * t + 128].astype(F32)
    pieces = [(4 * PIECE * s + PIECE * q, q, PIECE * s, PIECE) for s in range(16) for q in range(4)]
    for t in range(24):
        here = [p for p in pieces if p[0] < 128 * t + 128 and p[0] + PIECE > 128 * t]
        raw_ref[:, 128 * t : 128 * t + 128] = assemble(t, here, load).astype(BF)


class Exchange:
    def __init__(self, place, sent_ref, land_ref, sems, everywhere):
        self.p, self.sent, self.land, self.sems, self.everywhere = place, sent_ref, land_ref, sems, everywhere

    def copy(self, k, mine):
        p = self.p
        if self.everywhere:
            count = 32
            y, s = p.other(k)
            src, me = self.sent.at[s], p.flat()
        else:
            count = 16
            me = p.flat() % 16
            y, s = p.y, (me + k) % 16
            src = self.sent
        return pltpu.make_async_remote_copy(
            src_ref=src,
            dst_ref=self.land.at[me if mine else (me + count - k) % count],
            send_sem=self.sems.at[0, k],
            recv_sem=self.sems.at[1, k],
            device_id=(y, s),
            device_id_type=MESH,
        )

    def start(self):
        def send(k, carry):
            self.copy(k, True).start()
            return carry

        lax.fori_loop(1, self.land.shape[0], send, 0)

    def finish(self):
        def wait(k, carry):
            self.copy(k, False).wait_recv()
            self.copy(k, True).wait_send()
            return carry

        lax.fori_loop(1, self.land.shape[0], wait, 0)


def own_part(value, s):
    load = lambda key, t: value[:, 128 * t : 128 * t + 128]
    return assemble(0, [(0, 0, PIECE * s, PIECE)], load)


def history_kernel(mix_ref, history_ref, g_ref, grad_ref, earlier_ref, terms_ref):
    g = g_ref[...].astype(F32)
    earlier = None
    parts = []
    for k in range(history_ref.shape[0]):
        h = history_ref[k].astype(F32)
        grad_ref[k] = mix_ref[k] * g
        term = mix_ref[k] * h
        earlier = term if earlier is None else earlier + term
        parts.append(jnp.sum(fold8(h * g), axis=0, keepdims=True))
    earlier_ref[...] = earlier.astype(BF)
    new = jnp.concatenate(parts + [jnp.zeros((8 - len(parts), g.shape[1]), F32)], axis=0)

    @pl.when(pl.program_id(0) == 0)
    def _():
        terms_ref[...] = new

    @pl.when(pl.program_id(0) > 0)
    def _():
        terms_ref[...] += new


def history_pass(mix, history, g):
    past, length, width = history.shape
    height = 128
    return pl.pallas_call(
        history_kernel,
        grid=(length // height,),
        in_specs=[
            pl.BlockSpec(memory_space=pltpu.SMEM),
            pl.BlockSpec((past, height, width), lambda i: (0, i, 0)),
            pl.BlockSpec((height, width), lambda i: (i, 0)),
        ],
        out_specs=(
            pl.BlockSpec((past, height, width), lambda i: (0, i, 0)),
            pl.BlockSpec((height, width), lambda i: (i, 0)),
            pl.BlockSpec((8, width), lambda i: (0, 0)),
        ),
        out_shape=(
            jax.ShapeDtypeStruct((past, length, width), F32),
            jax.ShapeDtypeStruct((length, width), BF),
            jax.ShapeDtypeStruct((8, width), F32),
        ),
        name="history_pass",
    )(mix, history, g)


def first_norm(x_ref, par_ref, act_ref):
    height = 128

    def chunk(r, carry):
        at = rows(r * height, height)
        normed, _ = norm_parts(x_ref[at, :].astype(F32))
        act_ref[at, :] = (normed * par_ref[0:1, :] + par_ref[2:3, :]).astype(BF)
        return carry

    lax.fori_loop(0, x_ref.shape[0] // height, chunk, 0)


def pair_columns(h):
    base = (h // 2) * 768 + (h % 2) * 128
    return cols(h * 128), cols(base), cols(base + 256), cols(base + 512)


def unit(w_ref, u):
    return w_ref[u].reshape(768, 768)


def project(j, act_ref, w_ref, cos_ref, sin_ref, qkv_ref):
    height = 256
    low_quarter = (iota((height, 128), 1) % 64) < 32

    def chunk(r, carry):
        at = rows(r * height, height)
        out = dot(act_ref[at, :], unit(w_ref, j))
        cosine, sine = cos_ref[at, :], sin_ref[at, :]
        for piece in range(6):
            u = out[:, piece * 128 : piece * 128 + 128]
            if piece < 4:
                u = u * cosine + turn(u, low_quarter) * sine
            if piece < 2:
                u = u * 0.125
            qkv_ref[at, cols(j * 768 + piece * 128)] = u.astype(BF)
        return carry

    lax.fori_loop(0, act_ref.shape[0] // height, chunk, 0)


def attention_out(x_ref, mixed_ref, w_ref, par_ref, middle_ref, act_ref, actt_ref, out_ref, dact_ref):
    height = 256

    def chunk(r, carry):
        at = rows(r * height, height)
        middle = x_ref[at, :].astype(F32) + dot(mixed_ref[at, :], unit(w_ref, 3))
        middle_ref[at, :] = middle
        out_ref[at, :] = middle
        dact_ref[at, :] = jnp.zeros_like(middle)
        normed, _ = norm_parts(middle)
        act = (normed * par_ref[1:2, :] + par_ref[3:4, :]).astype(BF)
        act_ref[at, :] = act
        actt_ref[:, rows(r * height, height)] = act.T
        return carry

    lax.fori_loop(0, x_ref.shape[0] // height, chunk, 0)


def feed_forward(z, act_ref, actt_ref, gb_ref, w_ref, hid_ref, gu_ref, out_ref, dact_ref, after):
    height = 256

    def chunk(r, carry):
        at = rows(r * height, height)
        down, up = unit(w_ref, 4 + 2 * z), unit(w_ref, 5 + 2 * z)
        hidden, slope = gelu_parts(dot(act_ref[at, :], up))
        hidden = hidden.astype(BF)
        hid_ref[at, :] = hidden
        gu = (dot_bt(gb_ref[at, :], down) * slope).astype(BF)
        gu_ref[at, :] = gu
        out_ref[at, :] += dot(hidden, down)
        dact_ref[at, :] += dot_bt(gu, up)
        after(r)
        return carry

    lax.fori_loop(0, act_ref.shape[0] // height, chunk, 0)
    w_ref[4 + 2 * z] = dot_at(hid_ref[...], gb_ref[...]).astype(BF).reshape(w_ref.shape[1:])
    w_ref[5 + 2 * z] = dot(actt_ref[...], gu_ref[...]).astype(BF).reshape(w_ref.shape[1:])


def branch_grad(mix4, g_ref, gb_ref):
    height = 256

    def chunk(r, carry):
        at = rows(r * height, height)
        gb_ref[at, :] = (mix4 * g_ref[at, :].astype(F32)).astype(BF)
        return carry

    lax.fori_loop(0, g_ref.shape[0] // height, chunk, 0)


def middle_back(mix4, g_ref, earlier_ref, middle_ref, out_ref, dact_ref, mixed_ref, w_ref, par_ref,
                next_ref, ga_ref, do_ref, small_ref):
    height = 256
    width = g_ref.shape[1]
    zero = jnp.zeros((8, width), F32)

    def chunk(r, carry):
        gain, bias, terms = carry
        at = rows(r * height, height)
        g = g_ref[at, :].astype(F32)
        output = out_ref[at, :]
        next_ref[at, :] = (earlier_ref[at, :].astype(F32) + mix4 * output).astype(BF)
        terms = terms + fold8(g * output)
        normed, inverse = norm_parts(middle_ref[at, :])
        dact = dact_ref[at, :]
        gain = gain + fold8(dact * normed)
        bias = bias + fold8(dact)
        grad = mix4 * g + norm_back(dact, normed, inverse, par_ref[1:2, :])
        dact_ref[at, :] = grad
        low = grad.astype(BF)
        ga_ref[at, :] = low
        do_ref[at, :] = dot_bt(low, unit(w_ref, 3)).astype(BF)
        return gain, bias, terms

    gain, bias, terms = lax.fori_loop(0, g_ref.shape[0] // height, chunk, (zero, zero, zero))
    small_ref[1:2, :] = jnp.sum(gain, axis=0, keepdims=True)
    small_ref[3:4, :] = jnp.sum(bias, axis=0, keepdims=True)
    small_ref[5:6, :] = jnp.sum(terms, axis=0, keepdims=True)
    w_ref[3] = dot_at(mixed_ref[...], ga_ref[...]).astype(BF).reshape(w_ref.shape[1:])


def project_back(j, actt_ref, qkv_ref, w_ref, out_ref, grad_ref):
    height = 256
    grad_ref[...] = dot(actt_ref[...], qkv_ref[:, cols(j * 768, 768)]).astype(BF).reshape(grad_ref.shape)

    def chunk(r, carry):
        at = rows(r * height, height)
        share = dot_bt(qkv_ref[at, cols(j * 768, 768)], unit(w_ref, j))
        out_ref[at, :] = jnp.where(j == 0, 0.0, out_ref[at, :]) + share
        return carry

    @pl.when(j < 2)
    def _():
        lax.fori_loop(0, qkv_ref.shape[0] // height, chunk, 0)


def first_back(x_ref, qkv_ref, w_ref, dact_ref, par_ref, dmid_ref, small_ref, after):
    height = 256
    zero = jnp.zeros((8, x_ref.shape[1]), F32)

    def chunk(r, carry):
        gain, bias = carry
        at = rows(r * height, height)
        dact = dact_ref[at, :] + dot_bt(qkv_ref[at, cols(2 * 768, 768)], unit(w_ref, 2))
        normed, inverse = norm_parts(x_ref[at, :].astype(F32))
        gain = gain + fold8(dact * normed)
        bias = bias + fold8(dact)
        dmid_ref[at, :] += norm_back(dact, normed, inverse, par_ref[0:1, :])
        after(r, at)
        return gain, bias

    gain, bias = lax.fori_loop(0, x_ref.shape[0] // height, chunk, (zero, zero))
    small_ref[0:1, :] = jnp.sum(gain, axis=0, keepdims=True)
    small_ref[2:3, :] = jnp.sum(bias, axis=0, keepdims=True)


def fill_tables(table_ref, cos_ref, sin_ref):
    blocks = cos_ref.shape[0] // 32
    cb, sb, sign = table_ref[0], table_ref[1], table_ref[2]

    def block(a, carry):
        ca, sa = table_ref[3, pl.ds(a, 1), :], table_ref[4, pl.ds(a, 1), :]
        at = rows(a * 32, 32)
        cos_ref[at, :] = ca * cb - sa * sb
        sin_ref[at, :] = (sa * cb + ca * sb) * sign
        return carry

    lax.fori_loop(0, blocks, block, 0)


def rotary_table(length):
    freq = np.tile(np.exp(-np.log(10000.0) * np.arange(32) / 32.0), 4)[None, :]
    fine = np.arange(32)[:, None] * freq
    coarse = 32 * np.arange(32)[:, None] * freq
    sign = np.tile(np.repeat([-1.0, 1.0], 32), 2)[None, :] * np.ones((32, 1))
    return jnp.asarray(np.stack([np.cos(fine), np.sin(fine), sign, np.cos(coarse), np.sin(coarse)]), F32)


def block_kernel(joined, *refs):
    if joined:
        start_ref, mix_ref, x_hbm, g_hbm, earlier_hbm, gains_ref, biases_ref, terms_ref, table_ref = refs[:9]
        wq_hbm, wo_hbm, wu_hbm, wd_hbm = refs[9:13]
        next_hbm, dx_hbm, gq_hbm, go_hbm, gu_hbm, gd_hbm, small_out = refs[13:20]
        refs = refs[20:]
    else:
        start_ref, mix_ref, x_hbm, g_hbm, earlier_hbm, par_in, terms_ref, table_ref, w_hbm = refs[:9]
        next_hbm, dx_hbm, grad_hbm, small_out = refs[9:13]
        refs = refs[13:]
    x, g, gb, act1, act2, actt, mixed, earlier, hid, gu, qkv, lse, middle, out, dact = refs[:15]
    w, bias, dq, cosine, sine, small, par, loads = refs[15:23]
    start = start_ref[0]
    mix4 = mix_ref[4]
    length = x.shape[0]

    load = lambda src, dst, i: pltpu.make_async_copy(src, dst, loads.at[i])
    first = [load(x_hbm, x, 0)]
    later = [load(g_hbm, g, 1), load(earlier_hbm, earlier, 2)]
    if joined:
        own, rc, rdx, rdy, rxx, rxy, rz, raw, msg_p, land_p, msg_g, land_g, gsems, rsems, psems, ssems = refs[23:]
        place = Place()
        home = w.at[:, place.z, place.x, place.c]
        for j in range(3):
            for t in range(3):
                first.append(
                    load(wq_hbm.at[:, pl.ds(768 * t + 256 * j, 256)], home.at[j, :, pl.ds(256 * t, 256)], 3 + 3 * j + t)
                )
        first.append(load(wo_hbm, home.at[3], 12))
        for k in range(4):
            first.append(load(wd_hbm.at[k], home.at[4 + 2 * k], 13 + k))
        first.append(load(wu_hbm, raw, 17))
    else:
        spare = refs[23]
        first.append(load(w_hbm, w, 3))
    for copy in first + later:
        copy.start()
    if joined:
        for copy in first[1:]:
            copy.wait()
        barrier = pltpu.get_barrier_semaphore()

        def greet(k, carry):
            pl.semaphore_signal(barrier, inc=1, device_id=place.other(k), device_id_type=MESH)
            return carry

        lax.fori_loop(1, 32, greet, 0)
        pl.semaphore_wait(barrier, 31)
        gather = Gather(place, w, gsems).half_tick
        reduce = Reduce(place, w, own, rc, rdx, rdy, rxx, rxy, rz, rsems).half_tick
        params = Exchange(place, msg_p, land_p, psems, False)
        sums = Exchange(place, msg_g, land_g, ssems, True)
        gather(0, 0)
        msg_p[...] = jnp.zeros_like(msg_p)
        msg_p[0:2, 0:PIECE] = gains_ref[...].astype(F32)
        msg_p[2:4, 0:PIECE] = biases_ref[...].astype(F32)
        params.start()
        land_p[place.flat() % 16] = msg_p[...]
        fill_tables(table_ref, cosine, sine)
        gather(1, 0)
        split_up(raw, home)
    else:
        gather = reduce = lambda m, odd: None
        first[1].wait()
        par[...] = par_in[...]
        fill_tables(table_ref, cosine, sine)
    small[...] = jnp.zeros_like(small)
    fill_bias(start, bias, length // BL, False)
    gather(2, 0)
    gather(2, 1)
    for copy in [first[0]] + later:
        copy.wait()
    branch_grad(mix4, g, gb)
    if joined:
        params.finish()
        pieces = [(PIECE * s, s, 0, PIECE) for s in range(16)]
        for t in range(6):
            here = [p for p in pieces if p[0] < 128 * t + 128 and p[0] + PIECE > 128 * t]
            par[:, 128 * t : 128 * t + 128] = assemble(t, here, lambda s, _: land_p[s])
    gather(3, 0)
    gather(3, 1)
    first_norm(x, par, act1)
    gather(4, 0)
    gather(4, 1)

    def forward_group(j, carry):
        project(j, act1, w, cosine, sine, qkv)

        def inner(i, carry):
            m = 5 + 2 * j + i
            forward_pair(
                2 * j + i, start, qkv, bias, mixed, lse, lambda b: gather(m, b // 2) if b % 2 else None
            )
            return carry

        return lax.fori_loop(0, 2, inner, carry)

    lax.fori_loop(0, 3, forward_group, 0)
    attention_out(x, mixed, w, par, middle, act2, actt, out, dact)

    def ff_group(z, carry):
        def after(r):
            for odd in (0, 1):

                @pl.when(r % 2 == odd)
                def _():
                    gather(11 + 2 * z + r // 2, odd)
                    reduce(2 * z - 2 + r // 2, odd)

        feed_forward(z, act2, actt, gb, w, hid, gu, out, dact, after if joined else lambda r: None)
        return carry

    lax.fori_loop(0, 4, ff_group, 0)
    reduce(6, 0)
    ga, do, nxt = gb, act2, earlier
    middle_back(mix4, g, earlier, middle, out, dact, mixed, w, par, nxt, ga, do, small)
    store_next = load(nxt, next_hbm, 0)
    store_next.start()
    reduce(6, 1)
    fill_bias(start, bias, length // BL, True)
    actt[...] = act1[...].T

    def backward_group(j, carry):
        def inner(i, carry):
            m = 7 + 2 * (2 * j + i)
            backward_pair(
                2 * j + i, start, qkv, do, mixed, lse, cosine, sine, bias, dq, lambda b: reduce(m + b // 2, b % 2)
            )

            @pl.when(i == 1)
            def _():
                project_back(j, actt, qkv, w, out, w.at[4 + j] if joined else spare.at[j])

            return carry

        return lax.fori_loop(0, 2, inner, carry)

    lax.fori_loop(0, 3, backward_group, 0)
    reduce(19, 0)

    def store_dx(r, at):
        reduce(19 + r, 1)
        reduce(20 + r, 0)

    first_back(x, qkv, w, out, par, dact, small, store_dx)
    stores = [load(dact, dx_hbm, 1)]
    stores[0].start()
    totals = jnp.sum(terms_ref[...], axis=1, keepdims=True)
    lane = iota((1, 128), 1)
    mix_row = jnp.where(lane == 4, jnp.sum(small[5:6, :], axis=1, keepdims=True), 0.0)
    for k in range(4):
        mix_row = jnp.where(lane == k, totals[k : k + 1, :], mix_row)
    if joined:
        values = small[...]
        for s in range(16):
            msg_g[s] = own_part(values, s)
            msg_g[s, 4:5, :] = mix_row
        sums.start()
        land_g[place.flat()] = msg_g[place.flat() % 16]
        merge_up(own, raw)
        stores += [load(own.at[3], go_hbm, 2), load(raw, gu_hbm, 3)]
        stores += [load(own.at[4 + 2 * k], gd_hbm.at[k], 4 + k) for k in range(4)]
        for copy in stores[1:]:
            copy.start()
        reduce(23, 1)
        reduce(24, 0)
        sums.finish()

        def add(k, total):
            return total + land_g[k]

        small_out[...] = lax.fori_loop(0, 32, add, jnp.zeros(small_out.shape, F32))
        reduce(24, 1)
        reduce(25, 0)
        units = [
            load(own.at[j, :, pl.ds(256 * t, 256)], gq_hbm.at[:, pl.ds(768 * t + 256 * j, 256)], 8 + 3 * j + t)
            for j in range(3)
            for t in range(3)
        ]
        for copy in units:
            copy.start()
        stores += units
    else:
        small[4:5, 0:128] = mix_row
        small[4:5, 128:] = jnp.zeros_like(small[4:5, 128:])
        small_out[...] = small[...]
        stores += [load(spare, grad_hbm.at[0:3], 2), load(w.at[3:], grad_hbm.at[3:], 3)]
        for copy in stores[1:]:
            copy.start()
    store_next.wait()
    for copy in stores:
        copy.wait()


VMEM_LIMIT = 67043328
UNIT = (4, 2, 2, PIECE, 768)


def block_pass(joined, start, mix, x, g, earlier, par, terms, *weights):
    length, width = x.shape
    smem = pl.BlockSpec(memory_space=pltpu.SMEM)
    vmem = pl.BlockSpec(memory_space=pltpu.VMEM)
    anys = pl.BlockSpec(memory_space=pl.ANY)
    low = pltpu.VMEM((length, width), BF)
    full = pltpu.VMEM((length, width), F32)
    dma = pltpu.SemaphoreType.DMA
    small = (8, width)
    scratch = [low] * 5 + [pltpu.VMEM((width, length), BF)] + [low] * 4 + [pltpu.VMEM((length, 3 * width), BF)]
    scratch += [full] * 4
    scratch += [
        pltpu.VMEM((UNITS,) + UNIT, BF),
        pltpu.VMEM((length // BL + 1, BL, BL), F32),
        pltpu.VMEM((length, 128), F32),
        pltpu.VMEM((length, 128), F32),
        pltpu.VMEM((length, 128), F32),
        pltpu.VMEM(small, F32),
        pltpu.VMEM(small, F32),
        dma((18,)),
    ]
    grads = [((UNITS,) + UNIT, BF), (small, F32)]
    if joined:
        grads = [
            ((PIECE, 3 * width), BF), ((PIECE, width), BF), ((PIECE, 4 * width), BF), ((4, PIECE, width), BF), ((8, 128), F32)
        ]
        scratch += [
            pltpu.VMEM((UNITS, PIECE, width), BF),
            pltpu.VMEM((2, 4, 2, PIECE, width), BF),
            pltpu.VMEM((GAP, 2, PIECE, width // 2), BF),
            pltpu.VMEM((GAP, 2, PIECE, width // 2), BF),
            pltpu.VMEM((GAP, 4, PIECE, width // 2), BF),
            pltpu.VMEM((GAP, 4, PIECE, width // 2), BF),
            pltpu.VMEM((GAP, 3, PIECE, width // 2), BF),
            pltpu.VMEM((PIECE, 4 * width), BF),
            pltpu.VMEM((8, 128), F32),
            pltpu.VMEM((16, 8, 128), F32),
            pltpu.VMEM((16, 8, 128), F32),
            pltpu.VMEM((32, 8, 128), F32),
            dma((2, UNITS, 8)),
            dma((2, GAP, 9)),
            dma((2, 16)),
            dma((2, 32)),
        ]
    else:
        scratch += [pltpu.VMEM((3,) + UNIT, BF)]
    params = dict(vmem_limit_bytes=VMEM_LIMIT)
    if joined:
        params.update(collective_id=0, has_side_effects=True)
    outs = [((length, width), BF), ((length, width), F32)] + grads
    return pl.pallas_call(
        functools.partial(block_kernel, joined),
        in_specs=[smem, smem, anys, anys, anys] + [vmem] * (len(par) + 2) + [anys] * len(weights),
        out_specs=[anys] * (len(outs) - 1) + [vmem],
        out_shape=[jax.ShapeDtypeStruct(shape, dtype) for shape, dtype in outs],
        scratch_shapes=scratch,
        compiler_params=pltpu.CompilerParams(**params),
        name="block_pass",
    )(start, mix, x, g, earlier, *par, terms, rotary_table(length), *weights)


def to_units(wq, wo, wu, wd):
    d = wo.shape[0]
    down = wd.reshape(16, 4, PIECE, d).transpose(1, 0, 2, 3).reshape(4, d, d)
    up = wu.reshape(d, 16, 4, PIECE).transpose(2, 0, 1, 3).reshape(4, d, d)
    parts = [
        wq.reshape(d, 3, 3, 256).transpose(2, 0, 1, 3).reshape(3, d, d),
        wo[None],
        jnp.stack([down, up], axis=1).reshape(8, d, d),
    ]
    return jnp.concatenate(parts).reshape((UNITS,) + UNIT)


def from_units(units):
    d = units.shape[-1]
    units = units.reshape(UNITS, d, d)
    gq = units[0:3].reshape(3, d, 3, 256).transpose(1, 2, 0, 3).reshape(d, 3 * d)
    both = units[4:].reshape(4, 2, d, d)
    gd = both[:, 0].reshape(4, 16, PIECE, d).transpose(1, 0, 2, 3).reshape(4 * d, d)
    gu = both[:, 1].reshape(4, d, 16, PIECE).transpose(1, 2, 0, 3).reshape(d, 4 * d)
    return gq, units[3], gu, gd


def local(block_input, history, cotangent, span_start, w_qkv, w_out, w_up, w_down, ln_gains, ln_biases, mix_weights, joined):
    width = block_input.shape[1]
    own = ln_gains.shape[1]
    grad_history, earlier, terms = history_pass(mix_weights, history, cotangent)
    if joined:
        nxt, grad_input, gq, go, gu, gd, small = block_pass(
            True, span_start, mix_weights, block_input, cotangent, earlier, [ln_gains, ln_biases], terms,
            w_qkv, w_out, w_up, w_down.reshape(4, own, width),
        )
        gq, go, gu, gd = [item.astype(F32) for item in (gq, go, gu, gd.reshape(4 * own, width))]
        norm_grads = small[:4, :own]
        grad_mix = small[4, :5]
    else:
        gather = lambda item, axis: lax.all_gather(item, "shard", axis=axis, tiled=True)
        mine = jnp.concatenate([ln_gains, ln_biases])
        par = jnp.concatenate([gather(mine, 1).astype(F32), jnp.zeros((4, width), F32)])
        weights = to_units(gather(w_qkv, 0), gather(w_out, 0), gather(w_up, 0), gather(w_down, 0))
        nxt, grad_input, units, small = block_pass(
            False, span_start, mix_weights, block_input, cotangent, earlier, [par], terms, weights
        )

        def owned(item, axis):
            part = lax.psum_scatter(item.astype(BF), "shard", scatter_dimension=axis, tiled=True)
            return lax.psum(part, "rep").astype(F32)

        gq, go, gu, gd = [owned(item, 0) for item in from_units(units)]
        norm_grads = owned(small[:4], 1)
        grad_mix = lax.psum(small[4, :5], ("rep", "shard"))
    return nxt, grad_input, grad_history, grad_mix, gq, go, gu, gd, norm_grads[0:2], norm_grads[2], norm_grads[3]


def solution(mesh):
    token = P(("rep", "shard"), None)
    kept = P("shard", None)
    past = P(None, ("rep", "shard"), None)
    norm = P(None, "shard")
    joined = mesh.shape["rep"] == 2 and mesh.shape["shard"] == 16
    return jax.shard_map(
        functools.partial(local, joined=joined),
        mesh=mesh,
        in_specs=(token, past, token, P(("rep", "shard")), kept, kept, kept, kept, norm, norm, P()),
        out_specs=(token, token, past, P(), kept, kept, kept, kept, norm, P("shard"), P("shard")),
        check_vma=False,
    )
```

```python
import functools
import jax
import jax.numpy as jnp
import numpy as np
from jax import lax
from jax.experimental import pallas as pl
from jax.experimental.pallas import tpu as pltpu
from jax.sharding import PartitionSpec as P

BF = jnp.bfloat16
F32 = jnp.float32
HEADS = 12
SPAN = 256
BL = 256
NEG = -1e30
EPS = 1e-05
FB = 256


def dot(a, b):
    return lax.dot_general(a, b, (((1,), (0,)), ((), ())), preferred_element_type=F32)


def dot_bt(a, b):
    return lax.dot_general(a, b, (((1,), (1,)), ((), ())), preferred_element_type=F32)


def dot_at(a, b):
    return lax.dot_general(a, b, (((0,), (0,)), ((), ())), preferred_element_type=F32)


def iota(shape, axis):
    return lax.broadcasted_iota(jnp.int32, shape, axis)


def cols(start, width=128):
    return pl.ds(pl.multiple_of(start, 128), width)


def rows(start, height):
    return pl.ds(pl.multiple_of(start, height), height)


def norm_parts(values):
    average = jnp.mean(values, axis=-1, keepdims=True)
    centered = values - average
    inverse_std = lax.rsqrt(jnp.mean(centered * centered, axis=-1, keepdims=True) + EPS)
    return centered * inverse_std, inverse_std


def norm_back(incoming, normed, inverse_std, gain_row):
    scaled = incoming * gain_row
    inner = (
        scaled
        - jnp.mean(scaled, axis=-1, keepdims=True)
        - normed * jnp.mean(scaled * normed, axis=-1, keepdims=True)
    )
    return inverse_std * inner


def fold8(values):
    return jnp.sum(values.reshape(values.shape[0] // 8, 8, values.shape[1]), axis=0)


def turn(values, low_quarter):
    return jnp.where(low_quarter, pltpu.roll(values, 96, 1), pltpu.roll(values, 32, 1))


def gelu_parts(upper):
    size = jnp.abs(upper)
    t = 1.0 / (1.0 + 0.2316419 * size)
    density = jnp.exp(-0.5 * upper * upper) * 0.3989422804014327
    poly = ((((1.330274429 * t - 1.821255978) * t + 1.781477937) * t - 0.356563782) * t + 0.319381530) * t
    tail = density * poly
    cdf = jnp.where(upper >= 0, 1.0 - tail, tail)
    return upper * cdf, cdf + upper * density


def split3(values):
    high = values.astype(BF)
    rest = values - high.astype(F32)
    mid = rest.astype(BF)
    return high, mid, (rest - mid.astype(F32)).astype(BF)


def block_bias(start, query0, key0, causal, transposed):
    query = query0 + iota((BL, BL), 1 if transposed else 0)
    key = key0 + iota((BL, BL), 0 if transposed else 1)
    inside = (query >= start) & (query < start + SPAN) & (key >= start) & (key < start + SPAN)
    seen = (inside | (key <= query)) if causal else inside
    return jnp.where(seen, 0.0, NEG).astype(F32)


def fill_bias(start, bias_ref, blocks, transposed):
    span_block = start // BL
    for i in range(blocks):
        bias_ref[i] = block_bias(start, i * BL, i * BL, True, transposed)
    extra = block_bias(start, span_block * BL, (span_block + 1) * BL, False, transposed)
    bias_ref[blocks] = jnp.where(span_block + 1 < blocks, extra, NEG)


def pick(span_block, blocks, load):
    value = load(0)
    for b in range(1, blocks - 1):
        value = lax.select(span_block == b, load(b), value)
    return value


def forward_pair(h, start, qkv_ref, bias_ref, out_ref, lse_ref, after):
    length, width = out_ref.shape
    blocks = length // BL
    span_block = start // BL
    first = iota((BL, 128), 1) < 64
    first_all = iota((length, 128), 1) < 64
    zero = jnp.zeros((), BF)
    one = jnp.ones((), BF)

    oc, qc, kc, vc = pair_columns(h)
    keys = qkv_ref[:, kc]
    values = qkv_ref[:, vc]
    with_ones = (jnp.where(first_all, values, one), jnp.where(first_all, one, values))
    qx = pick(span_block, blocks, lambda b: qkv_ref[pl.ds(b * BL, BL), qc])
    kx = pick(span_block, blocks, lambda b: qkv_ref[pl.ds((b + 1) * BL, BL), kc])
    vx = pick(span_block, blocks, lambda b: qkv_ref[pl.ds((b + 1) * BL, BL), vc])
    extra = []
    for head in (0, 1):
        mine = first if head == 0 else ~first
        s = dot_bt(jnp.where(mine, qx, zero), kx) + bias_ref[blocks]
        peak = jnp.max(s, axis=1, keepdims=True)
        extra.append((peak, dot(jnp.exp(s - peak).astype(BF), jnp.where(mine, vx, one))))
    for i in range(blocks):
        outs, peaks = [], []
        here = span_block == i
        qi = qkv_ref[pl.ds(i * BL, BL), qc]
        for head in (0, 1):
            mine = first if head == 0 else ~first
            qm = jnp.where(mine, qi, zero)
            extra_peak, extra_out = extra[head]
            diag = dot_bt(qm, keys[i * BL : (i + 1) * BL]) + bias_ref[i]
            peak = jnp.max(diag, axis=1, keepdims=True)
            if i > 0:
                left = dot_bt(qm, keys[: i * BL])
                peak = jnp.maximum(peak, jnp.max(left, axis=1, keepdims=True))
            if i < blocks - 1:
                peak = jnp.maximum(peak, jnp.where(here, extra_peak, NEG))
            out = dot(jnp.exp(diag - peak).astype(BF), with_ones[head][i * BL : (i + 1) * BL])
            if i > 0:
                out = out + dot(jnp.exp(left - peak).astype(BF), with_ones[head][: i * BL])
            if i < blocks - 1:
                out = out + jnp.where(here, jnp.exp(extra_peak - peak), 0.0) * extra_out
            outs.append(out)
            peaks.append(peak)
        top = jnp.where(first, outs[0], outs[1])
        total = pltpu.roll(jnp.where(first, outs[1], outs[0]), 64, 1)
        out_ref[pl.ds(i * BL, BL), oc] = (top / total).astype(BF)
        lse_ref[pl.ds(i * BL, BL), oc] = jnp.where(first, peaks[0], peaks[1]) + jnp.log(total)
        after(i)


def backward_pair(h, start, qkv_ref, do_ref, out_ref, lse_ref, cos_ref, sin_ref, bias_ref, dq_ref, after):
    length, width = out_ref.shape
    blocks = length // BL
    span_block = start // BL
    lane_all = iota((length, 128), 1)
    lane = iota((BL, 128), 1)
    first = lane < 64
    low_quarter = (lane % 64) < 32
    zero = jnp.zeros((), BF)
    one = jnp.ones((), BF)

    def extend(values, column, head, lanes):
        a, b, c = split3(-column)
        base = 64 * (1 - head)
        parts = jnp.where(
            lanes == base, a, jnp.where(lanes == base + 1, b, jnp.where(lanes == base + 2, c, zero))
        )
        return jnp.where(lanes < 64, values, parts) if head == 0 else jnp.where(lanes < 64, parts, values)

    def keep(values, head, lanes, other):
        return jnp.where(lanes < 64, values, other) if head == 0 else jnp.where(lanes < 64, other, values)

    def rotate_back(values, cosine, sine):
        return values * cosine - turn(values, low_quarter) * sine

    oc, qc, kc, vc = pair_columns(h)

    def query_side(load, lanes):
        q, do, lse, out = load(qkv_ref, qc), load(do_ref, oc), load(lse_ref, oc), load(out_ref, oc)
        product = do.astype(F32) * out.astype(F32)
        sides = []
        for head in (0, 1):
            mine = (lanes < 64) if head == 0 else (lanes >= 64)
            delta = jnp.sum(jnp.where(mine, product, 0.0), axis=1, keepdims=True)
            sides.append(
                (
                    extend(q, lse[:, 64 * head : 64 * head + 1], head, lanes),
                    keep(q, head, lanes, zero),
                    extend(do, delta, head, lanes),
                    keep(do, head, lanes, zero),
                )
            )
        return sides

    everything = query_side(lambda ref, at: ref[:, at], lane_all)
    extra_side = query_side(
        lambda ref, at: pick(span_block, blocks, lambda b: ref[pl.ds(b * BL, BL), at]), lane
    )
    kx = pick(span_block, blocks, lambda b: qkv_ref[pl.ds((b + 1) * BL, BL), kc])
    vx = pick(span_block, blocks, lambda b: qkv_ref[pl.ds((b + 1) * BL, BL), vc])

    def block(k, v, head, qa, qm, da, dm, bias):
        s = dot_bt(keep(k, head, lane, one), qa)
        if bias is not None:
            s = s + bias
        p = jnp.exp(s)
        ds = (p * dot_bt(keep(v, head, lane, one), da)).astype(BF)
        return dot(p.astype(BF), dm), dot(ds, qm), dot_at(ds, keep(k, head, lane, zero))

    parts = [block(kx, vx, head, *extra_side[head], bias_ref[blocks]) for head in (0, 1)]
    dvx, dkx, dqx = [a + b for a, b in zip(*parts)]
    for j in range(blocks):
        at = slice(j * BL, (j + 1) * BL)
        rest = slice((j + 1) * BL, length)
        kj = qkv_ref[at, kc]
        vj = qkv_ref[at, vc]
        dv = jnp.where(span_block + 1 == j, dvx, 0.0) if j > 0 else None
        dk = jnp.where(span_block + 1 == j, dkx, 0.0) if j > 0 else None
        dq = jnp.where(span_block == j, dqx, 0.0) if j < blocks - 1 else None
        dq_rest = None
        add = lambda old, new: new if old is None else old + new
        for head in (0, 1):
            side = everything[head]
            a, b, c = block(kj, vj, head, *[item[at] for item in side], bias_ref[j])
            dv, dk, dq = add(dv, a), add(dk, b), add(dq, c)
            if j < blocks - 1:
                a, b, c = block(kj, vj, head, *[item[rest] for item in side], None)
                dv, dk, dq_rest = add(dv, a), add(dk, b), add(dq_rest, c)
        cosine, sine = cos_ref[at], sin_ref[at]
        if j > 0:
            dq = dq + dq_ref[at]
        qkv_ref[at, vc] = dv.astype(BF)
        qkv_ref[at, kc] = rotate_back(dk, cosine, sine).astype(BF)
        qkv_ref[at, qc] = rotate_back(dq * 0.125, cosine, sine).astype(BF)
        if j < blocks - 1:
            dq_ref[rest] = dq_rest if j == 0 else dq_ref[rest] + dq_rest
        after(j)


MESH = pl.DeviceIdType.MESH
UNITS = 12
PIECE = 48
GAP = 4
GATHER_AT = (-1, 7, 12, 16, 19)
GATHER_FROM = (4, 2, 2, 2, 2)
REDUCE_AT = (0, 2, 6, 11, 15, 18)
LATE_BEAT, LAST_BEAT = 11, 15


def at_tick(stages, beat, phase):
    return [(stage, beat - at // 4) for stage, at in reversed(list(enumerate(stages))) if at % 4 == phase]


class Place:
    def __init__(self):
        self.y = lax.axis_index("rep")
        s = lax.axis_index("shard")
        self.z, self.x, self.c = s // 4, (s // 2) % 2, s % 2

    def at(self, y, z, x, c):
        return (y, (z * 2 + x) * 2 + c)

    def twin(self):
        return self.at(self.y, self.z, self.x, 1 - self.c)

    def across_x(self):
        return self.at(self.y, self.z, 1 - self.x, self.c)

    def across_y(self):
        return self.at(1 - self.y, self.z, self.x, self.c)

    def along_z(self, k):
        return self.at(self.y, (self.z + k) % 4, self.x, self.c)

    def flat(self):
        return ((self.y * 4 + self.z) * 2 + self.x) * 2 + self.c

    def other(self, k):
        there = (self.flat() + k) % 32
        return there // 16, there % 16


def half(y):
    return pl.ds(pl.multiple_of(y * 384, 128), 384)


def remote(src, dst, sems, slot, kind, device):
    return pltpu.make_async_remote_copy(
        src_ref=src,
        dst_ref=dst,
        send_sem=sems.at[0, slot, kind],
        recv_sem=sems.at[1, slot, kind],
        device_id=device,
        device_id_type=MESH,
    )


class Gather:
    def __init__(self, place, w_ref, sems):
        self.p, self.w, self.sems = place, w_ref, sems

    def copies(self, stage, u, mine):
        p, w = self.p, self.w
        slot = u
        y, z, x, c = p.y, p.z, p.x, p.c

        def same(ref, kind, device):
            return remote(ref, ref, self.sems, slot, kind, device)

        if stage == 0:
            return [
                same(w.at[u, z if mine else (z + 4 - k) % 4, x, c, :, half(y)], k - 1, p.along_z(k)) for k in (1, 2, 3)
            ]
        if stage == 1:
            return [
                same(w.at[u, :, x if mine else 1 - x, c, :, half(y)], 3, p.across_x()),
                same(w.at[u, :, x, c, :, half(y if mine else 1 - y)], 4, p.across_y()),
            ]
        if stage == 2:
            return [
                same(w.at[u, 0:2, x if mine else 1 - x, c, :, half(1 - y)], 5, p.across_x()),
                same(w.at[u, 2:4, 1 - x, c, :, half(y if mine else 1 - y)], 6, p.across_y()),
            ]
        return [same(w.at[u, :, :, c if mine else 1 - c], 7, p.twin())]

    def step(self, stage, u):
        if stage > 0:
            for copy in self.copies(stage - 1, u, False):
                copy.wait_recv()
            for copy in self.copies(stage - 1, u, True):
                copy.wait_send()
        if stage < 4:
            for copy in self.copies(stage, u, True):
                copy.start()

    def tick(self, beat, phase):
        for stage, u in at_tick(GATHER_AT, beat, phase):
            pl.when((u >= GATHER_FROM[stage]) & (u < UNITS))(functools.partial(self.step, stage, u))


class Reduce:
    def __init__(self, place, w_ref, own_ref, rc, rdx, rdy, rxx, rxy, rz, sems):
        self.p, self.w, self.own, self.sems = place, w_ref, own_ref, sems
        self.rc, self.rdx, self.rdy, self.rxx, self.rxy, self.rz = rc, rdx, rdy, rxx, rxy, rz

    def copies(self, stage, n, mine):
        p, w = self.p, self.w
        u = held_in(n)
        slot = n % GAP
        y, z, x, c = p.y, p.z, p.x, p.c

        def send(src, dst, kind, device):
            return remote(src, dst, self.sems, slot, kind, device)

        if stage == 0:
            return [send(w.at[u, :, :, 1 - c], self.rc.at[n % 2], 0, p.twin())]
        if stage == 1:
            return [
                send(w.at[u, 0:2, 1 - x, c, :, half(1 - y)], self.rdx.at[slot], 1, p.across_x()),
                send(w.at[u, 2:4, 1 - x, c, :, half(1 - y)], self.rdy.at[slot], 2, p.across_y()),
            ]
        if stage == 2:
            return [
                send(w.at[u, :, 1 - x, c, :, half(y)], self.rxx.at[slot], 3, p.across_x()),
                send(w.at[u, :, x, c, :, half(1 - y)], self.rxy.at[slot], 4, p.across_y()),
            ]
        if stage == 3:
            return [
                send(w.at[u, (z + k) % 4, x, c, :, half(y)], self.rz.at[slot, k - 1], 4 + k, p.along_z(k))
                for k in (1, 2, 3)
            ]
        there = self.own.at[unit_of(n), :, half(y if mine else 1 - y)]
        return [send(there, there, 8, p.across_y())]

    def add(self, stage, n):
        p, w = self.p, self.w
        u = held_in(n)
        slot = n % GAP
        y, z, x, c = p.y, p.z, p.x, p.c
        f = lambda value: value.astype(F32)
        if stage == 1:

            def piece(zz, carry):
                w[u, zz, :, c] = w[u, zz, :, c] + self.rc[n % 2, zz]
                return carry

            lax.fori_loop(0, 4, piece, 0)
        if stage == 2:
            w[u, 0:2, x, c, :, half(1 - y)] = w[u, 0:2, x, c, :, half(1 - y)] + self.rdx[slot]
            w[u, 2:4, 1 - x, c, :, half(y)] = w[u, 2:4, 1 - x, c, :, half(y)] + self.rdy[slot]
        if stage == 3:
            w[u, :, x, c, :, half(y)] = (
                f(w[u, :, x, c, :, half(y)]) + f(self.rxx[slot]) + f(self.rxy[slot])
            ).astype(BF)
        if stage == 4:
            total = f(w[u, z, x, c, :, half(y)])
            for k in (0, 1, 2):
                total = total + f(self.rz[slot, k])
            self.own[unit_of(n), :, half(y)] = total.astype(BF)

    def step(self, stage, n):
        if stage > 0:
            for copy in self.copies(stage - 1, n, False):
                copy.wait_recv()
            for copy in self.copies(stage - 1, n, True):
                copy.wait_send()
            self.add(stage, n)
        if stage < 5:
            for copy in self.copies(stage, n, True):
                copy.start()

    def tick(self, beat, phase):
        for stage, place in at_tick(REDUCE_AT, beat, phase):
            if isinstance(place, int):
                if place == LAST_BEAT:
                    self.step(stage, UNITS - 1)
            else:
                last = place == LAST_BEAT
                late = place == LATE_BEAT
                n = jnp.where(last, UNITS - 1, jnp.where(late, UNITS - 2, place))
                here = ((place >= 0) & (place < UNITS - 2)) | late | last
                pl.when(here)(functools.partial(self.step, stage, n))


def unit_of(n):
    if isinstance(n, int):
        return 4 + n if n < 8 else 3 if n == 8 else n - 9
    return jnp.where(n < 8, 4 + n, jnp.where(n == 8, 3, n - 9))


def held_in(n):
    if isinstance(n, int):
        return 4 + n if n < 8 else 3 if n == 8 else n - 5
    return jnp.where(n < 8, 4 + n, jnp.where(n == 8, 3, n - 5))


def assemble(tile, pieces, load):
    total = None
    for dst, key, src, length in pieces:
        at = max(dst, 128 * tile)
        while at < min(dst + length, 128 * tile + 128):
            lane = src + at - dst
            count = min(dst + length, 128 * tile + 128, at + 128 - lane % 128) - at
            value = load(key, lane // 128)
            shift = (at - lane) % 128
            value = value if shift == 0 else pltpu.roll(value, shift, 1)
            lanes = iota(value.shape, 1)
            low = at - 128 * tile
            inside = (lanes >= low) & (lanes < low + count)
            total = jnp.where(inside, value, 0.0 if total is None else total)
            at += count
    return total


def split_up(raw_ref, home_ref):
    load = lambda key, t: raw_ref[:, 128 * t : 128 * t + 128].astype(F32)
    for q in range(4):
        pieces = [(PIECE * s, 0, 4 * PIECE * s + PIECE * q, PIECE) for s in range(16)]
        for t in range(6):
            home_ref[5 + 2 * q, :, 128 * t : 128 * t + 128] = assemble(t, pieces, load).astype(BF)


def merge_up(own_ref, out_ref):
    load = lambda q, t: own_ref[5 + 2 * q, :, 128 * t : 128 * t + 128].astype(F32)
    pieces = [(4 * PIECE * s + PIECE * q, q, PIECE * s, PIECE) for s in range(16) for q in range(4)]
    for t in range(24):
        here = [p for p in pieces if p[0] < 128 * t + 128 and p[0] + PIECE > 128 * t]
        at = PIECE * (t // 6)
        out_ref[at : at + PIECE, 128 * (t % 6) : 128 * (t % 6) + 128] = assemble(t, here, load)


class Exchange:
    def __init__(self, place, sent_ref, land_ref, sems, everywhere):
        self.p, self.sent, self.land, self.sems, self.everywhere = place, sent_ref, land_ref, sems, everywhere

    def copy(self, k, mine):
        p = self.p
        if self.everywhere:
            count = 32
            y, s = p.other(k)
            src, me = self.sent.at[s], p.flat()
        else:
            count = 16
            me = p.flat() % 16
            y, s = p.y, (me + k) % 16
            src = self.sent
        return pltpu.make_async_remote_copy(
            src_ref=src,
            dst_ref=self.land.at[me if mine else (me + count - k) % count],
            send_sem=self.sems.at[0, k],
            recv_sem=self.sems.at[1, k],
            device_id=(y, s),
            device_id_type=MESH,
        )

    def start(self):
        def send(k, carry):
            self.copy(k, True).start()
            return carry

        lax.fori_loop(1, self.land.shape[0], send, 0)

    def finish(self):
        def wait(k, carry):
            self.copy(k, False).wait_recv()
            self.copy(k, True).wait_send()
            return carry

        lax.fori_loop(1, self.land.shape[0], wait, 0)


def own_part(value, s):
    load = lambda key, t: value[:, 128 * t : 128 * t + 128]
    return assemble(0, [(0, 0, PIECE * s, PIECE)], load)


def history_kernel(mix_ref, g_ref, grad_ref):
    g = g_ref[...].astype(F32)
    for k in range(grad_ref.shape[0]):
        grad_ref[k] = mix_ref[k] * g


def history_grad(mix, g, past):
    length, width = g.shape
    height = 128
    return pl.pallas_call(
        history_kernel,
        grid=(length // height,),
        in_specs=[pl.BlockSpec(memory_space=pltpu.SMEM), pl.BlockSpec((height, width), lambda i: (i, 0))],
        out_specs=pl.BlockSpec((past, height, width), lambda i: (0, i, 0)),
        out_shape=jax.ShapeDtypeStruct((past, length, width), F32),
        name="history_grad",
    )(mix, g)


def average(mix_ref, history, g_ref, out_ref, next_ref, small_ref, after):
    height = 256
    past = len(history)
    zero = jnp.zeros((8, g_ref.shape[1]), F32)

    def chunk(r, terms):
        at = rows(r * height, height)
        g = g_ref[at, :].astype(F32)
        output = out_ref[at, :]
        total = mix_ref[past] * output
        new = []
        for k in range(past):
            h = history[k][at, :].astype(F32)
            total = total + mix_ref[k] * h
            new.append(terms[k] + fold8(g * h))
        next_ref[at, :] = total.astype(BF)
        after(r)
        return tuple(new) + (terms[past] + fold8(g * output),)

    terms = lax.fori_loop(0, g_ref.shape[0] // height, chunk, (zero,) * (past + 1))
    for k in range(past + 1):
        small_ref[k : k + 1, :] = jnp.sum(terms[k], axis=0, keepdims=True)


def first_norm(x_ref, par_ref, act_ref):
    height = 128

    def chunk(r, carry):
        at = rows(r * height, height)
        normed, _ = norm_parts(x_ref[at, :].astype(F32))
        act_ref[at, :] = (normed * par_ref[0:1, :] + par_ref[2:3, :]).astype(BF)
        return carry

    lax.fori_loop(0, x_ref.shape[0] // height, chunk, 0)


def pair_columns(h):
    base = (h // 2) * 768 + (h % 2) * 128
    return cols(h * 128), cols(base), cols(base + 256), cols(base + 512)


def unit(w_ref, u):
    return w_ref[u].reshape(768, 768)


def project(j, act_ref, w_ref, cos_ref, sin_ref, qkv_ref):
    height = 256
    low_quarter = (iota((height, 128), 1) % 64) < 32

    def chunk(r, carry):
        at = rows(r * height, height)
        out = dot(act_ref[at, :], unit(w_ref, j))
        cosine, sine = cos_ref[at, :], sin_ref[at, :]
        for piece in range(6):
            u = out[:, piece * 128 : piece * 128 + 128]
            if piece < 4:
                u = u * cosine + turn(u, low_quarter) * sine
            if piece < 2:
                u = u * 0.125
            qkv_ref[at, cols(j * 768 + piece * 128)] = u.astype(BF)
        return carry

    lax.fori_loop(0, act_ref.shape[0] // height, chunk, 0)


def attention_out(x_ref, mixed_ref, w_ref, par_ref, middle_ref, act_ref, actt_ref, out_ref, dact_ref, after):
    height = 256

    def chunk(r, carry):
        at = rows(r * height, height)
        middle = x_ref[at, :].astype(F32) + dot(mixed_ref[at, :], unit(w_ref, 3))
        middle_ref[at, :] = middle
        out_ref[at, :] = middle
        dact_ref[at, :] = jnp.zeros_like(middle)
        normed, _ = norm_parts(middle)
        act = (normed * par_ref[1:2, :] + par_ref[3:4, :]).astype(BF)
        act_ref[at, :] = act
        actt_ref[:, rows(r * height, height)] = act.T
        after(r)
        return carry

    lax.fori_loop(0, x_ref.shape[0] // height, chunk, 0)


def feed_forward(z, act_ref, actt_ref, gb_ref, w_ref, hid_ref, gu_ref, out_ref, dact_ref, after):
    height = 256

    def chunk(r, carry):
        at = rows(r * height, height)
        down, up = unit(w_ref, 4 + 2 * z), unit(w_ref, 5 + 2 * z)
        hidden, slope = gelu_parts(dot(act_ref[at, :], up))
        hidden = hidden.astype(BF)
        hid_ref[at, :] = hidden
        gu = (dot_bt(gb_ref[at, :], down) * slope).astype(BF)
        gu_ref[at, :] = gu
        out_ref[at, :] += dot(hidden, down)
        dact_ref[at, :] += dot_bt(gu, up)
        after(r)
        return carry

    lax.fori_loop(0, act_ref.shape[0] // height, chunk, 0)
    w_ref[4 + 2 * z] = dot_at(hid_ref[...], gb_ref[...]).astype(BF).reshape(w_ref.shape[1:])
    w_ref[5 + 2 * z] = dot(actt_ref[...], gu_ref[...]).astype(BF).reshape(w_ref.shape[1:])


def branch_grad(mix4, g_ref, gb_ref):
    height = 256

    def chunk(r, carry):
        at = rows(r * height, height)
        gb_ref[at, :] = (mix4 * g_ref[at, :].astype(F32)).astype(BF)
        return carry

    lax.fori_loop(0, g_ref.shape[0] // height, chunk, 0)


def middle_back(mix4, g_ref, middle_ref, dact_ref, mixed_ref, w_ref, par_ref, ga_ref, do_ref, small_ref, after):
    height = 256
    zero = jnp.zeros((8, g_ref.shape[1]), F32)

    def chunk(r, carry):
        gain, bias = carry
        at = rows(r * height, height)
        normed, inverse = norm_parts(middle_ref[at, :])
        dact = dact_ref[at, :]
        gain = gain + fold8(dact * normed)
        bias = bias + fold8(dact)
        grad = mix4 * g_ref[at, :].astype(F32) + norm_back(dact, normed, inverse, par_ref[1:2, :])
        dact_ref[at, :] = grad
        low = grad.astype(BF)
        ga_ref[at, :] = low
        do_ref[at, :] = dot_bt(low, unit(w_ref, 3)).astype(BF)
        after(r)
        return gain, bias

    gain, bias = lax.fori_loop(0, g_ref.shape[0] // height, chunk, (zero, zero))
    small_ref[1:2, :] = jnp.sum(gain, axis=0, keepdims=True)
    small_ref[3:4, :] = jnp.sum(bias, axis=0, keepdims=True)
    w_ref[3] = dot_at(mixed_ref[...], ga_ref[...]).astype(BF).reshape(w_ref.shape[1:])


def first_back(x_ref, qkv_ref, w_ref, par_ref, dmid_ref, small_ref, after):
    height = 256
    zero = jnp.zeros((8, x_ref.shape[1]), F32)

    def chunk(r, carry):
        gain, bias = carry
        at = rows(r * height, height)
        dact = None
        for j in range(3):
            share = dot_bt(qkv_ref[at, cols(j * 768, 768)], unit(w_ref, j))
            dact = share if dact is None else dact + share
        normed, inverse = norm_parts(x_ref[at, :].astype(F32))
        gain = gain + fold8(dact * normed)
        bias = bias + fold8(dact)
        dmid_ref[at, :] += norm_back(dact, normed, inverse, par_ref[0:1, :])
        after(r)
        return gain, bias

    gain, bias = lax.fori_loop(0, x_ref.shape[0] // height, chunk, (zero, zero))
    small_ref[0:1, :] = jnp.sum(gain, axis=0, keepdims=True)
    small_ref[2:3, :] = jnp.sum(bias, axis=0, keepdims=True)


def fill_tables(table_ref, cos_ref, sin_ref):
    blocks = cos_ref.shape[0] // 32
    cb, sb, sign = table_ref[0], table_ref[1], table_ref[2]

    def block(a, carry):
        ca, sa = table_ref[3, pl.ds(a, 1), :], table_ref[4, pl.ds(a, 1), :]
        at = rows(a * 32, 32)
        cos_ref[at, :] = ca * cb - sa * sb
        sin_ref[at, :] = (sa * cb + ca * sb) * sign
        return carry

    lax.fori_loop(0, blocks, block, 0)


def rotary_table(length):
    freq = np.tile(np.exp(-np.log(10000.0) * np.arange(32) / 32.0), 4)[None, :]
    fine = np.arange(32)[:, None] * freq
    coarse = 32 * np.arange(32)[:, None] * freq
    sign = np.tile(np.repeat([-1.0, 1.0], 32), 2)[None, :] * np.ones((32, 1))
    return jnp.asarray(np.stack([np.cos(fine), np.sin(fine), sign, np.cos(coarse), np.sin(coarse)]), F32)


def block_kernel(joined, *refs):
    if joined:
        start_ref, mix_ref, x_hbm, g_hbm, history_hbm, gains_ref, biases_ref, table_ref = refs[:8]
        wq_hbm, wo_hbm, wu_hbm, wd_hbm = refs[8:12]
        next_hbm, dx_hbm, gq_hbm, go_hbm, gu_hbm, gd_hbm, mix_out, gains_out, first_out, second_out = refs[12:22]
        refs = refs[22:]
    else:
        start_ref, mix_ref, x_hbm, g_hbm, history_hbm, par_in, table_ref, w_hbm = refs[:8]
        next_hbm, dx_hbm, grad_hbm, small_out = refs[8:12]
        refs = refs[12:]
    x, g, gb, act1, act2, actt, mixed, nxt, hid, gu, qkv, lse, middle, out, dact = refs[:15]
    w, bias, dq, cosine, sine, small, par, terms, loads = refs[15:24]
    start = start_ref[0]
    mix4 = mix_ref[4]
    length = x.shape[0]

    load = lambda src, dst, i: pltpu.make_async_copy(src, dst, loads.at[i])
    first = [load(x_hbm, x, 0)]
    later = [load(g_hbm, g, 1)]
    if joined:
        own, rc, rdx, rdy, rxx, rxy, rz, raw, msg_p, land_p, msg_g, land_g, gsems, rsems, psems, ssems = refs[24:]
        place = Place()
        home = w.at[:, place.z, place.x, place.c]
        for j in range(3):
            for t in range(3):
                first.append(
                    load(wq_hbm.at[:, pl.ds(768 * t + 256 * j, 256)], home.at[j, :, pl.ds(256 * t, 256)], 3 + 3 * j + t)
                )
        first.append(load(wo_hbm, home.at[3], 12))
        for k in range(4):
            first.append(load(wd_hbm.at[k], home.at[4 + 2 * k], 13 + k))
        first.append(load(wu_hbm, raw, 17))
    else:
        spare = refs[24]
        first.append(load(w_hbm, w, 3))
    for copy in first + later:
        copy.start()
    if joined:
        for copy in first[1:]:
            copy.wait()
        barrier = pltpu.get_barrier_semaphore()

        def greet(k, carry):
            pl.semaphore_signal(barrier, inc=1, device_id=place.other(k), device_id_type=MESH)
            return carry

        lax.fori_loop(1, 32, greet, 0)
        pl.semaphore_wait(barrier, 31)
        units = Gather(place, w, gsems)
        gather = units.tick
        reduce = Reduce(place, w, own, rc, rdx, rdy, rxx, rxy, rz, rsems).tick
        params = Exchange(place, msg_p, land_p, psems, False)
        sums = Exchange(place, msg_g, land_g, ssems, True)
        units.step(0, 0)
        msg_p[...] = jnp.zeros_like(msg_p)
        msg_p[0:2, 0:PIECE] = gains_ref[...].astype(F32)
        msg_p[2:4, 0:PIECE] = biases_ref[...].astype(F32)
        params.start()
        land_p[place.flat() % 16] = msg_p[...]
        fill_tables(table_ref, cosine, sine)
        split_up(raw, home)
        units.step(1, 0)
        for u in (1, 2, 3):
            units.step(0, u)
    else:
        gather = reduce = lambda beat, phase: None
        first[1].wait()
        par[...] = par_in[...]
        fill_tables(table_ref, cosine, sine)
    small[...] = jnp.zeros_like(small)
    fill_bias(start, bias, length // BL, False)
    for copy in [first[0]] + later:
        copy.wait()
    branch_grad(mix4, g, gb)
    if joined:
        params.finish()
        pieces = [(PIECE * s, s, 0, PIECE) for s in range(16)]
        for t in range(6):
            here = [p for p in pieces if p[0] < 128 * t + 128 and p[0] + PIECE > 128 * t]
            par[:, 128 * t : 128 * t + 128] = assemble(t, here, lambda s, _: land_p[s])
        units.step(2, 0)
    first_norm(x, par, act1)
    if joined:
        units.step(3, 0)
        units.step(1, 1)
        units.step(4, 0)

    def forward_group(j, carry):
        project(j, act1, w, cosine, sine, qkv)

        def inner(i, carry):
            p = 2 * j + i

            def after(b):
                for stage, pair, at in ((2, 0, 3), (3, 1, 2), (4, 1, 3)):
                    if joined and b == at:
                        pl.when(p == pair)(functools.partial(units.step, stage, 1))
                gather(3 + p, b)

            forward_pair(p, start, qkv, bias, mixed, lse, after)
            return carry

        return lax.fori_loop(0, 2, inner, carry)

    lax.fori_loop(0, 3, forward_group, 0)

    def after_rows(r):
        for phase in (0, 3):
            pl.when(r == phase)(lambda: gather(r - phase + 9, phase))

    attention_out(x, mixed, w, par, middle, act2, actt, out, dact, after_rows)

    def ff_group(z, carry):
        def after(r):
            @pl.when(r % 2 == 0)
            def _():
                gather(10 + 2 * z + r // 2, 0)
                reduce(2 * z - 4 + r // 2, 0)

            @pl.when(r % 2 == 1)
            def _():
                gather(10 + 2 * z + r // 2, 3)
                reduce(2 * z - 4 + r // 2, 2)
                reduce(2 * z - 4 + r // 2, 3)

        feed_forward(z, act2, actt, gb, w, hid, gu, out, dact, after)
        return carry

    lax.fori_loop(0, 4, ff_group, 0)

    def after_middle(r):
        for phase in (0, 2, 3):
            pl.when(r == phase)(lambda: reduce(r - phase + 4, phase))

    ga, do = gb, act2
    middle_back(mix4, g, middle, dact, mixed, w, par, ga, do, small, after_middle)
    fill_bias(start, bias, length // BL, True)
    actt[...] = act1[...].T
    history = [hid, gu, gb, act1]
    past = [load(history_hbm.at[k], history[k], 12 + k) for k in range(4)]
    for copy in past:
        copy.start()

    def backward_group(j, carry):
        def inner(i, carry):
            p = 2 * j + i

            def after(b):
                early = p < 2
                beat = jnp.where(early, 5 + p, 3 + 2 * p + b // 2)
                if b == 0:
                    reduce(beat, 0)
                elif b == 2:
                    pl.when(early)(lambda: reduce(beat, 2))
                    pl.when(jnp.logical_not(early))(lambda: reduce(beat, 0))
                else:
                    pl.when(jnp.logical_not(early))(lambda: reduce(beat, 2))
                    pl.when((b == 3) | jnp.logical_not(early))(lambda: reduce(beat, 3))

            backward_pair(p, start, qkv, do, mixed, lse, cosine, sine, bias, dq, after)

            @pl.when(i == 1)
            def _():
                grad = dot(actt[...], qkv[:, cols(j * 768, 768)]).astype(BF).reshape(UNIT)
                if joined:
                    w[4 + j] = grad
                else:
                    spare[j] = grad

            return carry

        return lax.fori_loop(0, 2, inner, carry)

    lax.fori_loop(0, 3, backward_group, 0)
    reduce(LAST_BEAT, 0)

    def after_first(r):
        @pl.when(r % 2 == 0)
        def _():
            reduce(LAST_BEAT + r // 2, 2)
            reduce(LAST_BEAT + r // 2, 3)

    first_back(x, qkv, w, par, dact, small, after_first)
    stores = [load(dact, dx_hbm, 1), load(nxt, next_hbm, 0)]
    stores[0].start()
    for copy in past:
        copy.wait()

    def after_average(r):
        pl.when(r == 0)(lambda: reduce(r + LAST_BEAT + 2, 3))
        pl.when(r == 3)(lambda: reduce(r + LAST_BEAT, 3))

    average(mix_ref, history, g, out, nxt, terms, after_average)
    stores[1].start()
    totals = jnp.sum(terms[...], axis=1, keepdims=True)
    lane = iota((1, 128), 1)
    mix_row = jnp.zeros((1, 128), F32)
    for k in range(5):
        mix_row = jnp.where(lane == k, totals[k : k + 1, :], mix_row)
    if joined:
        values = small[...]
        for s in range(16):
            msg_g[s] = own_part(values, s)
            msg_g[s, 4:5, :] = mix_row
        sums.start()
        land_g[place.flat()] = msg_g[place.flat() % 16]
        merge_up(own, lse)
        part = lambda i: pl.ds(PIECE * i, PIECE)
        for u in (3, 4, 6, 8, 10):
            middle[part(u)] = own[u].astype(F32)
        stores += [load(middle.at[part(3)], go_hbm, 2)]
        stores += [load(lse.at[part(k)], gu_hbm.at[:, pl.ds(768 * k, 768)], 3 + k) for k in range(4)]
        stores += [load(middle.at[part(4 + 2 * k)], gd_hbm.at[part(k)], 7 + k) for k in range(4)]
        for copy in stores[2:]:
            copy.start()
        sums.finish()

        def add(k, total):
            return total + land_g[k]

        total = lax.fori_loop(0, 32, add, jnp.zeros(land_g.shape[1:], F32))
        gains_out[...] = total[0:2, 0:PIECE]
        first_out[...] = total[2:3, 0:PIECE]
        second_out[...] = total[3:4, 0:PIECE]
        mix_out[...] = total[4:5, 0:5]
        reduce(LAST_BEAT + 4, 2)
        for j in range(3):
            middle[part(j)] = own[j].astype(F32)
            for t in range(3):
                src, dst = middle.at[part(j), pl.ds(256 * t, 256)], gq_hbm.at[:, pl.ds(768 * t + 256 * j, 256)]
                stores.append(load(src, dst, 11 + 3 * j + t))
                stores[-1].start()
    else:
        small[4:5, 0:128] = mix_row
        small[4:5, 128:] = jnp.zeros_like(small[4:5, 128:])
        small_out[...] = small[...]
        stores += [load(spare, grad_hbm.at[0:3], 2), load(w.at[3:], grad_hbm.at[3:], 3)]
        for copy in stores[2:]:
            copy.start()
    for copy in stores:
        copy.wait()


VMEM_LIMIT = 67043328
UNIT = (4, 2, 2, PIECE, 768)


def block_pass(joined, start, mix, x, g, history, par, *weights):
    length, width = x.shape
    smem = pl.BlockSpec(memory_space=pltpu.SMEM)
    vmem = pl.BlockSpec(memory_space=pltpu.VMEM)
    anys = pl.BlockSpec(memory_space=pl.ANY)
    low = pltpu.VMEM((length, width), BF)
    full = pltpu.VMEM((length, width), F32)
    dma = pltpu.SemaphoreType.DMA
    small = (8, width)
    scratch = [low] * 5 + [pltpu.VMEM((width, length), BF)] + [low] * 4 + [pltpu.VMEM((length, 3 * width), BF)]
    scratch += [full] * 4
    scratch += [
        pltpu.VMEM((UNITS,) + UNIT, BF),
        pltpu.VMEM((length // BL + 1, BL, BL), F32),
        pltpu.VMEM((length, 128), F32),
        pltpu.VMEM((length, 128), F32),
        pltpu.VMEM((length, 128), F32),
        pltpu.VMEM(small, F32),
        pltpu.VMEM(small, F32),
        pltpu.VMEM(small, F32),
        dma((20,)),
    ]
    grads, sums = [((UNITS,) + UNIT, BF)], [(small, F32)]
    if joined:
        grads = [(shape, F32) for shape in ((PIECE, 3 * width), (PIECE, width), (PIECE, 4 * width), (4 * PIECE, width))]
        sums = [(shape, F32) for shape in ((1, 5), (2, PIECE), (1, PIECE), (1, PIECE))]
        scratch += [
            pltpu.VMEM((UNITS, PIECE, width), BF),
            pltpu.VMEM((2, 4, 2, PIECE, width), BF),
            pltpu.VMEM((GAP, 2, PIECE, width // 2), BF),
            pltpu.VMEM((GAP, 2, PIECE, width // 2), BF),
            pltpu.VMEM((GAP, 4, PIECE, width // 2), BF),
            pltpu.VMEM((GAP, 4, PIECE, width // 2), BF),
            pltpu.VMEM((GAP, 3, PIECE, width // 2), BF),
            pltpu.VMEM((PIECE, 4 * width), BF),
            pltpu.VMEM((8, 128), F32),
            pltpu.VMEM((16, 8, 128), F32),
            pltpu.VMEM((16, 8, 128), F32),
            pltpu.VMEM((32, 8, 128), F32),
            dma((2, UNITS, 8)),
            dma((2, GAP, 9)),
            dma((2, 16)),
            dma((2, 32)),
        ]
    else:
        scratch += [pltpu.VMEM((3,) + UNIT, BF)]
    params = dict(vmem_limit_bytes=VMEM_LIMIT)
    if joined:
        params.update(collective_id=0, has_side_effects=True)
    outs = [((length, width), BF), ((length, width), F32)] + grads + sums
    return pl.pallas_call(
        functools.partial(block_kernel, joined),
        in_specs=[smem, smem, anys, anys, anys] + [vmem] * (len(par) + 1) + [anys] * len(weights),
        out_specs=[anys] * (2 + len(grads)) + [vmem] * len(sums),
        out_shape=[jax.ShapeDtypeStruct(shape, dtype) for shape, dtype in outs],
        scratch_shapes=scratch,
        compiler_params=pltpu.CompilerParams(**params),
        name="block_pass",
    )(start, mix, x, g, history, *par, rotary_table(length), *weights)


def to_units(wq, wo, wu, wd):
    d = wo.shape[0]
    down = wd.reshape(16, 4, PIECE, d).transpose(1, 0, 2, 3).reshape(4, d, d)
    up = wu.reshape(d, 16, 4, PIECE).transpose(2, 0, 1, 3).reshape(4, d, d)
    parts = [
        wq.reshape(d, 3, 3, 256).transpose(2, 0, 1, 3).reshape(3, d, d),
        wo[None],
        jnp.stack([down, up], axis=1).reshape(8, d, d),
    ]
    return jnp.concatenate(parts).reshape((UNITS,) + UNIT)


def from_units(units):
    d = units.shape[-1]
    units = units.reshape(UNITS, d, d)
    gq = units[0:3].reshape(3, d, 3, 256).transpose(1, 2, 0, 3).reshape(d, 3 * d)
    both = units[4:].reshape(4, 2, d, d)
    gd = both[:, 0].reshape(4, 16, PIECE, d).transpose(1, 0, 2, 3).reshape(4 * d, d)
    gu = both[:, 1].reshape(4, d, 16, PIECE).transpose(1, 2, 0, 3).reshape(d, 4 * d)
    return gq, units[3], gu, gd


def local(block_input, history, cotangent, span_start, w_qkv, w_out, w_up, w_down, ln_gains, ln_biases, mix_weights, joined):
    width = block_input.shape[1]
    own = ln_gains.shape[1]
    grad_history = history_grad(mix_weights, cotangent, history.shape[0])
    if joined:
        nxt, grad_input, gq, go, gu, gd, mix, gains, first, second = block_pass(
            True, span_start, mix_weights, block_input, cotangent, history, [ln_gains, ln_biases],
            w_qkv, w_out, w_up, w_down.reshape(4, own, width),
        )
        return nxt, grad_input, grad_history, mix[0], gq, go, gu, gd, gains, first[0], second[0]
    else:
        gather = lambda item, axis: lax.all_gather(item, "shard", axis=axis, tiled=True)
        mine = jnp.concatenate([ln_gains, ln_biases])
        par = jnp.concatenate([gather(mine, 1).astype(F32), jnp.zeros((4, width), F32)])
        weights = to_units(gather(w_qkv, 0), gather(w_out, 0), gather(w_up, 0), gather(w_down, 0))
        nxt, grad_input, units, small = block_pass(
            False, span_start, mix_weights, block_input, cotangent, history, [par], weights
        )

        def owned(item, axis):
            part = lax.psum_scatter(item.astype(BF), "shard", scatter_dimension=axis, tiled=True)
            return lax.psum(part, "rep").astype(F32)

        gq, go, gu, gd = [owned(item, 0) for item in from_units(units)]
        norm_grads = owned(small[:4], 1)
        grad_mix = lax.psum(small[4, :5], ("rep", "shard"))
    return nxt, grad_input, grad_history, grad_mix, gq, go, gu, gd, norm_grads[0:2], norm_grads[2], norm_grads[3]


def solution(mesh):
    token = P(("rep", "shard"), None)
    kept = P("shard", None)
    past = P(None, ("rep", "shard"), None)
    norm = P(None, "shard")
    joined = mesh.shape["rep"] == 2 and mesh.shape["shard"] == 16
    return jax.shard_map(
        functools.partial(local, joined=joined),
        mesh=mesh,
        in_specs=(token, past, token, P(("rep", "shard")), kept, kept, kept, kept, norm, norm, P()),
        out_specs=(token, token, past, P(), kept, kept, kept, kept, norm, P("shard"), P("shard")),
        check_vma=False,
    )
```

```python
import functools
import jax
import jax.numpy as jnp
import numpy as np
from jax import lax
from jax.experimental import pallas as pl
from jax.experimental.pallas import tpu as pltpu
from jax.sharding import PartitionSpec as P

BF = jnp.bfloat16
F32 = jnp.float32
HEADS = 12
SPAN = 256
BL = 256
NEG = -1e30
EPS = 1e-05
FB = 256


def dot(a, b):
    return lax.dot_general(a, b, (((1,), (0,)), ((), ())), preferred_element_type=F32)


def dot_bt(a, b):
    return lax.dot_general(a, b, (((1,), (1,)), ((), ())), preferred_element_type=F32)


def dot_at(a, b):
    return lax.dot_general(a, b, (((0,), (0,)), ((), ())), preferred_element_type=F32)


def iota(shape, axis):
    return lax.broadcasted_iota(jnp.int32, shape, axis)


def cols(start, width=128):
    return pl.ds(pl.multiple_of(start, 128), width)


def rows(start, height):
    return pl.ds(pl.multiple_of(start, height), height)


def norm_parts(values):
    average = jnp.mean(values, axis=-1, keepdims=True)
    centered = values - average
    inverse_std = lax.rsqrt(jnp.mean(centered * centered, axis=-1, keepdims=True) + EPS)
    return centered * inverse_std, inverse_std


def norm_back(incoming, normed, inverse_std, gain_row):
    scaled = incoming * gain_row
    inner = (
        scaled
        - jnp.mean(scaled, axis=-1, keepdims=True)
        - normed * jnp.mean(scaled * normed, axis=-1, keepdims=True)
    )
    return inverse_std * inner


def fold8(values):
    return jnp.sum(values.reshape(values.shape[0] // 8, 8, values.shape[1]), axis=0)


def turn(values, low_quarter):
    return jnp.where(low_quarter, pltpu.roll(values, 96, 1), pltpu.roll(values, 32, 1))


def gelu_parts(upper):
    size = jnp.abs(upper)
    t = 1.0 / (1.0 + 0.2316419 * size)
    density = jnp.exp(-0.5 * upper * upper) * 0.3989422804014327
    poly = ((((1.330274429 * t - 1.821255978) * t + 1.781477937) * t - 0.356563782) * t + 0.319381530) * t
    tail = density * poly
    cdf = jnp.where(upper >= 0, 1.0 - tail, tail)
    return upper * cdf, cdf + upper * density


def split3(values):
    high = values.astype(BF)
    rest = values - high.astype(F32)
    mid = rest.astype(BF)
    return high, mid, (rest - mid.astype(F32)).astype(BF)


def block_bias(start, query0, key0, causal, transposed):
    query = query0 + iota((BL, BL), 1 if transposed else 0)
    key = key0 + iota((BL, BL), 0 if transposed else 1)
    inside = (query >= start) & (query < start + SPAN) & (key >= start) & (key < start + SPAN)
    seen = (inside | (key <= query)) if causal else inside
    return jnp.where(seen, 0.0, NEG).astype(F32)


def fill_bias(start, bias_ref, blocks, transposed):
    span_block = start // BL
    for i in range(blocks):
        bias_ref[i] = block_bias(start, i * BL, i * BL, True, transposed)
    extra = block_bias(start, span_block * BL, (span_block + 1) * BL, False, transposed)
    bias_ref[blocks] = jnp.where(span_block + 1 < blocks, extra, NEG)


def pick(span_block, blocks, load):
    value = load(0)
    for b in range(1, blocks - 1):
        value = lax.select(span_block == b, load(b), value)
    return value


def forward_pair(h, start, qkv_ref, bias_ref, out_ref, lse_ref, after):
    length, width = out_ref.shape
    blocks = length // BL
    span_block = start // BL
    first = iota((BL, 128), 1) < 64
    first_all = iota((length, 128), 1) < 64
    zero = jnp.zeros((), BF)
    one = jnp.ones((), BF)

    oc, qc, kc, vc = pair_columns(h)
    keys = qkv_ref[:, kc]
    values = qkv_ref[:, vc]
    with_ones = (jnp.where(first_all, values, one), jnp.where(first_all, one, values))
    qx = pick(span_block, blocks, lambda b: qkv_ref[pl.ds(b * BL, BL), qc])
    kx = pick(span_block, blocks, lambda b: qkv_ref[pl.ds((b + 1) * BL, BL), kc])
    vx = pick(span_block, blocks, lambda b: qkv_ref[pl.ds((b + 1) * BL, BL), vc])
    extra = []
    for head in (0, 1):
        mine = first if head == 0 else ~first
        s = dot_bt(jnp.where(mine, qx, zero), kx) + bias_ref[blocks]
        peak = jnp.max(s, axis=1, keepdims=True)
        extra.append((peak, dot(jnp.exp(s - peak).astype(BF), jnp.where(mine, vx, one))))
    for i in range(blocks):
        outs, peaks = [], []
        here = span_block == i
        qi = qkv_ref[pl.ds(i * BL, BL), qc]
        for head in (0, 1):
            mine = first if head == 0 else ~first
            qm = jnp.where(mine, qi, zero)
            extra_peak, extra_out = extra[head]
            diag = dot_bt(qm, keys[i * BL : (i + 1) * BL]) + bias_ref[i]
            peak = jnp.max(diag, axis=1, keepdims=True)
            if i > 0:
                left = dot_bt(qm, keys[: i * BL])
                peak = jnp.maximum(peak, jnp.max(left, axis=1, keepdims=True))
            if i < blocks - 1:
                peak = jnp.maximum(peak, jnp.where(here, extra_peak, NEG))
            out = dot(jnp.exp(diag - peak).astype(BF), with_ones[head][i * BL : (i + 1) * BL])
            if i > 0:
                out = out + dot(jnp.exp(left - peak).astype(BF), with_ones[head][: i * BL])
            if i < blocks - 1:
                out = out + jnp.where(here, jnp.exp(extra_peak - peak), 0.0) * extra_out
            outs.append(out)
            peaks.append(peak)
        top = jnp.where(first, outs[0], outs[1])
        total = pltpu.roll(jnp.where(first, outs[1], outs[0]), 64, 1)
        out_ref[pl.ds(i * BL, BL), oc] = (top / total).astype(BF)
        lse_ref[pl.ds(i * BL, BL), oc] = jnp.where(first, peaks[0], peaks[1]) + jnp.log(total)
        after(i)


def backward_pair(h, start, qkv_ref, do_ref, out_ref, lse_ref, cos_ref, sin_ref, bias_ref, dq_ref, after):
    length, width = out_ref.shape
    blocks = length // BL
    span_block = start // BL
    lane_all = iota((length, 128), 1)
    lane = iota((BL, 128), 1)
    first = lane < 64
    low_quarter = (lane % 64) < 32
    zero = jnp.zeros((), BF)
    one = jnp.ones((), BF)

    def extend(values, column, head, lanes):
        a, b, c = split3(-column)
        base = 64 * (1 - head)
        parts = jnp.where(
            lanes == base, a, jnp.where(lanes == base + 1, b, jnp.where(lanes == base + 2, c, zero))
        )
        return jnp.where(lanes < 64, values, parts) if head == 0 else jnp.where(lanes < 64, parts, values)

    def keep(values, head, lanes, other):
        return jnp.where(lanes < 64, values, other) if head == 0 else jnp.where(lanes < 64, other, values)

    def rotate_back(values, cosine, sine):
        return values * cosine - turn(values, low_quarter) * sine

    oc, qc, kc, vc = pair_columns(h)

    def query_side(load, lanes):
        q, do, lse, out = load(qkv_ref, qc), load(do_ref, oc), load(lse_ref, oc), load(out_ref, oc)
        product = do.astype(F32) * out.astype(F32)
        sides = []
        for head in (0, 1):
            mine = (lanes < 64) if head == 0 else (lanes >= 64)
            delta = jnp.sum(jnp.where(mine, product, 0.0), axis=1, keepdims=True)
            sides.append(
                (
                    extend(q, lse[:, 64 * head : 64 * head + 1], head, lanes),
                    keep(q, head, lanes, zero),
                    extend(do, delta, head, lanes),
                    keep(do, head, lanes, zero),
                )
            )
        return sides

    everything = query_side(lambda ref, at: ref[:, at], lane_all)
    extra_side = query_side(
        lambda ref, at: pick(span_block, blocks, lambda b: ref[pl.ds(b * BL, BL), at]), lane
    )
    kx = pick(span_block, blocks, lambda b: qkv_ref[pl.ds((b + 1) * BL, BL), kc])
    vx = pick(span_block, blocks, lambda b: qkv_ref[pl.ds((b + 1) * BL, BL), vc])

    def block(k, v, head, qa, qm, da, dm, bias):
        s = dot_bt(keep(k, head, lane, one), qa)
        if bias is not None:
            s = s + bias
        p = jnp.exp(s)
        ds = (p * dot_bt(keep(v, head, lane, one), da)).astype(BF)
        return dot(p.astype(BF), dm), dot(ds, qm), dot_at(ds, keep(k, head, lane, zero))

    parts = [block(kx, vx, head, *extra_side[head], bias_ref[blocks]) for head in (0, 1)]
    dvx, dkx, dqx = [a + b for a, b in zip(*parts)]
    for j in range(blocks):
        at = slice(j * BL, (j + 1) * BL)
        rest = slice((j + 1) * BL, length)
        kj = qkv_ref[at, kc]
        vj = qkv_ref[at, vc]
        dv = jnp.where(span_block + 1 == j, dvx, 0.0) if j > 0 else None
        dk = jnp.where(span_block + 1 == j, dkx, 0.0) if j > 0 else None
        dq = jnp.where(span_block == j, dqx, 0.0) if j < blocks - 1 else None
        dq_rest = None
        add = lambda old, new: new if old is None else old + new
        for head in (0, 1):
            side = everything[head]
            a, b, c = block(kj, vj, head, *[item[at] for item in side], bias_ref[j])
            dv, dk, dq = add(dv, a), add(dk, b), add(dq, c)
            if j < blocks - 1:
                a, b, c = block(kj, vj, head, *[item[rest] for item in side], None)
                dv, dk, dq_rest = add(dv, a), add(dk, b), add(dq_rest, c)
        cosine, sine = cos_ref[at], sin_ref[at]
        if j > 0:
            dq = dq + dq_ref[at]
        qkv_ref[at, vc] = dv.astype(BF)
        qkv_ref[at, kc] = rotate_back(dk, cosine, sine).astype(BF)
        qkv_ref[at, qc] = rotate_back(dq * 0.125, cosine, sine).astype(BF)
        if j < blocks - 1:
            dq_ref[rest] = dq_rest if j == 0 else dq_ref[rest] + dq_rest
        after(j)


MESH = pl.DeviceIdType.MESH
UNITS = 12
PIECE = 48
GAP = 4
GATHER_AT = (-1, 7, 12, 16, 19)
GATHER_FROM = (4, 2, 2, 2, 2)
REDUCE_AT = (0, 2, 6, 11, 15, 18)
LATE_BEAT, LAST_BEAT = 11, 15


def at_tick(stages, beat, phase):
    return [(stage, beat - at // 4) for stage, at in reversed(list(enumerate(stages))) if at % 4 == phase]


class Place:
    def __init__(self):
        self.y = lax.axis_index("rep")
        s = lax.axis_index("shard")
        self.z, self.x, self.c = s // 4, (s // 2) % 2, s % 2

    def at(self, y, z, x, c):
        return (y, (z * 2 + x) * 2 + c)

    def twin(self):
        return self.at(self.y, self.z, self.x, 1 - self.c)

    def across_x(self):
        return self.at(self.y, self.z, 1 - self.x, self.c)

    def across_y(self):
        return self.at(1 - self.y, self.z, self.x, self.c)

    def along_z(self, k):
        return self.at(self.y, (self.z + k) % 4, self.x, self.c)

    def flat(self):
        return ((self.y * 4 + self.z) * 2 + self.x) * 2 + self.c

    def other(self, k):
        there = (self.flat() + k) % 32
        return there // 16, there % 16


def half(y):
    return pl.ds(pl.multiple_of(y * 384, 128), 384)


def remote(src, dst, sems, slot, kind, device):
    return pltpu.make_async_remote_copy(
        src_ref=src,
        dst_ref=dst,
        send_sem=sems.at[0, slot, kind],
        recv_sem=sems.at[1, slot, kind],
        device_id=device,
        device_id_type=MESH,
    )


class Gather:
    def __init__(self, place, w_ref, sems):
        self.p, self.w, self.sems = place, w_ref, sems

    def copies(self, stage, u, mine):
        p, w = self.p, self.w
        slot = u
        y, z, x, c = p.y, p.z, p.x, p.c

        def same(ref, kind, device):
            return remote(ref, ref, self.sems, slot, kind, device)

        if stage == 0:
            return [
                same(w.at[u, z if mine else (z + 4 - k) % 4, x, c, :, half(y)], k - 1, p.along_z(k)) for k in (1, 2, 3)
            ]
        if stage == 1:
            return [
                same(w.at[u, :, x if mine else 1 - x, c, :, half(y)], 3, p.across_x()),
                same(w.at[u, :, x, c, :, half(y if mine else 1 - y)], 4, p.across_y()),
            ]
        if stage == 2:
            return [
                same(w.at[u, 0:2, x if mine else 1 - x, c, :, half(1 - y)], 5, p.across_x()),
                same(w.at[u, 2:4, 1 - x, c, :, half(y if mine else 1 - y)], 6, p.across_y()),
            ]
        return [same(w.at[u, :, :, c if mine else 1 - c], 7, p.twin())]

    def step(self, stage, u):
        if stage > 0:
            for copy in self.copies(stage - 1, u, False):
                copy.wait_recv()
            for copy in self.copies(stage - 1, u, True):
                copy.wait_send()
        if stage < 4:
            for copy in self.copies(stage, u, True):
                copy.start()

    def tick(self, beat, phase):
        for stage, u in at_tick(GATHER_AT, beat, phase):
            pl.when((u >= GATHER_FROM[stage]) & (u < UNITS))(functools.partial(self.step, stage, u))


class Reduce:
    def __init__(self, place, w_ref, own_ref, rc, rdx, rdy, rxx, rxy, rz, sems):
        self.p, self.w, self.own, self.sems = place, w_ref, own_ref, sems
        self.rc, self.rdx, self.rdy, self.rxx, self.rxy, self.rz = rc, rdx, rdy, rxx, rxy, rz

    def copies(self, stage, n, mine):
        p, w = self.p, self.w
        u = held_in(n)
        slot = n % GAP
        y, z, x, c = p.y, p.z, p.x, p.c

        def send(src, dst, kind, device):
            return remote(src, dst, self.sems, slot, kind, device)

        if stage == 0:
            return [send(w.at[u, :, :, 1 - c], self.rc.at[n % 2], 0, p.twin())]
        if stage == 1:
            return [
                send(w.at[u, 0:2, 1 - x, c, :, half(1 - y)], self.rdx.at[slot], 1, p.across_x()),
                send(w.at[u, 2:4, 1 - x, c, :, half(1 - y)], self.rdy.at[slot], 2, p.across_y()),
            ]
        if stage == 2:
            return [
                send(w.at[u, :, 1 - x, c, :, half(y)], self.rxx.at[slot], 3, p.across_x()),
                send(w.at[u, :, x, c, :, half(1 - y)], self.rxy.at[slot], 4, p.across_y()),
            ]
        if stage == 3:
            return [
                send(w.at[u, (z + k) % 4, x, c, :, half(y)], self.rz.at[slot, k - 1], 4 + k, p.along_z(k))
                for k in (1, 2, 3)
            ]
        there = self.own.at[unit_of(n), :, half(y if mine else 1 - y)]
        return [send(there, there, 8, p.across_y())]

    def add(self, stage, n):
        p, w = self.p, self.w
        u = held_in(n)
        slot = n % GAP
        y, z, x, c = p.y, p.z, p.x, p.c
        f = lambda value: value.astype(F32)
        if stage == 1:

            def piece(zz, carry):
                w[u, zz, :, c] = w[u, zz, :, c] + self.rc[n % 2, zz]
                return carry

            lax.fori_loop(0, 4, piece, 0)
        if stage == 2:
            w[u, 0:2, x, c, :, half(1 - y)] = w[u, 0:2, x, c, :, half(1 - y)] + self.rdx[slot]
            w[u, 2:4, 1 - x, c, :, half(y)] = w[u, 2:4, 1 - x, c, :, half(y)] + self.rdy[slot]
        if stage == 3:
            w[u, :, x, c, :, half(y)] = (
                f(w[u, :, x, c, :, half(y)]) + f(self.rxx[slot]) + f(self.rxy[slot])
            ).astype(BF)
        if stage == 4:
            total = f(w[u, z, x, c, :, half(y)])
            for k in (0, 1, 2):
                total = total + f(self.rz[slot, k])
            self.own[unit_of(n), :, half(y)] = total.astype(BF)

    def step(self, stage, n):
        if stage > 0:
            for copy in self.copies(stage - 1, n, False):
                copy.wait_recv()
            for copy in self.copies(stage - 1, n, True):
                copy.wait_send()
            self.add(stage, n)
        if stage < 5:
            for copy in self.copies(stage, n, True):
                copy.start()

    def tick(self, beat, phase):
        for stage, place in at_tick(REDUCE_AT, beat, phase):
            if isinstance(place, int):
                if place == LAST_BEAT:
                    self.step(stage, UNITS - 1)
            else:
                last = place == LAST_BEAT
                late = place == LATE_BEAT
                n = jnp.where(last, UNITS - 1, jnp.where(late, UNITS - 2, place))
                here = ((place >= 0) & (place < UNITS - 2)) | late | last
                pl.when(here)(functools.partial(self.step, stage, n))


def unit_of(n):
    if isinstance(n, int):
        return 4 + n if n < 8 else 3 if n == 8 else n - 9
    return jnp.where(n < 8, 4 + n, jnp.where(n == 8, 3, n - 9))


def held_in(n):
    if isinstance(n, int):
        return 4 + n if n < 8 else 3 if n == 8 else n - 5
    return jnp.where(n < 8, 4 + n, jnp.where(n == 8, 3, n - 5))


def assemble(tile, pieces, load):
    total = None
    for dst, key, src, length in pieces:
        at = max(dst, 128 * tile)
        while at < min(dst + length, 128 * tile + 128):
            lane = src + at - dst
            count = min(dst + length, 128 * tile + 128, at + 128 - lane % 128) - at
            value = load(key, lane // 128)
            shift = (at - lane) % 128
            value = value if shift == 0 else pltpu.roll(value, shift, 1)
            lanes = iota(value.shape, 1)
            low = at - 128 * tile
            inside = (lanes >= low) & (lanes < low + count)
            total = jnp.where(inside, value, 0.0 if total is None else total)
            at += count
    return total


def split_up(raw_ref, home_ref):
    load = lambda key, t: raw_ref[:, 128 * t : 128 * t + 128].astype(F32)
    for q in range(4):
        pieces = [(PIECE * s, 0, 4 * PIECE * s + PIECE * q, PIECE) for s in range(16)]
        for t in range(6):
            home_ref[5 + 2 * q, :, 128 * t : 128 * t + 128] = assemble(t, pieces, load).astype(BF)


def merge_up(own_ref, out_ref):
    load = lambda q, t: own_ref[5 + 2 * q, :, 128 * t : 128 * t + 128].astype(F32)
    pieces = [(4 * PIECE * s + PIECE * q, q, PIECE * s, PIECE) for s in range(16) for q in range(4)]
    for t in range(24):
        here = [p for p in pieces if p[0] < 128 * t + 128 and p[0] + PIECE > 128 * t]
        at = PIECE * (t // 6)
        out_ref[at : at + PIECE, 128 * (t % 6) : 128 * (t % 6) + 128] = assemble(t, here, load)


class Exchange:
    def __init__(self, place, sent_ref, land_ref, sems, everywhere):
        self.p, self.sent, self.land, self.sems, self.everywhere = place, sent_ref, land_ref, sems, everywhere

    def copy(self, k, mine):
        p = self.p
        if self.everywhere:
            count = 32
            y, s = p.other(k)
            src, me = self.sent.at[s], p.flat()
        else:
            count = 16
            me = p.flat() % 16
            y, s = p.y, (me + k) % 16
            src = self.sent
        return pltpu.make_async_remote_copy(
            src_ref=src,
            dst_ref=self.land.at[me if mine else (me + count - k) % count],
            send_sem=self.sems.at[0, k],
            recv_sem=self.sems.at[1, k],
            device_id=(y, s),
            device_id_type=MESH,
        )

    def start(self):
        def send(k, carry):
            self.copy(k, True).start()
            return carry

        lax.fori_loop(1, self.land.shape[0], send, 0)

    def finish(self):
        def wait(k, carry):
            self.copy(k, False).wait_recv()
            self.copy(k, True).wait_send()
            return carry

        lax.fori_loop(1, self.land.shape[0], wait, 0)


def own_part(value, s):
    load = lambda key, t: value[:, 128 * t : 128 * t + 128]
    return assemble(0, [(0, 0, PIECE * s, PIECE)], load)


def history_kernel(mix_ref, g_ref, grad_ref):
    g = g_ref[...].astype(F32)
    for k in range(grad_ref.shape[0]):
        grad_ref[k] = mix_ref[k] * g


def history_grad(mix, g, past):
    length, width = g.shape
    height = 256
    return pl.pallas_call(
        history_kernel,
        grid=(length // height,),
        in_specs=[pl.BlockSpec(memory_space=pltpu.SMEM), pl.BlockSpec((height, width), lambda i: (i, 0))],
        out_specs=pl.BlockSpec((past, height, width), lambda i: (0, i, 0)),
        out_shape=jax.ShapeDtypeStruct((past, length, width), F32),
        name="history_grad",
    )(mix, g)


def average(mix_ref, history, g_ref, out_ref, next_ref, small_ref, after):
    height = 256
    past = len(history)
    zero = jnp.zeros((8, g_ref.shape[1]), F32)

    def chunk(r, terms):
        at = rows(r * height, height)
        g = g_ref[at, :].astype(F32)
        output = out_ref[at, :]
        total = mix_ref[past] * output
        new = []
        for k in range(past):
            h = history[k][at, :].astype(F32)
            total = total + mix_ref[k] * h
            new.append(terms[k] + fold8(g * h))
        next_ref[at, :] = total.astype(BF)
        after(r)
        return tuple(new) + (terms[past] + fold8(g * output),)

    terms = lax.fori_loop(0, g_ref.shape[0] // height, chunk, (zero,) * (past + 1))
    for k in range(past + 1):
        small_ref[k : k + 1, :] = jnp.sum(terms[k], axis=0, keepdims=True)


def first_norm(x_ref, par_ref, act_ref):
    height = 128

    def chunk(r, carry):
        at = rows(r * height, height)
        normed, _ = norm_parts(x_ref[at, :].astype(F32))
        act_ref[at, :] = (normed * par_ref[0:1, :] + par_ref[2:3, :]).astype(BF)
        return carry

    lax.fori_loop(0, x_ref.shape[0] // height, chunk, 0)


def pair_columns(h):
    base = (h // 2) * 768 + (h % 2) * 128
    return cols(h * 128), cols(base), cols(base + 256), cols(base + 512)


def unit(w_ref, u):
    return w_ref[u].reshape(768, 768)


def project(j, act_ref, w_ref, cos_ref, sin_ref, qkv_ref):
    height = 256
    low_quarter = (iota((height, 128), 1) % 64) < 32

    def chunk(r, carry):
        at = rows(r * height, height)
        out = dot(act_ref[at, :], unit(w_ref, j))
        cosine, sine = cos_ref[at, :], sin_ref[at, :]
        for piece in range(6):
            u = out[:, piece * 128 : piece * 128 + 128]
            if piece < 4:
                u = u * cosine + turn(u, low_quarter) * sine
            if piece < 2:
                u = u * 0.125
            qkv_ref[at, cols(j * 768 + piece * 128)] = u.astype(BF)
        return carry

    lax.fori_loop(0, act_ref.shape[0] // height, chunk, 0)


def attention_out(x_ref, mixed_ref, w_ref, par_ref, middle_ref, act_ref, actt_ref, out_ref, dact_ref, after):
    height = 256

    def chunk(r, carry):
        at = rows(r * height, height)
        middle = x_ref[at, :].astype(F32) + dot(mixed_ref[at, :], unit(w_ref, 3))
        middle_ref[at, :] = middle
        out_ref[at, :] = middle
        dact_ref[at, :] = jnp.zeros_like(middle)
        normed, _ = norm_parts(middle)
        act = (normed * par_ref[1:2, :] + par_ref[3:4, :]).astype(BF)
        act_ref[at, :] = act
        actt_ref[:, rows(r * height, height)] = act.T
        after(r)
        return carry

    lax.fori_loop(0, x_ref.shape[0] // height, chunk, 0)


def feed_forward(z, act_ref, actt_ref, gb_ref, w_ref, hid_ref, gu_ref, out_ref, dact_ref, after):
    height = 256

    def chunk(r, carry):
        at = rows(r * height, height)
        down, up = unit(w_ref, 4 + 2 * z), unit(w_ref, 5 + 2 * z)
        hidden, slope = gelu_parts(dot(act_ref[at, :], up))
        hidden = hidden.astype(BF)
        hid_ref[at, :] = hidden
        gu = (dot_bt(gb_ref[at, :], down) * slope).astype(BF)
        gu_ref[at, :] = gu
        out_ref[at, :] += dot(hidden, down)
        dact_ref[at, :] += dot_bt(gu, up)
        after(r)
        return carry

    lax.fori_loop(0, act_ref.shape[0] // height, chunk, 0)
    w_ref[4 + 2 * z] = dot_at(hid_ref[...], gb_ref[...]).astype(BF).reshape(w_ref.shape[1:])
    w_ref[5 + 2 * z] = dot(actt_ref[...], gu_ref[...]).astype(BF).reshape(w_ref.shape[1:])


def branch_grad(mix4, g_ref, gb_ref):
    height = 256

    def chunk(r, carry):
        at = rows(r * height, height)
        gb_ref[at, :] = (mix4 * g_ref[at, :].astype(F32)).astype(BF)
        return carry

    lax.fori_loop(0, g_ref.shape[0] // height, chunk, 0)


def middle_back(mix4, g_ref, middle_ref, dact_ref, mixed_ref, w_ref, par_ref, ga_ref, do_ref, small_ref, after):
    height = 256
    zero = jnp.zeros((8, g_ref.shape[1]), F32)

    def chunk(r, carry):
        gain, bias = carry
        at = rows(r * height, height)
        normed, inverse = norm_parts(middle_ref[at, :])
        dact = dact_ref[at, :]
        gain = gain + fold8(dact * normed)
        bias = bias + fold8(dact)
        grad = mix4 * g_ref[at, :].astype(F32) + norm_back(dact, normed, inverse, par_ref[1:2, :])
        dact_ref[at, :] = grad
        low = grad.astype(BF)
        ga_ref[at, :] = low
        do_ref[at, :] = dot_bt(low, unit(w_ref, 3)).astype(BF)
        after(r)
        return gain, bias

    gain, bias = lax.fori_loop(0, g_ref.shape[0] // height, chunk, (zero, zero))
    small_ref[1:2, :] = jnp.sum(gain, axis=0, keepdims=True)
    small_ref[3:4, :] = jnp.sum(bias, axis=0, keepdims=True)
    w_ref[3] = dot_at(mixed_ref[...], ga_ref[...]).astype(BF).reshape(w_ref.shape[1:])


def first_back(x_ref, qkv_ref, w_ref, par_ref, dmid_ref, small_ref, after):
    height = 256
    zero = jnp.zeros((8, x_ref.shape[1]), F32)

    def chunk(r, carry):
        gain, bias = carry
        at = rows(r * height, height)
        dact = None
        for j in range(3):
            share = dot_bt(qkv_ref[at, cols(j * 768, 768)], unit(w_ref, j))
            dact = share if dact is None else dact + share
        normed, inverse = norm_parts(x_ref[at, :].astype(F32))
        gain = gain + fold8(dact * normed)
        bias = bias + fold8(dact)
        dmid_ref[at, :] += norm_back(dact, normed, inverse, par_ref[0:1, :])
        after(r)
        return gain, bias

    gain, bias = lax.fori_loop(0, x_ref.shape[0] // height, chunk, (zero, zero))
    small_ref[0:1, :] = jnp.sum(gain, axis=0, keepdims=True)
    small_ref[2:3, :] = jnp.sum(bias, axis=0, keepdims=True)


def fill_tables(table_ref, cos_ref, sin_ref):
    blocks = cos_ref.shape[0] // 32
    cb, sb, sign = table_ref[0], table_ref[1], table_ref[2]

    def block(a, carry):
        ca, sa = table_ref[3, pl.ds(a, 1), :], table_ref[4, pl.ds(a, 1), :]
        at = rows(a * 32, 32)
        cos_ref[at, :] = ca * cb - sa * sb
        sin_ref[at, :] = (sa * cb + ca * sb) * sign
        return carry

    lax.fori_loop(0, blocks, block, 0)


def rotary_table(length):
    freq = np.tile(np.exp(-np.log(10000.0) * np.arange(32) / 32.0), 4)[None, :]
    fine = np.arange(32)[:, None] * freq
    coarse = 32 * np.arange(32)[:, None] * freq
    sign = np.tile(np.repeat([-1.0, 1.0], 32), 2)[None, :] * np.ones((32, 1))
    return jnp.asarray(np.stack([np.cos(fine), np.sin(fine), sign, np.cos(coarse), np.sin(coarse)]), F32)


def block_kernel(joined, *refs):
    if joined:
        start_ref, mix_ref, x_hbm, g_hbm, history_hbm, gains_ref, biases_ref, table_ref = refs[:8]
        wq_hbm, wo_hbm, wu_hbm, wd_hbm = refs[8:12]
        next_hbm, dx_hbm, gq_hbm, go_hbm, gu_hbm, gd_hbm, mix_out, gains_out, first_out, second_out = refs[12:22]
        refs = refs[22:]
    else:
        start_ref, mix_ref, x_hbm, g_hbm, history_hbm, par_in, table_ref, w_hbm = refs[:8]
        next_hbm, dx_hbm, grad_hbm, small_out = refs[8:12]
        refs = refs[12:]
    x, g, gb, act1, act2, actt, mixed, nxt, hid, gu, qkv, lse, middle, out, dact = refs[:15]
    w, bias, dq, cosine, sine, small, par, terms, loads = refs[15:24]
    start = start_ref[0]
    mix4 = mix_ref[4]
    length = x.shape[0]

    load = lambda src, dst, i: pltpu.make_async_copy(src, dst, loads.at[i])
    first = [load(x_hbm, x, 0)]
    later = [load(g_hbm, g, 1)]
    if joined:
        own, rc, rdx, rdy, rxx, rxy, rz, raw, msg_p, land_p, msg_g, land_g, gsems, rsems, psems, ssems = refs[24:]
        place = Place()
        home = w.at[:, place.z, place.x, place.c]
        for j in range(3):
            for t in range(3):
                first.append(
                    load(wq_hbm.at[:, pl.ds(768 * t + 256 * j, 256)], home.at[j, :, pl.ds(256 * t, 256)], 3 + 3 * j + t)
                )
        first.append(load(wo_hbm, home.at[3], 12))
        for k in range(4):
            first.append(load(wd_hbm.at[k], home.at[4 + 2 * k], 13 + k))
        first.append(load(wu_hbm, raw, 17))
    else:
        spare = refs[24]
        first.append(load(w_hbm, w, 3))
    for copy in first + later:
        copy.start()
    if joined:
        for copy in first[1:]:
            copy.wait()
        barrier = pltpu.get_barrier_semaphore()

        def greet(k, carry):
            pl.semaphore_signal(barrier, inc=1, device_id=place.other(k), device_id_type=MESH)
            return carry

        lax.fori_loop(1, 32, greet, 0)
        pl.semaphore_wait(barrier, 31)
        units = Gather(place, w, gsems)
        gather = units.tick
        reduce = Reduce(place, w, own, rc, rdx, rdy, rxx, rxy, rz, rsems).tick
        params = Exchange(place, msg_p, land_p, psems, False)
        sums = Exchange(place, msg_g, land_g, ssems, True)
        units.step(0, 0)
        msg_p[...] = jnp.zeros_like(msg_p)
        msg_p[0:2, 0:PIECE] = gains_ref[...].astype(F32)
        msg_p[2:4, 0:PIECE] = biases_ref[...].astype(F32)
        params.start()
        land_p[place.flat() % 16] = msg_p[...]
        fill_tables(table_ref, cosine, sine)
        split_up(raw, home)
        units.step(1, 0)
        for u in (1, 2, 3):
            units.step(0, u)
    else:
        gather = reduce = lambda beat, phase: None
        first[1].wait()
        par[...] = par_in[...]
        fill_tables(table_ref, cosine, sine)
    small[...] = jnp.zeros_like(small)
    fill_bias(start, bias, length // BL, False)
    for copy in [first[0]] + later:
        copy.wait()
    branch_grad(mix4, g, gb)
    if joined:
        params.finish()
        pieces = [(PIECE * s, s, 0, PIECE) for s in range(16)]
        for t in range(6):
            here = [p for p in pieces if p[0] < 128 * t + 128 and p[0] + PIECE > 128 * t]
            par[:, 128 * t : 128 * t + 128] = assemble(t, here, lambda s, _: land_p[s])
        units.step(2, 0)
    first_norm(x, par, act1)
    if joined:
        units.step(3, 0)
        units.step(1, 1)
        units.step(4, 0)

    def forward_group(j, carry):
        project(j, act1, w, cosine, sine, qkv)

        def inner(i, carry):
            p = 2 * j + i

            def after(b):
                for stage, pair, at in ((2, 0, 3), (3, 1, 2), (4, 1, 3)):
                    if joined and b == at:
                        pl.when(p == pair)(functools.partial(units.step, stage, 1))
                gather(3 + p, b)

            forward_pair(p, start, qkv, bias, mixed, lse, after)
            return carry

        return lax.fori_loop(0, 2, inner, carry)

    lax.fori_loop(0, 3, forward_group, 0)

    def after_rows(r):
        for phase in (0, 3):
            pl.when(r == phase)(lambda: gather(r - phase + 9, phase))

    attention_out(x, mixed, w, par, middle, act2, actt, out, dact, after_rows)

    def ff_group(z, carry):
        def after(r):
            @pl.when(r % 2 == 0)
            def _():
                gather(10 + 2 * z + r // 2, 0)
                reduce(2 * z - 4 + r // 2, 0)

            @pl.when(r % 2 == 1)
            def _():
                gather(10 + 2 * z + r // 2, 3)
                reduce(2 * z - 4 + r // 2, 2)
                reduce(2 * z - 4 + r // 2, 3)

        feed_forward(z, act2, actt, gb, w, hid, gu, out, dact, after)
        return carry

    lax.fori_loop(0, 4, ff_group, 0)

    def after_middle(r):
        for phase in (0, 2, 3):
            pl.when(r == phase)(lambda: reduce(r - phase + 4, phase))

    ga, do = gb, act2
    middle_back(mix4, g, middle, dact, mixed, w, par, ga, do, small, after_middle)
    fill_bias(start, bias, length // BL, True)
    actt[...] = act1[...].T
    history = [hid, gu, gb, act1]
    past = [load(history_hbm.at[k], history[k], 12 + k) for k in range(4)]
    for copy in past:
        copy.start()

    def backward_group(j, carry):
        def inner(i, carry):
            p = 2 * j + i

            def after(b):
                early = p < 2
                beat = jnp.where(early, 5 + p, 3 + 2 * p + b // 2)
                if b == 0:
                    reduce(beat, 0)
                elif b == 2:
                    pl.when(early)(lambda: reduce(beat, 2))
                    pl.when(jnp.logical_not(early))(lambda: reduce(beat, 0))
                else:
                    pl.when(jnp.logical_not(early))(lambda: reduce(beat, 2))
                    pl.when((b == 3) | jnp.logical_not(early))(lambda: reduce(beat, 3))

            backward_pair(p, start, qkv, do, mixed, lse, cosine, sine, bias, dq, after)

            @pl.when(i == 1)
            def _():
                grad = dot(actt[...], qkv[:, cols(j * 768, 768)]).astype(BF).reshape(UNIT)
                if joined:
                    w[4 + j] = grad
                else:
                    spare[j] = grad

            return carry

        return lax.fori_loop(0, 2, inner, carry)

    lax.fori_loop(0, 3, backward_group, 0)
    reduce(LAST_BEAT, 0)

    def after_first(r):
        @pl.when(r % 2 == 0)
        def _():
            reduce(LAST_BEAT + r // 2, 2)
            reduce(LAST_BEAT + r // 2, 3)

    first_back(x, qkv, w, par, dact, small, after_first)
    stores = [load(dact, dx_hbm, 1), load(nxt, next_hbm, 0)]
    stores[0].start()
    for copy in past:
        copy.wait()

    def after_average(r):
        pl.when(r == 0)(lambda: reduce(r + LAST_BEAT + 2, 3))
        pl.when(r == 3)(lambda: reduce(r + LAST_BEAT, 3))

    average(mix_ref, history, g, out, nxt, terms, after_average)
    stores[1].start()
    totals = jnp.sum(terms[...], axis=1, keepdims=True)
    lane = iota((1, 128), 1)
    mix_row = jnp.zeros((1, 128), F32)
    for k in range(5):
        mix_row = jnp.where(lane == k, totals[k : k + 1, :], mix_row)
    if joined:
        values = small[...]
        for s in range(16):
            msg_g[s] = own_part(values, s)
            msg_g[s, 4:5, :] = mix_row
        sums.start()
        land_g[place.flat()] = msg_g[place.flat() % 16]
        merge_up(own, lse)
        part = lambda i: pl.ds(PIECE * i, PIECE)
        for u in (3, 4, 6, 8, 10):
            middle[part(u)] = own[u].astype(F32)
        stores += [load(middle.at[part(3)], go_hbm, 2)]
        stores += [load(lse.at[part(k)], gu_hbm.at[:, pl.ds(768 * k, 768)], 3 + k) for k in range(4)]
        stores += [load(middle.at[part(4 + 2 * k)], gd_hbm.at[part(k)], 7 + k) for k in range(4)]
        for copy in stores[2:]:
            copy.start()
        sums.finish()

        def add(k, total):
            return total + land_g[k]

        total = lax.fori_loop(0, 32, add, jnp.zeros(land_g.shape[1:], F32))
        gains_out[...] = total[0:2, 0:PIECE]
        first_out[...] = total[2:3, 0:PIECE]
        second_out[...] = total[3:4, 0:PIECE]
        mix_out[...] = total[4:5, 0:5]
        reduce(LAST_BEAT + 4, 2)
        for j in range(3):
            middle[part(j)] = own[j].astype(F32)
            for t in range(3):
                src, dst = middle.at[part(j), pl.ds(256 * t, 256)], gq_hbm.at[:, pl.ds(768 * t + 256 * j, 256)]
                stores.append(load(src, dst, 11 + 3 * j + t))
                stores[-1].start()
    else:
        small[4:5, 0:128] = mix_row
        small[4:5, 128:] = jnp.zeros_like(small[4:5, 128:])
        small_out[...] = small[...]
        stores += [load(spare, grad_hbm.at[0:3], 2), load(w.at[3:], grad_hbm.at[3:], 3)]
        for copy in stores[2:]:
            copy.start()
    for copy in stores:
        copy.wait()


VMEM_LIMIT = 67043328
UNIT = (4, 2, 2, PIECE, 768)


def block_pass(joined, start, mix, x, g, history, par, *weights):
    length, width = x.shape
    smem = pl.BlockSpec(memory_space=pltpu.SMEM)
    vmem = pl.BlockSpec(memory_space=pltpu.VMEM)
    anys = pl.BlockSpec(memory_space=pl.ANY)
    low = pltpu.VMEM((length, width), BF)
    full = pltpu.VMEM((length, width), F32)
    dma = pltpu.SemaphoreType.DMA
    small = (8, width)
    scratch = [low] * 5 + [pltpu.VMEM((width, length), BF)] + [low] * 4 + [pltpu.VMEM((length, 3 * width), BF)]
    scratch += [full] * 4
    scratch += [
        pltpu.VMEM((UNITS,) + UNIT, BF),
        pltpu.VMEM((length // BL + 1, BL, BL), F32),
        pltpu.VMEM((length, 128), F32),
        pltpu.VMEM((length, 128), F32),
        pltpu.VMEM((length, 128), F32),
        pltpu.VMEM(small, F32),
        pltpu.VMEM(small, F32),
        pltpu.VMEM(small, F32),
        dma((20,)),
    ]
    grads, sums = [((UNITS,) + UNIT, BF)], [(small, F32)]
    if joined:
        grads = [(shape, F32) for shape in ((PIECE, 3 * width), (PIECE, width), (PIECE, 4 * width), (4 * PIECE, width))]
        sums = [(shape, F32) for shape in ((1, 5), (2, PIECE), (1, PIECE), (1, PIECE))]
        scratch += [
            pltpu.VMEM((UNITS, PIECE, width), BF),
            pltpu.VMEM((2, 4, 2, PIECE, width), BF),
            pltpu.VMEM((GAP, 2, PIECE, width // 2), BF),
            pltpu.VMEM((GAP, 2, PIECE, width // 2), BF),
            pltpu.VMEM((GAP, 4, PIECE, width // 2), BF),
            pltpu.VMEM((GAP, 4, PIECE, width // 2), BF),
            pltpu.VMEM((GAP, 3, PIECE, width // 2), BF),
            pltpu.VMEM((PIECE, 4 * width), BF),
            pltpu.VMEM((8, 128), F32),
            pltpu.VMEM((16, 8, 128), F32),
            pltpu.VMEM((16, 8, 128), F32),
            pltpu.VMEM((32, 8, 128), F32),
            dma((2, UNITS, 8)),
            dma((2, GAP, 9)),
            dma((2, 16)),
            dma((2, 32)),
        ]
    else:
        scratch += [pltpu.VMEM((3,) + UNIT, BF)]
    params = dict(vmem_limit_bytes=VMEM_LIMIT)
    if joined:
        params.update(collective_id=0, has_side_effects=True)
    outs = [((length, width), BF), ((length, width), F32)] + grads + sums
    return pl.pallas_call(
        functools.partial(block_kernel, joined),
        in_specs=[smem, smem, anys, anys, anys] + [vmem] * (len(par) + 1) + [anys] * len(weights),
        out_specs=[anys] * (2 + len(grads)) + [vmem] * len(sums),
        out_shape=[jax.ShapeDtypeStruct(shape, dtype) for shape, dtype in outs],
        scratch_shapes=scratch,
        compiler_params=pltpu.CompilerParams(**params),
        name="block_pass",
    )(start, mix, x, g, history, *par, rotary_table(length), *weights)


def to_units(wq, wo, wu, wd):
    d = wo.shape[0]
    down = wd.reshape(16, 4, PIECE, d).transpose(1, 0, 2, 3).reshape(4, d, d)
    up = wu.reshape(d, 16, 4, PIECE).transpose(2, 0, 1, 3).reshape(4, d, d)
    parts = [
        wq.reshape(d, 3, 3, 256).transpose(2, 0, 1, 3).reshape(3, d, d),
        wo[None],
        jnp.stack([down, up], axis=1).reshape(8, d, d),
    ]
    return jnp.concatenate(parts).reshape((UNITS,) + UNIT)


def from_units(units):
    d = units.shape[-1]
    units = units.reshape(UNITS, d, d)
    gq = units[0:3].reshape(3, d, 3, 256).transpose(1, 2, 0, 3).reshape(d, 3 * d)
    both = units[4:].reshape(4, 2, d, d)
    gd = both[:, 0].reshape(4, 16, PIECE, d).transpose(1, 0, 2, 3).reshape(4 * d, d)
    gu = both[:, 1].reshape(4, d, 16, PIECE).transpose(1, 2, 0, 3).reshape(d, 4 * d)
    return gq, units[3], gu, gd


def local(block_input, history, cotangent, span_start, w_qkv, w_out, w_up, w_down, ln_gains, ln_biases, mix_weights, joined):
    width = block_input.shape[1]
    own = ln_gains.shape[1]
    grad_history = history_grad(mix_weights, cotangent, history.shape[0])
    if joined:
        nxt, grad_input, gq, go, gu, gd, mix, gains, first, second = block_pass(
            True, span_start, mix_weights, block_input, cotangent, history, [ln_gains, ln_biases],
            w_qkv, w_out, w_up, w_down.reshape(4, own, width),
        )
        return nxt, grad_input, grad_history, mix[0], gq, go, gu, gd, gains, first[0], second[0]
    else:
        gather = lambda item, axis: lax.all_gather(item, "shard", axis=axis, tiled=True)
        mine = jnp.concatenate([ln_gains, ln_biases])
        par = jnp.concatenate([gather(mine, 1).astype(F32), jnp.zeros((4, width), F32)])
        weights = to_units(gather(w_qkv, 0), gather(w_out, 0), gather(w_up, 0), gather(w_down, 0))
        nxt, grad_input, units, small = block_pass(
            False, span_start, mix_weights, block_input, cotangent, history, [par], weights
        )

        def owned(item, axis):
            part = lax.psum_scatter(item.astype(BF), "shard", scatter_dimension=axis, tiled=True)
            return lax.psum(part, "rep").astype(F32)

        gq, go, gu, gd = [owned(item, 0) for item in from_units(units)]
        norm_grads = owned(small[:4], 1)
        grad_mix = lax.psum(small[4, :5], ("rep", "shard"))
    return nxt, grad_input, grad_history, grad_mix, gq, go, gu, gd, norm_grads[0:2], norm_grads[2], norm_grads[3]


def solution(mesh):
    token = P(("rep", "shard"), None)
    kept = P("shard", None)
    past = P(None, ("rep", "shard"), None)
    norm = P(None, "shard")
    joined = mesh.shape["rep"] == 2 and mesh.shape["shard"] == 16
    return jax.shard_map(
        functools.partial(local, joined=joined),
        mesh=mesh,
        in_specs=(token, past, token, P(("rep", "shard")), kept, kept, kept, kept, norm, norm, P()),
        out_specs=(token, token, past, P(), kept, kept, kept, kept, norm, P("shard"), P("shard")),
        check_vma=False,
    )
```
